32 devices in a mesh: dp: 16 (over z, x, core), sp: 2 (over y).
Axes of the slice: x: 2, y: 2, z: 4, core: 2. Of those that a mesh axis runs over, the one named last changes fastest.
Arguments:
- tokens: bfloat16 [4096, 1024], P(('dp', 'sp')), may hold values from -6 to 6
- seq_start: int32 [4096], P('dp'), may hold values from 0 to 192, as said below
- qkv_weight: bfloat16 [2, 1024, 3072], P(None, 'dp'), may hold values from -0.1875 to 0.1875
- out_weight: bfloat16 [2, 1024, 1024], P(None, 'dp'), may hold values from -0.1875 to 0.1875
- fc1_weight: bfloat16 [2, 1024, 4096], P(None, 'dp'), may hold values from -0.1875 to 0.1875
- fc2_weight: bfloat16 [2, 4096, 1024], P(None, 'dp'), may hold values from -0.09375 to 0.09375
- norm_gain: float32 [2, 3, 1024], replicated, may hold values from 0.5 to 1.5
- norm_bias: float32 [2, 3, 1024], replicated, may hold values from -2.5 to 2.5
- mid_gain: float32 [2, 4096], replicated, may hold values from 0.5 to 1.5
- mid_bias: float32 [2, 4096], replicated, may hold values from -2.5 to 2.5
- head_scale: float32 [2, 16], replicated, may hold values from 0.25 to 1.75
- cotangent: bfloat16 [4096, 1024], P(('dp', 'sp')), may hold values from -6 to 6
Outputs:
- output: bfloat16 [4096, 1024], P(('dp', 'sp'))
- grad_tokens: float32 [4096, 1024], P(('dp', 'sp'))
- grad_qkv: float32 [2, 1024, 3072], P(None, 'dp', 'sp')
- grad_out: float32 [2, 1024, 1024], P(None, 'dp', 'sp')
- grad_fc1: float32 [2, 1024, 4096], P(None, 'dp', 'sp')
- grad_fc2: float32 [2, 4096, 1024], P(None, 'dp', 'sp')
- grad_norm_gain: float32 [2, 3, 1024], replicated
- grad_norm_bias: float32 [2, 3, 1024], replicated
- grad_mid_gain: float32 [2, 4096], replicated
- grad_mid_bias: float32 [2, 4096], replicated
- grad_head_scale: float32 [2, 16], replicated
The draws below stay inside these ranges and needn't reach their ends.
Inputs may be any that keep to these rules, and one draw needn't show every extreme that they name: Within each dp group of 256 tokens the sequences are aligned runs of 64, 128 or 256 tokens, and seq_start gives each token the index within its group of its sequence's first token. In the first group the first half is one sequence and the last two quarters are sequences of their own.
All inputs are finite; a program needn't handle non-finite values.
Results may differ from the reference program's by a relative error of at most 0.02.
Values may be sent and summed in bfloat16 or wider, within the bound.
No kernel may reach another device: no remote copies, remote signals or barrier semaphores. Data moves between devices by JAX's collectives and lax.ppermute only.
A program may use at most 256 MiB of HBM per device.

```python
import math
import jax
import jax.numpy as jnp
from jax import lax

D = 1024
H = 16
HD = 64
FF = 4096
LAYERS = 2
GROUP = 256
TOKENS = 4096


def draw_seq_start(key, part):
    group_count = TOKENS // GROUP
    quarter = GROUP // 4
    first_key, second_key = jax.random.split(key)
    halves = jax.random.randint(first_key, (group_count, 1), 0, 2)
    quarters = jax.random.randint(second_key, (group_count, 2), 0, 2)
    group_idx = jnp.arange(group_count, dtype=jnp.int32)
    first_group = (group_idx == 0).astype(jnp.int32)
    halves = jnp.maximum(halves, first_group[:, None])
    forced = jnp.stack([jnp.zeros_like(first_group), first_group], axis=1)
    quarters = jnp.where(first_group[:, None] == 1, forced, quarters)
    position = jnp.arange(GROUP, dtype=jnp.int32)
    quarter_idx = position // quarter
    half_idx = quarter_idx // 2
    start_pos = halves * (half_idx[None, :] * 2 * quarter + quarters[:, half_idx] * (quarter_idx[None, :] % 2) * quarter)
    return start_pos.reshape(-1).astype(jnp.int32)


def block_levels(stream_key, dims, shards, smallest, top_value):
    loudness = 1.0
    for dim, shards_of in shards:
        draws = jax.random.uniform(jax.random.fold_in(jax.random.fold_in(stream_key, 6), dim), (shards_of,), jnp.float32, smallest / len(shards), top_value / len(shards))
        loudness = loudness * jnp.repeat(jnp.exp(draws), dims[dim] // shards_of).reshape((-1,) + (1,) * (len(dims) - 1 - dim))
    return loudness


def normal_values(own_key, extent, deviation, bound, shards=(), held_as=jnp.bfloat16):
    level = block_levels(own_key, extent, shards, -0.22, 0.18) if shards else 1.0
    drawn = jax.random.normal(own_key, extent, jnp.float32) * deviation * level
    return jnp.minimum(jnp.maximum(drawn, -bound), bound).astype(held_as)


def setup_inputs(seed: int = 0) -> dict:
    key_list = jax.random.split(jax.random.key(seed), 13)
    tokens = normal_values(key_list[0], (TOKENS, D), 1.0, 6.0, ((0, 32),))
    seq_start = draw_seq_start(jax.random.fold_in(key_list[12], 71), 0)
    qkv_weight = normal_values(key_list[2], (LAYERS, D, 3 * D), D ** -0.5, 0.1875, ((1, 16),))
    out_weight = normal_values(key_list[3], (LAYERS, D, D), D ** -0.5, 0.1875, ((1, 16),))
    fc1_weight = normal_values(key_list[4], (LAYERS, D, FF), D ** -0.5, 0.1875, ((1, 16),))
    fc2_weight = normal_values(key_list[5], (LAYERS, FF, D), FF ** -0.5, 0.09375, ((1, 16),))
    norm_gain = jnp.clip(1.0 + 0.1 * jax.random.normal(key_list[6], (LAYERS, 3, D), jnp.float32), 0.5, 1.5)
    norm_bias = normal_values(key_list[7], (LAYERS, 3, D), 0.3, 2.5, (), jnp.float32)
    mid_gain = jnp.clip(1.0 + 0.1 * jax.random.normal(key_list[8], (LAYERS, FF), jnp.float32), 0.5, 1.5)
    mid_bias = normal_values(key_list[9], (LAYERS, FF), 0.3, 2.5, (), jnp.float32)
    head_scale = jnp.clip(1.0 + 0.15 * jax.random.normal(key_list[10], (LAYERS, H), jnp.float32), 0.25, 1.75)
    cotangent = normal_values(key_list[11], (TOKENS, D), 1.0, 6.0, ((0, 32),))
    return {"tokens": tokens, "seq_start": seq_start, "qkv_weight": qkv_weight, "out_weight": out_weight, "fc1_weight": fc1_weight, "fc2_weight": fc2_weight, "norm_gain": norm_gain, "norm_bias": norm_bias, "mid_gain": mid_gain, "mid_bias": mid_bias, "head_scale": head_scale, "cotangent": cotangent}


norm_eps = 1e-05
highest_precision = lax.Precision.HIGHEST

@jax.custom_vjp
def low(v):
    return lax.optimization_barrier(v.astype(jnp.bfloat16)).astype(jnp.float32)

@jax.custom_vjp
def low_back(v):
    return v

def low_keep(v):
    return (low(v), None)

def low_pass(kept, grad):
    return (grad,)

def back_keep(v):
    return (v, None)

def back_low(kept, grad):
    return (low(grad),)
low.defvjp(low_keep, low_pass)
low_back.defvjp(back_keep, back_low)

def layer_norm(values, gain, bias):
    center = values - lax.optimization_barrier(jnp.mean(values, axis=-1, keepdims=True))
    spread = lax.optimization_barrier(jnp.mean(center * center, axis=-1, keepdims=True))
    return center * lax.rsqrt(spread + norm_eps) * gain + bias

def matmul(left, right):
    return jnp.dot(left, right, precision=highest_precision)

def group_forward(hidden, starts, params):
    qkv_mats, out_mats, up_mats, down_mats, gains, biases, mid_gains, mid_biases, scales = params
    length = hidden.shape[0]
    position = jnp.arange(length, dtype=jnp.int32)
    allowed = (position[None, :] >= starts[:, None]) & (position[None, :] <= position[:, None])
    score_scale = 1.0 / math.sqrt(HD)
    for which_layer in range(LAYERS):
        normed = low(layer_norm(hidden, gains[which_layer, 0], biases[which_layer, 0]))
        project = low(low_back(matmul(normed, qkv_mats[which_layer])))
        queries = project[:, :D].reshape(length, H, HD)
        key_rows = project[:, D:2 * D].reshape(length, H, HD)
        value_rows = project[:, 2 * D:].reshape(length, H, HD)
        scores = low_back(jnp.einsum('qhd,khd->hqk', queries, key_rows, precision=highest_precision) * score_scale)
        scores = jnp.where(allowed[None], scores, -1e+30)
        row_max = lax.optimization_barrier(jnp.max(scores, axis=-1, keepdims=True))
        exponent = jnp.exp(scores - row_max)
        weights_full = exponent / lax.optimization_barrier(jnp.sum(exponent, axis=-1, keepdims=True))
        attended = low_back(jnp.einsum('hqk,khd->qhd', low(weights_full), value_rows, precision=highest_precision))
        scaled = low(low_back(attended * scales[which_layer][None, :, None])).reshape(length, D)
        branch = low_back(matmul(scaled, out_mats[which_layer]))
        middle = hidden + layer_norm(branch, gains[which_layer, 1], biases[which_layer, 1])
        normed_ff = low(layer_norm(middle, gains[which_layer, 2], biases[which_layer, 2]))
        pre_act = low_back(matmul(normed_ff, up_mats[which_layer]))
        activated = jax.nn.gelu(pre_act, approximate=False)
        mixed = low(layer_norm(activated, mid_gains[which_layer], mid_biases[which_layer]))
        hidden = middle + low_back(matmul(mixed, down_mats[which_layer]))
    return hidden

def reference(tokens, seq_start, qkv_weight, out_weight, fc1_weight, fc2_weight, norm_gain, norm_bias, mid_gain, mid_bias, head_scale, cotangent):
    group_count = TOKENS // GROUP
    hidden = tokens.astype(jnp.float32).reshape(group_count, GROUP, D)
    starts = seq_start.astype(jnp.int32).reshape(group_count, GROUP)
    params = (qkv_weight.astype(jnp.float32), out_weight.astype(jnp.float32), fc1_weight.astype(jnp.float32), fc2_weight.astype(jnp.float32), norm_gain.astype(jnp.float32), norm_bias.astype(jnp.float32), mid_gain.astype(jnp.float32), mid_bias.astype(jnp.float32), head_scale.astype(jnp.float32))

    def whole(inputs, weights):

        def group_step(paired):
            return group_forward(paired[0], paired[1], weights)
        return lax.map(jax.checkpoint(group_step), (inputs, starts))
    result, pullback = jax.vjp(whole, hidden, params)
    grad_hidden, grad_params = pullback(cotangent.astype(jnp.float32).reshape(group_count, GROUP, D))
    return (result.reshape(TOKENS, D).astype(jnp.bfloat16), grad_hidden.reshape(TOKENS, D), grad_params[0], grad_params[1], grad_params[2], grad_params[3], grad_params[4], grad_params[5], grad_params[6], grad_params[7], grad_params[8])
```

```python
from functools import partial
import math

import jax
import jax.numpy as jnp
from jax import lax
from jax.sharding import Mesh, PartitionSpec as P

H = 16
HD = 64
LAYERS = 2


norm_eps = 1e-05


def for_sending(array):

    def short(part):
        return part.astype(jnp.bfloat16) if part.dtype == jnp.float32 else part

    return jax.tree.map(short, array)


def norm_forward(values, gain, bias):
    center = values - jnp.mean(values, axis=-1, keepdims=True)
    inverse = lax.rsqrt(jnp.mean(center * center, axis=-1, keepdims=True) + norm_eps)
    normal = center * inverse
    return (normal * gain + bias, normal, inverse)


def norm_backward(upstream, normal, inverse, gain):
    scaled = upstream * gain
    grad_values = inverse * (
        scaled
        - jnp.mean(scaled, axis=-1, keepdims=True)
        - normal * jnp.mean(scaled * normal, axis=-1, keepdims=True)
    )
    return (grad_values, jnp.sum(upstream * normal, axis=0), jnp.sum(upstream, axis=0))


def product(left, right):
    return jnp.dot(left, right, preferred_element_type=jnp.float32)


def block_layout(length):
    block_count = min(4, max(1, length // 512))
    return (block_count, length // block_count)


def score_block(query_block, query_pos, query_start, key_rows, score_scale):
    key_pos = jnp.arange(key_rows.shape[0], dtype=jnp.int32)
    scores = (
        jnp.einsum("qhd,khd->hqk", query_block, key_rows, preferred_element_type=jnp.float32)
        * score_scale
    )
    allowed = (key_pos[None, :] >= query_start[:, None]) & (key_pos[None, :] <= query_pos[:, None])
    return jnp.where(allowed[None], scores, -1e30)


def attend_forward(queries, key_rows, value_rows, starts, score_scale):
    length = queries.shape[0]
    block_count, block_rows = block_layout(length)
    positions = jnp.arange(length, dtype=jnp.int32)
    results, maxima, totals = ([], [], [])
    for block_index in range(block_count):
        row_first = block_index * block_rows
        row_end = row_first + block_rows
        scores = score_block(
            queries[row_first:row_end],
            positions[row_first:row_end],
            starts[row_first:row_end],
            key_rows[:row_end],
            score_scale,
        )
        row_max = jnp.max(scores, axis=-1, keepdims=True)
        exponent = jnp.exp(scores - row_max)
        row_total = jnp.sum(exponent, axis=-1, keepdims=True)
        weights_low = (exponent / row_total).astype(jnp.bfloat16)
        results.append(
            jnp.einsum(
                "hqk,khd->qhd",
                weights_low,
                value_rows[:row_end],
                preferred_element_type=jnp.float32,
            )
        )
        maxima.append(row_max)
        totals.append(row_total)
    return (jnp.concatenate(results, axis=0), maxima, totals)


def attend_backward(queries, key_rows, value_rows, starts, score_scale, grad_out, maxima, totals):
    length, heads_here, head_dim = queries.shape
    block_count, block_rows = block_layout(length)
    positions = jnp.arange(length, dtype=jnp.int32)
    grad_keys = jnp.zeros((length, heads_here, head_dim), jnp.float32)
    grad_values = jnp.zeros((length, heads_here, head_dim), jnp.float32)
    query_grads = []
    for block_index in range(block_count):
        row_first = block_index * block_rows
        row_end = row_first + block_rows
        query_block = queries[row_first:row_end]
        grad_block = grad_out[row_first:row_end]
        scores = score_block(
            query_block,
            positions[row_first:row_end],
            starts[row_first:row_end],
            key_rows[:row_end],
            score_scale,
        )
        weights_full = jnp.exp(scores - maxima[block_index]) / totals[block_index]
        weights_low = weights_full.astype(jnp.bfloat16)
        grad_weights = jnp.einsum(
            "qhd,khd->hqk", grad_block, value_rows[:row_end], preferred_element_type=jnp.float32
        )
        inner = jnp.sum(weights_full * grad_weights, axis=-1, keepdims=True)
        grad_scores = (weights_full * (grad_weights - inner)).astype(jnp.bfloat16)
        query_grads.append(
            jnp.einsum(
                "hqk,khd->qhd", grad_scores, key_rows[:row_end], preferred_element_type=jnp.float32
            )
            * score_scale
        )
        grad_keys = grad_keys.at[:row_end].add(
            jnp.einsum("hqk,qhd->khd", grad_scores, query_block, preferred_element_type=jnp.float32)
            * score_scale
        )
        grad_values = grad_values.at[:row_end].add(
            jnp.einsum("hqk,qhd->khd", weights_low, grad_block, preferred_element_type=jnp.float32)
        )
    return (jnp.concatenate(query_grads, axis=0), grad_keys, grad_values)


def local_any(
    tokens,
    seq_start,
    qkv_weight,
    out_weight,
    fc1_weight,
    fc2_weight,
    norm_gain,
    norm_bias,
    mid_gain,
    mid_bias,
    head_scale,
    cotangent,
):
    split_count = lax.axis_size("sp")
    split_rank = lax.axis_index("sp")
    local_rows, width_model = tokens.shape
    group_rows = seq_start.shape[0]
    heads_here = H // split_count
    head_width = heads_here * HD
    score_scale = 1.0 / math.sqrt(HD)
    scale_here = lax.dynamic_slice_in_dim(head_scale, split_rank * heads_here, heads_here, axis=1)
    hidden = tokens.astype(jnp.float32)
    kept_layers = []
    kept_matrices = []
    for which_layer in range(LAYERS):
        matrices = (
            lax.all_gather(qkv_weight[which_layer], "dp", axis=0, tiled=True),
            lax.all_gather(out_weight[which_layer], "dp", axis=0, tiled=True),
            lax.all_gather(fc1_weight[which_layer], "dp", axis=0, tiled=True),
            lax.all_gather(fc2_weight[which_layer], "dp", axis=0, tiled=True),
        )
        qkv_full, out_full, up_full, down_full = matrices
        normed, norm_a, inv_a = norm_forward(
            hidden, norm_gain[which_layer, 0], norm_bias[which_layer, 0]
        )
        normed_low = normed.astype(jnp.bfloat16)
        project = (
            product(normed_low, qkv_full)
            .astype(jnp.bfloat16)
            .reshape(local_rows, 3, split_count, head_width)
        )
        by_heads = lax.all_to_all(project, "sp", split_axis=2, concat_axis=0, tiled=True)
        queries = by_heads[:, 0, 0].reshape(group_rows, heads_here, HD)
        key_rows = by_heads[:, 1, 0].reshape(group_rows, heads_here, HD)
        value_rows = by_heads[:, 2, 0].reshape(group_rows, heads_here, HD)
        attended, maxima, totals = attend_forward(
            queries, key_rows, value_rows, seq_start, score_scale
        )
        scaled = (
            (attended * scale_here[which_layer][None, :, None])
            .astype(jnp.bfloat16)
            .reshape(group_rows, 1, head_width)
        )
        gathered = lax.all_to_all(scaled, "sp", split_axis=0, concat_axis=1, tiled=True).reshape(
            local_rows, width_model
        )
        branch = product(gathered, out_full)
        branch_norm, norm_z, inv_z = norm_forward(
            branch, norm_gain[which_layer, 1], norm_bias[which_layer, 1]
        )
        middle = hidden + branch_norm
        normed_ff, norm_b, inv_b = norm_forward(
            middle, norm_gain[which_layer, 2], norm_bias[which_layer, 2]
        )
        ff_low = normed_ff.astype(jnp.bfloat16)
        pre_act = product(ff_low, up_full)
        activated = jax.nn.gelu(pre_act, approximate=False)
        mixed, norm_m, inv_m = norm_forward(activated, mid_gain[which_layer], mid_bias[which_layer])
        mixed_low = mixed.astype(jnp.bfloat16)
        hidden = middle + product(mixed_low, down_full)
        kept_layers.append(
            (
                norm_a,
                inv_a,
                normed_low,
                queries,
                key_rows,
                value_rows,
                attended,
                maxima,
                totals,
                gathered,
                norm_z,
                inv_z,
                norm_b,
                inv_b,
                ff_low,
                pre_act,
                norm_m,
                inv_m,
                mixed_low,
            )
        )
        kept_matrices.append(matrices)
    output = hidden.astype(jnp.bfloat16)
    grad_hidden = cotangent.astype(jnp.float32)
    matrix_grads = [None] * LAYERS
    gain_grads = [None] * LAYERS
    bias_grads = [None] * LAYERS
    mid_gain_grads = [None] * LAYERS
    mid_bias_grads = [None] * LAYERS
    scale_grads = [None] * LAYERS
    for which_layer in reversed(range(LAYERS)):
        (
            norm_a,
            inv_a,
            normed_low,
            queries,
            key_rows,
            value_rows,
            attended,
            maxima,
            totals,
            gathered,
            norm_z,
            inv_z,
            norm_b,
            inv_b,
            ff_low,
            pre_act,
            norm_m,
            inv_m,
            mixed_low,
        ) = kept_layers[which_layer]
        qkv_full, out_full, up_full, down_full = (
            lax.all_gather(qkv_weight[which_layer], "dp", axis=0, tiled=True),
            lax.all_gather(out_weight[which_layer], "dp", axis=0, tiled=True),
            lax.all_gather(fc1_weight[which_layer], "dp", axis=0, tiled=True),
            lax.all_gather(fc2_weight[which_layer], "dp", axis=0, tiled=True),
        )
        grad_final = grad_hidden.astype(jnp.bfloat16)
        grad_mixed = product(grad_final, down_full.T)
        grad_act, mid_gain_grad, mid_bias_grad = norm_backward(
            grad_mixed, norm_m, inv_m, mid_gain[which_layer]
        )
        gelu_value, gelu_pull = jax.vjp(partial(jax.nn.gelu, approximate=False), pre_act)
        grad_pre = gelu_pull(grad_act)[0].astype(jnp.bfloat16)
        grad_ff_in = product(grad_pre, up_full.T)
        grad_mid_in, gain_two, bias_two = norm_backward(
            grad_ff_in, norm_b, inv_b, norm_gain[which_layer, 2]
        )
        grad_middle = grad_hidden + grad_mid_in
        grad_branch_full, gain_one, bias_one = norm_backward(
            grad_middle, norm_z, inv_z, norm_gain[which_layer, 1]
        )
        grad_branch = grad_branch_full.astype(jnp.bfloat16)
        grad_gathered = (
            product(grad_branch, out_full.T)
            .astype(jnp.bfloat16)
            .reshape(local_rows, split_count, head_width)
        )
        grad_heads = lax.all_to_all(
            grad_gathered, "sp", split_axis=1, concat_axis=0, tiled=True
        ).reshape(group_rows, heads_here, HD)
        scale_grad_here = jnp.sum(grad_heads.astype(jnp.float32) * attended, axis=(0, 2))
        grad_attended = (grad_heads * scale_here[which_layer][None, :, None]).astype(jnp.bfloat16)
        grad_queries, grad_keys, grad_values = attend_backward(
            queries, key_rows, value_rows, seq_start, score_scale, grad_attended, maxima, totals
        )
        stacked = jnp.stack(
            [
                grad_queries.reshape(group_rows, head_width),
                grad_keys.reshape(group_rows, head_width),
                grad_values.reshape(group_rows, head_width),
            ],
            axis=1,
        )
        stacked = stacked.astype(jnp.bfloat16).reshape(group_rows, 3, 1, head_width)
        back_rows = lax.all_to_all(stacked, "sp", split_axis=0, concat_axis=2, tiled=True).reshape(
            local_rows, 3 * width_model
        )
        grad_normed = product(back_rows, qkv_full.T)
        grad_input, gain_zero, bias_zero = norm_backward(
            grad_normed, norm_a, inv_a, norm_gain[which_layer, 0]
        )
        grad_hidden = grad_middle + grad_input
        group_inputs = (
            lax.all_gather(normed_low, "sp", axis=0, tiled=True),
            lax.all_gather(gathered, "sp", axis=0, tiled=True),
            lax.all_gather(ff_low, "sp", axis=0, tiled=True),
            lax.all_gather(mixed_low, "sp", axis=0, tiled=True),
        )
        group_columns = (
            lax.all_to_all(
                back_rows.reshape(local_rows, split_count, -1),
                "sp",
                split_axis=1,
                concat_axis=0,
                tiled=True,
            ),
            lax.all_to_all(
                grad_branch.reshape(local_rows, split_count, -1),
                "sp",
                split_axis=1,
                concat_axis=0,
                tiled=True,
            ),
            lax.all_to_all(
                grad_pre.reshape(local_rows, split_count, -1),
                "sp",
                split_axis=1,
                concat_axis=0,
                tiled=True,
            ),
            lax.all_to_all(
                grad_final.reshape(local_rows, split_count, -1),
                "sp",
                split_axis=1,
                concat_axis=0,
                tiled=True,
            ),
        )
        terms = tuple(
            (
                product(group_inputs[which].T, group_columns[which].reshape(group_rows, -1))
                for which in range(4)
            )
        )
        matrix_grads[which_layer] = jax.tree.map(
            lambda part: part.astype(jnp.float32),
            lax.psum_scatter(for_sending(terms), "dp", scatter_dimension=0, tiled=True),
        )
        gain_grads[which_layer] = jnp.stack([gain_zero, gain_one, gain_two])
        bias_grads[which_layer] = jnp.stack([bias_zero, bias_one, bias_two])
        mid_gain_grads[which_layer] = mid_gain_grad
        mid_bias_grads[which_layer] = mid_bias_grad
        scale_grads[which_layer] = lax.dynamic_update_slice(
            jnp.zeros((H,), jnp.float32), scale_grad_here, (split_rank * heads_here,)
        )
    summed = tuple((jnp.stack([pieces[which] for pieces in matrix_grads]) for which in range(4)))
    small_sums = lax.psum(
        (
            jnp.stack(gain_grads),
            jnp.stack(bias_grads),
            jnp.stack(mid_gain_grads),
            jnp.stack(mid_bias_grads),
            jnp.stack(scale_grads),
        ),
        ("dp", "sp"),
    )
    return (
        output,
        grad_hidden,
        summed[0],
        summed[1],
        summed[2],
        summed[3],
        small_sums[0],
        small_sums[1],
        small_sums[2],
        small_sums[3],
        small_sums[4],
    )


SWAP = ((0, 1), (1, 0))


def swap(array, axis):
    return lax.ppermute(array, axis, SWAP)


def shift(array, axis, count, step):
    return lax.ppermute(array, axis, [(i, (i + step) % count) for i in range(count)])


def gather_rows(part):
    pair = jnp.concatenate([part, swap(part, "y")], axis=0)
    return jnp.concatenate([pair, swap(pair, "c")], axis=0)


def reduce_rows(partial_sum):
    half = partial_sum.shape[0] // 2
    mine = partial_sum[:half] + swap(partial_sum[half:].astype(jnp.bfloat16), "c").astype(
        jnp.float32
    )
    half = half // 2
    return mine[:half] + swap(mine[half:].astype(jnp.bfloat16), "y").astype(jnp.float32)


def sum_four(values):
    values = values + swap(values, "c")
    return values + swap(values, "y")


def from_there(array, axis_name, axis):
    blocks = 2 if axis_name == "c" else 4
    there = jnp.split(swap(array, axis_name), blocks, axis=axis)
    order = (1, 0) if axis_name == "c" else (1, 0, 3, 2)
    return jnp.concatenate([there[which] for which in order], axis=axis)


def sum_rows(values):
    values = values + from_there(values, "c", values.ndim - 1)
    return values + from_there(values, "y", values.ndim - 1)


def reorder(array, order, axis):
    return jnp.concatenate(
        [lax.dynamic_index_in_dim(array, which, axis, keepdims=True) for which in order], axis=axis
    )


def local_four(
    tokens,
    seq_start,
    qkv_weight,
    out_weight,
    fc1_weight,
    fc2_weight,
    norm_gain,
    norm_bias,
    mid_gain,
    mid_bias,
    head_scale,
    cotangent,
):
    nz, nx = lax.axis_size("z"), lax.axis_size("x")
    iz, ix, ic, iy = (lax.axis_index(name) for name in ("z", "x", "c", "y"))
    rows, width = tokens.shape
    group_rows = seq_start.shape[0]
    hidden_width = fc1_weight.shape[2]
    chips = nz * nx
    quarter = 2 * iy + ic
    quarter_there = 2 * iy + 1 - ic
    unit_quarter = 2 * ic + iy
    unit_quarter_there = 2 * (1 - ic) + iy
    chip_rows = width // chips
    core_rows = chip_rows // 2
    heads_here = H // 4
    head_width = width // 4
    score_scale = 1.0 / math.sqrt(HD)
    f32, bf16 = jnp.float32, jnp.bfloat16

    far = [((iz - k // nx) % nz, (ix - k % nx) % nx) for k in range(chips)]
    relative = [a * nx + b for a, b in far]
    absolute = [((iz - k // nx) % nz) * nx + (ix - k % nx) % nx for k in range(chips)]

    def to_relative(values):
        blocks = values.reshape(values.shape[0], chips, -1)
        return reorder(blocks, relative, 1).reshape(values.shape)

    def to_absolute(values):
        blocks = values.reshape(values.shape[0], chips, -1)
        return reorder(blocks, absolute, 1).reshape(values.shape)

    def core_order(own, other):
        first = jnp.where(ic == 0, own, other)
        second = jnp.where(ic == 0, other, own)
        return jnp.concatenate([first, second], axis=0)

    def pieces(which_layer):
        def columns(weight, parts, blocks, which):
            view = weight.reshape(weight.shape[0], parts, blocks, -1)
            return lax.dynamic_index_in_dim(view, which, 2, keepdims=False).reshape(
                weight.shape[0], -1
            )

        qkv, out = qkv_weight[which_layer], out_weight[which_layer]
        up, down = fc1_weight[which_layer], fc2_weight[which_layer]
        own = jnp.concatenate([columns(qkv, 3, 4, quarter), columns(out, 1, 4, quarter)], axis=1)
        send = jnp.concatenate(
            [columns(qkv, 3, 4, quarter_there), columns(out, 1, 4, quarter_there)], axis=1
        )
        first = core_order(own, swap(send, "c"))
        own = columns(up, chips, 4, unit_quarter)
        send = columns(up, chips, 4, unit_quarter_there)
        second = core_order(own, swap(send, "c"))
        third = lax.dynamic_slice_in_dim(down, iy * (down.shape[0] // 2), down.shape[0] // 2, 0)
        return first, second, third

    def gather_chips(part):
        got = []
        for step in range(nz):
            here = part if step == 0 else shift(part, "z", nz, step)
            got.append(here)
            for side in range(1, nx):
                got.append(shift(here, "x", nx, side))
        return got

    def scatter_chips(blocks):
        held = blocks[:, 0].astype(f32)
        for side in range(1, nx):
            there = blocks[:, side].astype(bf16)
            held = held + lax.ppermute(
                there, "x", [(i, (i - side) % nx) for i in range(nx)]
            ).astype(f32)
        total = held[0]
        for step in range(1, nz):
            total = total + lax.ppermute(
                held[step].astype(bf16), "z", [(i, (i - step) % nz) for i in range(nz)]
            ).astype(f32)
        return total

    first0, second0, third0 = pieces(0)
    first1, second1, third1 = pieces(1)
    got0 = gather_chips(first0)
    got0b = gather_chips(jnp.stack([second0, third0]))
    got1 = gather_chips(jnp.stack([first1, second1, third1]))
    firsts = [jnp.concatenate(got0, axis=0), jnp.concatenate([g[0] for g in got1], axis=0)]
    seconds = [
        jnp.concatenate([g[0] for g in got0b], axis=0),
        jnp.concatenate([g[1] for g in got1], axis=0),
    ]
    thirds = [
        reorder(jnp.stack([g[1] for g in got0b]), absolute, 0).reshape(-1, width),
        reorder(jnp.stack([g[2] for g in got1]), absolute, 0).reshape(-1, width),
    ]

    def out_rows(block):
        view = block.reshape(nz, nx * chip_rows, head_width)

        def rows_of(which):
            return lax.dynamic_index_in_dim(view, (iz - which) % nz, 0, keepdims=False)

        own = rows_of(quarter)
        own_y = rows_of(2 * (1 - iy) + ic)
        there = rows_of(quarter_there)
        there_y = rows_of(2 * (1 - iy) + 1 - ic)
        other, other_y = swap((there, there_y), "c")
        mine = jnp.where(ic == 0, jnp.stack([own, other]), jnp.stack([other, own]))
        mine_y = jnp.where(ic == 0, jnp.stack([own_y, other_y]), jnp.stack([other_y, own_y]))
        from_y = swap(mine_y, "y")
        both = jnp.where(iy == 0, jnp.stack([mine, from_y]), jnp.stack([from_y, mine]))
        both = both.reshape(4, nx, chip_rows, head_width)
        both = reorder(both, [(ix - k) % nx for k in range(nx)], 1)
        return both.transpose(1, 2, 0, 3).reshape(nx * chip_rows, width)

    qkv_mats = [block[:, : 3 * head_width] for block in firsts]
    out_mats = [out_rows(block[:, 3 * head_width :]) for block in firsts]
    up_mats, down_mats = seconds, thirds

    own_pos = iy * rows + jnp.arange(rows, dtype=jnp.int32)
    there_pos = (1 - iy) * rows + jnp.arange(rows, dtype=jnp.int32)
    pos = jnp.concatenate([own_pos, there_pos])
    starts = jnp.concatenate(
        [
            lax.dynamic_slice_in_dim(seq_start, iy * rows, rows),
            lax.dynamic_slice_in_dim(seq_start, (1 - iy) * rows, rows),
        ]
    )
    starts = jnp.stack([starts, swap(starts, "c")])
    allowed = (pos[None, None, :] >= starts[:, :, None]) & (
        pos[None, None, :] <= pos[None, :, None]
    )
    allowed = allowed[:, None]
    scale_here = lax.dynamic_slice_in_dim(head_scale, quarter * heads_here, heads_here, axis=1)

    def mine_of(vector):
        view = vector.reshape(chips, 4, -1)
        return lax.dynamic_index_in_dim(view, unit_quarter, 1, keepdims=False).reshape(-1)

    def split_heads(values):
        return values.reshape(2, group_rows, heads_here, HD)

    hidden = tokens.astype(f32)
    kept = []
    for which in range(LAYERS):
        normed, norm_a, inv_a = norm_forward(hidden, norm_gain[which, 0], norm_bias[which, 0])
        a_full = gather_rows(to_relative(normed.astype(bf16)))
        project = product(a_full, qkv_mats[which]).astype(bf16)
        queries = split_heads(project[:, :head_width])
        key_rows = split_heads(project[:, head_width : 2 * head_width])
        value_rows = split_heads(project[:, 2 * head_width :])
        scores = (
            jnp.einsum("gqhd,gkhd->ghqk", queries, key_rows, preferred_element_type=f32)
            * score_scale
        )
        scores = jnp.where(allowed, scores, -1e30)
        row_max = jnp.max(scores, axis=-1, keepdims=True)
        exponent = jnp.exp(scores - row_max)
        weights = exponent / jnp.sum(exponent, axis=-1, keepdims=True)
        weights_low = weights.astype(bf16)
        attended = jnp.einsum("ghqk,gkhd->gqhd", weights_low, value_rows, preferred_element_type=f32)
        scaled = (attended * scale_here[which][None, None, :, None]).astype(bf16)
        scaled = scaled.reshape(2 * group_rows, head_width)
        y_all = gather_four(scaled, ic, iy)
        branch = reduce_rows(product(scaled, out_mats[which]))
        branch_norm, norm_z, inv_z = norm_forward(branch, norm_gain[which, 1], norm_bias[which, 1])
        middle = hidden + branch_norm
        normed_ff, norm_b, inv_b = norm_forward(middle, norm_gain[which, 2], norm_bias[which, 2])
        b_full = gather_rows(to_relative(normed_ff.astype(bf16)))
        pre_act = product(b_full, up_mats[which])
        activated = jax.nn.gelu(pre_act, approximate=False)
        gain_m, bias_m = mine_of(mid_gain[which]), mine_of(mid_bias[which])
        mean_here = jnp.mean(activated, axis=-1)
        center = activated - mean_here[:, None]
        spread_here = jnp.mean(center * center, axis=-1)
        mean_all = sum_rows(mean_here) * 0.25
        spread_all = sum_rows(spread_here + (mean_here - mean_all) ** 2) * 0.25
        inv_m = lax.rsqrt(spread_all + norm_eps)[:, None]
        norm_m = (activated - mean_all[:, None]) * inv_m
        mixed_low = (norm_m * gain_m + bias_m).astype(bf16)
        hidden = middle + reduce_rows(product(mixed_low, down_mats[which]))
        kept.append(
            (
                norm_a, inv_a, a_full, queries, key_rows, value_rows, weights, weights_low, attended,
                y_all, norm_z, inv_z, norm_b, inv_b, b_full, pre_act, norm_m, inv_m, mixed_low, gain_m,
            )
        )
    output = hidden.astype(bf16)
    grad_hidden = cotangent.astype(f32)
    matrix_grads, vector_grads = [None] * LAYERS, [None] * LAYERS
    for which in reversed(range(LAYERS)):
        (
            norm_a, inv_a, a_full, queries, key_rows, value_rows, weights, weights_low, attended,
            y_all, norm_z, inv_z, norm_b, inv_b, b_full, pre_act, norm_m, inv_m, mixed_low, gain_m,
        ) = kept[which]
        final_full = gather_rows(grad_hidden.astype(bf16))
        grad_mixed = product(final_full, down_mats[which].T)
        down_term = product(mixed_low.T, final_full)
        mid_gain_grad = jnp.sum(grad_mixed * norm_m, axis=0)
        mid_bias_grad = jnp.sum(grad_mixed, axis=0)
        scaled_grad = grad_mixed * gain_m
        sums = sum_rows(
            jnp.stack([jnp.sum(scaled_grad, axis=-1), jnp.sum(scaled_grad * norm_m, axis=-1)])
        ) / hidden_width
        grad_act = inv_m * (scaled_grad - sums[0][:, None] - norm_m * sums[1][:, None])
        gelu_value, gelu_pull = jax.vjp(partial(jax.nn.gelu, approximate=False), pre_act)
        grad_pre = gelu_pull(grad_act)[0].astype(bf16)
        grad_ff_in = to_absolute(reduce_rows(product(grad_pre, up_mats[which].T)))
        up_term = product(b_full.T, grad_pre)
        grad_mid_in, gain_two, bias_two = norm_backward(
            grad_ff_in, norm_b, inv_b, norm_gain[which, 2]
        )
        grad_middle = grad_hidden + grad_mid_in
        grad_branch, gain_one, bias_one = norm_backward(
            grad_middle, norm_z, inv_z, norm_gain[which, 1]
        )
        branch_full = gather_rows(grad_branch.astype(bf16))
        columns_z = lax.dynamic_slice_in_dim(branch_full, quarter * head_width, head_width, 1)
        out_term = product(y_all.T, columns_z)
        grad_scaled = product(branch_full, out_mats[which].T).astype(bf16)
        grad_heads = split_heads(grad_scaled)
        scale_grad = jnp.sum(grad_heads.astype(f32) * attended, axis=(0, 1, 3))
        grad_attended = (grad_heads * scale_here[which][None, None, :, None]).astype(bf16)
        grad_weights = jnp.einsum(
            "gqhd,gkhd->ghqk", grad_attended, value_rows, preferred_element_type=f32
        )
        inner = jnp.sum(weights * grad_weights, axis=-1, keepdims=True)
        grad_scores = (weights * (grad_weights - inner)).astype(bf16)
        grad_queries = jnp.einsum(
            "ghqk,gkhd->gqhd", grad_scores, key_rows, preferred_element_type=f32
        ) * score_scale
        grad_keys = jnp.einsum(
            "ghqk,gqhd->gkhd", grad_scores, queries, preferred_element_type=f32
        ) * score_scale
        grad_values = jnp.einsum(
            "ghqk,gqhd->gkhd", weights_low, grad_attended, preferred_element_type=f32
        )
        grad_project = jnp.concatenate(
            [
                part.astype(bf16).reshape(2 * group_rows, head_width)
                for part in (grad_queries, grad_keys, grad_values)
            ],
            axis=1,
        )
        grad_normed = to_absolute(reduce_rows(product(grad_project, qkv_mats[which].T)))
        qkv_term = product(a_full.T, grad_project)
        grad_input, gain_zero, bias_zero = norm_backward(
            grad_normed, norm_a, inv_a, norm_gain[which, 0]
        )
        grad_hidden = grad_middle + grad_input

        down_blocks = reorder(down_term.astype(bf16).reshape(chips, -1, width), relative, 0)
        up_blocks = up_term.astype(bf16).reshape(chips, chip_rows, -1)
        ff_sum = scatter_chips(
            jnp.stack([up_blocks, down_blocks], axis=1).reshape(nz, nx, 2, chip_rows, -1)
        )
        out_blocks = reorder(out_term.astype(bf16).reshape(chips, chip_rows, -1), relative, 0)
        qkv_blocks = qkv_term.astype(bf16).reshape(chips, chip_rows, -1)
        at_sum = scatter_chips(
            jnp.concatenate([qkv_blocks, out_blocks], axis=2).reshape(nz, nx, chip_rows, -1)
        )

        def core_swap_rows(values):
            own = lax.dynamic_slice_in_dim(values, ic * core_rows, core_rows, 0)
            there = lax.dynamic_slice_in_dim(values, (1 - ic) * core_rows, core_rows, 0)
            other = swap(there.astype(bf16), "c").astype(f32)
            return jnp.where(ic == 0, jnp.stack([own, other]), jnp.stack([other, own]))

        def y_pair(keep, send):
            other = swap(send.astype(bf16), "y").astype(f32)
            return jnp.where(iy == 0, jnp.stack([keep, other]), jnp.stack([other, keep]))

        at_rows = core_swap_rows(at_sum)
        qkv_rows = at_rows[:, :, : 3 * head_width].reshape(2, core_rows, 3, head_width)
        q_rows, k_rows, v_rows = (
            qkv_rows[:, :, part].transpose(1, 0, 2).reshape(core_rows, -1) for part in range(3)
        )
        out_part = at_rows[:, :, 3 * head_width :].transpose(1, 0, 2).reshape(core_rows, -1)
        moved = swap(jnp.where(iy == 0, v_rows, q_rows).astype(bf16), "y").astype(f32)
        grad_qkv = jnp.where(
            iy == 0,
            jnp.concatenate([q_rows, moved, k_rows], axis=1),
            jnp.concatenate([k_rows, moved, v_rows], axis=1),
        )
        grad_out = out_part
        half_chips = chips // 2
        up_rows = core_swap_rows(ff_sum[0]).reshape(2, core_rows, chips, -1)
        up_keep = lax.dynamic_slice_in_dim(up_rows, iy * half_chips, half_chips, 2)
        up_send = lax.dynamic_slice_in_dim(up_rows, (1 - iy) * half_chips, half_chips, 2)
        up_both = y_pair(up_keep, up_send)
        grad_up = up_both.transpose(2, 3, 1, 0, 4).reshape(core_rows, -1)
        half_width = width // 2
        down_keep = lax.dynamic_slice_in_dim(ff_sum[1], iy * half_width, half_width, 1)
        down_send = lax.dynamic_slice_in_dim(ff_sum[1], (1 - iy) * half_width, half_width, 1)
        grad_down = y_pair(down_keep, down_send).reshape(-1, half_width)
        matrix_grads[which] = (grad_qkv, grad_out, grad_up, grad_down)

        def spread_units(vector):
            view = jnp.zeros((chips, 4, hidden_width // chips // 4), f32)
            return lax.dynamic_update_slice(
                view, vector.reshape(chips, 1, -1), (0, unit_quarter, 0)
            ).reshape(-1)

        scale_full = lax.dynamic_update_slice(
            jnp.zeros((128,), f32), scale_grad, (quarter * heads_here,)
        )
        vector = jnp.concatenate(
            [
                gain_zero, gain_one, gain_two, bias_zero, bias_one, bias_two,
                spread_units(mid_gain_grad), spread_units(mid_bias_grad), scale_full,
            ]
        )
        vector = sum_four(vector)
        vector = vector + swap(vector, "x")
        for bit in (1, 2):
            vector = vector + lax.ppermute(vector, "z", [(i, i ^ bit) for i in range(nz)])
        vector_grads[which] = vector

    summed = [jnp.stack([grads[which] for grads in matrix_grads]) for which in range(4)]
    vectors = jnp.stack(vector_grads)
    ends = [0, 3 * width, 6 * width, 6 * width + hidden_width, 6 * width + 2 * hidden_width]
    return (
        output,
        grad_hidden,
        summed[0],
        summed[1],
        summed[2],
        summed[3],
        vectors[:, ends[0] : ends[1]].reshape(LAYERS, 3, width),
        vectors[:, ends[1] : ends[2]].reshape(LAYERS, 3, width),
        vectors[:, ends[2] : ends[3]],
        vectors[:, ends[3] : ends[4]],
        vectors[:, ends[4] : ends[4] + H],
    )


def gather_four(part, ic, iy):
    other = from_there(part, "c", 0)
    pair = jnp.where(
        ic == 0, jnp.concatenate([part, other], axis=1), jnp.concatenate([other, part], axis=1)
    )
    there = from_there(pair, "y", 0)
    return jnp.where(
        iy == 0, jnp.concatenate([pair, there], axis=1), jnp.concatenate([there, pair], axis=1)
    )


def solution(mesh):
    dp, sp = mesh.shape["dp"], mesh.shape["sp"]
    if sp == 2 and dp == 16:
        mesh = Mesh(mesh.devices.reshape(4, dp // 8, 2, 2), ("z", "x", "c", "y"))
        rows, every, cols, body = ("z", "x", "c"), ("z", "x", "c", "y"), "y", local_four
    else:
        rows, every, cols, body = "dp", ("dp", "sp"), "sp", local_any
    weight = P(None, rows, None)
    in_specs = (P(every, None), P(rows), weight, weight, weight, weight)
    in_specs = in_specs + (P(),) * 5 + (P(every, None),)
    grad = P(None, rows, cols)
    out_specs = (P(every, None), P(every, None), grad, grad, grad, grad) + (P(),) * 5
    return jax.shard_map(body, mesh=mesh, in_specs=in_specs, out_specs=out_specs, check_vma=False)
```

```python
from functools import partial
import math

import jax
import jax.numpy as jnp
from jax import lax
from jax.experimental import pallas as pl
from jax.experimental.pallas import tpu as pltpu
from jax.sharding import Mesh, PartitionSpec as P

H = 16
HD = 64
LAYERS = 2


norm_eps = 1e-05


def for_sending(array):

    def short(part):
        return part.astype(jnp.bfloat16) if part.dtype == jnp.float32 else part

    return jax.tree.map(short, array)


def norm_forward(values, gain, bias):
    center = values - jnp.mean(values, axis=-1, keepdims=True)
    inverse = lax.rsqrt(jnp.mean(center * center, axis=-1, keepdims=True) + norm_eps)
    normal = center * inverse
    return (normal * gain + bias, normal, inverse)


def norm_backward(upstream, normal, inverse, gain):
    scaled = upstream * gain
    grad_values = inverse * (
        scaled
        - jnp.mean(scaled, axis=-1, keepdims=True)
        - normal * jnp.mean(scaled * normal, axis=-1, keepdims=True)
    )
    return (grad_values, jnp.sum(upstream * normal, axis=0), jnp.sum(upstream, axis=0))


def product(left, right):
    return jnp.dot(left, right, preferred_element_type=jnp.float32)


def block_layout(length):
    block_count = min(4, max(1, length // 512))
    return (block_count, length // block_count)


def score_block(query_block, query_pos, query_start, key_rows, score_scale):
    key_pos = jnp.arange(key_rows.shape[0], dtype=jnp.int32)
    scores = (
        jnp.einsum("qhd,khd->hqk", query_block, key_rows, preferred_element_type=jnp.float32)
        * score_scale
    )
    allowed = (key_pos[None, :] >= query_start[:, None]) & (key_pos[None, :] <= query_pos[:, None])
    return jnp.where(allowed[None], scores, -1e30)


def attend_forward(queries, key_rows, value_rows, starts, score_scale):
    length = queries.shape[0]
    block_count, block_rows = block_layout(length)
    positions = jnp.arange(length, dtype=jnp.int32)
    results, maxima, totals = ([], [], [])
    for block_index in range(block_count):
        row_first = block_index * block_rows
        row_end = row_first + block_rows
        scores = score_block(
            queries[row_first:row_end],
            positions[row_first:row_end],
            starts[row_first:row_end],
            key_rows[:row_end],
            score_scale,
        )
        row_max = jnp.max(scores, axis=-1, keepdims=True)
        exponent = jnp.exp(scores - row_max)
        row_total = jnp.sum(exponent, axis=-1, keepdims=True)
        weights_low = (exponent / row_total).astype(jnp.bfloat16)
        results.append(
            jnp.einsum(
                "hqk,khd->qhd",
                weights_low,
                value_rows[:row_end],
                preferred_element_type=jnp.float32,
            )
        )
        maxima.append(row_max)
        totals.append(row_total)
    return (jnp.concatenate(results, axis=0), maxima, totals)


def attend_backward(queries, key_rows, value_rows, starts, score_scale, grad_out, maxima, totals):
    length, heads_here, head_dim = queries.shape
    block_count, block_rows = block_layout(length)
    positions = jnp.arange(length, dtype=jnp.int32)
    grad_keys = jnp.zeros((length, heads_here, head_dim), jnp.float32)
    grad_values = jnp.zeros((length, heads_here, head_dim), jnp.float32)
    query_grads = []
    for block_index in range(block_count):
        row_first = block_index * block_rows
        row_end = row_first + block_rows
        query_block = queries[row_first:row_end]
        grad_block = grad_out[row_first:row_end]
        scores = score_block(
            query_block,
            positions[row_first:row_end],
            starts[row_first:row_end],
            key_rows[:row_end],
            score_scale,
        )
        weights_full = jnp.exp(scores - maxima[block_index]) / totals[block_index]
        weights_low = weights_full.astype(jnp.bfloat16)
        grad_weights = jnp.einsum(
            "qhd,khd->hqk", grad_block, value_rows[:row_end], preferred_element_type=jnp.float32
        )
        inner = jnp.sum(weights_full * grad_weights, axis=-1, keepdims=True)
        grad_scores = (weights_full * (grad_weights - inner)).astype(jnp.bfloat16)
        query_grads.append(
            jnp.einsum(
                "hqk,khd->qhd", grad_scores, key_rows[:row_end], preferred_element_type=jnp.float32
            )
            * score_scale
        )
        grad_keys = grad_keys.at[:row_end].add(
            jnp.einsum("hqk,qhd->khd", grad_scores, query_block, preferred_element_type=jnp.float32)
            * score_scale
        )
        grad_values = grad_values.at[:row_end].add(
            jnp.einsum("hqk,qhd->khd", weights_low, grad_block, preferred_element_type=jnp.float32)
        )
    return (jnp.concatenate(query_grads, axis=0), grad_keys, grad_values)


def local_any(
    tokens,
    seq_start,
    qkv_weight,
    out_weight,
    fc1_weight,
    fc2_weight,
    norm_gain,
    norm_bias,
    mid_gain,
    mid_bias,
    head_scale,
    cotangent,
):
    split_count = lax.axis_size("sp")
    split_rank = lax.axis_index("sp")
    local_rows, width_model = tokens.shape
    group_rows = seq_start.shape[0]
    heads_here = H // split_count
    head_width = heads_here * HD
    score_scale = 1.0 / math.sqrt(HD)
    scale_here = lax.dynamic_slice_in_dim(head_scale, split_rank * heads_here, heads_here, axis=1)
    hidden = tokens.astype(jnp.float32)
    kept_layers = []
    kept_matrices = []
    for which_layer in range(LAYERS):
        matrices = (
            lax.all_gather(qkv_weight[which_layer], "dp", axis=0, tiled=True),
            lax.all_gather(out_weight[which_layer], "dp", axis=0, tiled=True),
            lax.all_gather(fc1_weight[which_layer], "dp", axis=0, tiled=True),
            lax.all_gather(fc2_weight[which_layer], "dp", axis=0, tiled=True),
        )
        qkv_full, out_full, up_full, down_full = matrices
        normed, norm_a, inv_a = norm_forward(
            hidden, norm_gain[which_layer, 0], norm_bias[which_layer, 0]
        )
        normed_low = normed.astype(jnp.bfloat16)
        project = (
            product(normed_low, qkv_full)
            .astype(jnp.bfloat16)
            .reshape(local_rows, 3, split_count, head_width)
        )
        by_heads = lax.all_to_all(project, "sp", split_axis=2, concat_axis=0, tiled=True)
        queries = by_heads[:, 0, 0].reshape(group_rows, heads_here, HD)
        key_rows = by_heads[:, 1, 0].reshape(group_rows, heads_here, HD)
        value_rows = by_heads[:, 2, 0].reshape(group_rows, heads_here, HD)
        attended, maxima, totals = attend_forward(
            queries, key_rows, value_rows, seq_start, score_scale
        )
        scaled = (
            (attended * scale_here[which_layer][None, :, None])
            .astype(jnp.bfloat16)
            .reshape(group_rows, 1, head_width)
        )
        gathered = lax.all_to_all(scaled, "sp", split_axis=0, concat_axis=1, tiled=True).reshape(
            local_rows, width_model
        )
        branch = product(gathered, out_full)
        branch_norm, norm_z, inv_z = norm_forward(
            branch, norm_gain[which_layer, 1], norm_bias[which_layer, 1]
        )
        middle = hidden + branch_norm
        normed_ff, norm_b, inv_b = norm_forward(
            middle, norm_gain[which_layer, 2], norm_bias[which_layer, 2]
        )
        ff_low = normed_ff.astype(jnp.bfloat16)
        pre_act = product(ff_low, up_full)
        activated = jax.nn.gelu(pre_act, approximate=False)
        mixed, norm_m, inv_m = norm_forward(activated, mid_gain[which_layer], mid_bias[which_layer])
        mixed_low = mixed.astype(jnp.bfloat16)
        hidden = middle + product(mixed_low, down_full)
        kept_layers.append(
            (
                norm_a,
                inv_a,
                normed_low,
                queries,
                key_rows,
                value_rows,
                attended,
                maxima,
                totals,
                gathered,
                norm_z,
                inv_z,
                norm_b,
                inv_b,
                ff_low,
                pre_act,
                norm_m,
                inv_m,
                mixed_low,
            )
        )
        kept_matrices.append(matrices)
    output = hidden.astype(jnp.bfloat16)
    grad_hidden = cotangent.astype(jnp.float32)
    matrix_grads = [None] * LAYERS
    gain_grads = [None] * LAYERS
    bias_grads = [None] * LAYERS
    mid_gain_grads = [None] * LAYERS
    mid_bias_grads = [None] * LAYERS
    scale_grads = [None] * LAYERS
    for which_layer in reversed(range(LAYERS)):
        (
            norm_a,
            inv_a,
            normed_low,
            queries,
            key_rows,
            value_rows,
            attended,
            maxima,
            totals,
            gathered,
            norm_z,
            inv_z,
            norm_b,
            inv_b,
            ff_low,
            pre_act,
            norm_m,
            inv_m,
            mixed_low,
        ) = kept_layers[which_layer]
        qkv_full, out_full, up_full, down_full = (
            lax.all_gather(qkv_weight[which_layer], "dp", axis=0, tiled=True),
            lax.all_gather(out_weight[which_layer], "dp", axis=0, tiled=True),
            lax.all_gather(fc1_weight[which_layer], "dp", axis=0, tiled=True),
            lax.all_gather(fc2_weight[which_layer], "dp", axis=0, tiled=True),
        )
        grad_final = grad_hidden.astype(jnp.bfloat16)
        grad_mixed = product(grad_final, down_full.T)
        grad_act, mid_gain_grad, mid_bias_grad = norm_backward(
            grad_mixed, norm_m, inv_m, mid_gain[which_layer]
        )
        gelu_value, gelu_pull = jax.vjp(partial(jax.nn.gelu, approximate=False), pre_act)
        grad_pre = gelu_pull(grad_act)[0].astype(jnp.bfloat16)
        grad_ff_in = product(grad_pre, up_full.T)
        grad_mid_in, gain_two, bias_two = norm_backward(
            grad_ff_in, norm_b, inv_b, norm_gain[which_layer, 2]
        )
        grad_middle = grad_hidden + grad_mid_in
        grad_branch_full, gain_one, bias_one = norm_backward(
            grad_middle, norm_z, inv_z, norm_gain[which_layer, 1]
        )
        grad_branch = grad_branch_full.astype(jnp.bfloat16)
        grad_gathered = (
            product(grad_branch, out_full.T)
            .astype(jnp.bfloat16)
            .reshape(local_rows, split_count, head_width)
        )
        grad_heads = lax.all_to_all(
            grad_gathered, "sp", split_axis=1, concat_axis=0, tiled=True
        ).reshape(group_rows, heads_here, HD)
        scale_grad_here = jnp.sum(grad_heads.astype(jnp.float32) * attended, axis=(0, 2))
        grad_attended = (grad_heads * scale_here[which_layer][None, :, None]).astype(jnp.bfloat16)
        grad_queries, grad_keys, grad_values = attend_backward(
            queries, key_rows, value_rows, seq_start, score_scale, grad_attended, maxima, totals
        )
        stacked = jnp.stack(
            [
                grad_queries.reshape(group_rows, head_width),
                grad_keys.reshape(group_rows, head_width),
                grad_values.reshape(group_rows, head_width),
            ],
            axis=1,
        )
        stacked = stacked.astype(jnp.bfloat16).reshape(group_rows, 3, 1, head_width)
        back_rows = lax.all_to_all(stacked, "sp", split_axis=0, concat_axis=2, tiled=True).reshape(
            local_rows, 3 * width_model
        )
        grad_normed = product(back_rows, qkv_full.T)
        grad_input, gain_zero, bias_zero = norm_backward(
            grad_normed, norm_a, inv_a, norm_gain[which_layer, 0]
        )
        grad_hidden = grad_middle + grad_input
        group_inputs = (
            lax.all_gather(normed_low, "sp", axis=0, tiled=True),
            lax.all_gather(gathered, "sp", axis=0, tiled=True),
            lax.all_gather(ff_low, "sp", axis=0, tiled=True),
            lax.all_gather(mixed_low, "sp", axis=0, tiled=True),
        )
        group_columns = (
            lax.all_to_all(
                back_rows.reshape(local_rows, split_count, -1),
                "sp",
                split_axis=1,
                concat_axis=0,
                tiled=True,
            ),
            lax.all_to_all(
                grad_branch.reshape(local_rows, split_count, -1),
                "sp",
                split_axis=1,
                concat_axis=0,
                tiled=True,
            ),
            lax.all_to_all(
                grad_pre.reshape(local_rows, split_count, -1),
                "sp",
                split_axis=1,
                concat_axis=0,
                tiled=True,
            ),
            lax.all_to_all(
                grad_final.reshape(local_rows, split_count, -1),
                "sp",
                split_axis=1,
                concat_axis=0,
                tiled=True,
            ),
        )
        terms = tuple(
            (
                product(group_inputs[which].T, group_columns[which].reshape(group_rows, -1))
                for which in range(4)
            )
        )
        matrix_grads[which_layer] = jax.tree.map(
            lambda part: part.astype(jnp.float32),
            lax.psum_scatter(for_sending(terms), "dp", scatter_dimension=0, tiled=True),
        )
        gain_grads[which_layer] = jnp.stack([gain_zero, gain_one, gain_two])
        bias_grads[which_layer] = jnp.stack([bias_zero, bias_one, bias_two])
        mid_gain_grads[which_layer] = mid_gain_grad
        mid_bias_grads[which_layer] = mid_bias_grad
        scale_grads[which_layer] = lax.dynamic_update_slice(
            jnp.zeros((H,), jnp.float32), scale_grad_here, (split_rank * heads_here,)
        )
    summed = tuple((jnp.stack([pieces[which] for pieces in matrix_grads]) for which in range(4)))
    small_sums = lax.psum(
        (
            jnp.stack(gain_grads),
            jnp.stack(bias_grads),
            jnp.stack(mid_gain_grads),
            jnp.stack(mid_bias_grads),
            jnp.stack(scale_grads),
        ),
        ("dp", "sp"),
    )
    return (
        output,
        grad_hidden,
        summed[0],
        summed[1],
        summed[2],
        summed[3],
        small_sums[0],
        small_sums[1],
        small_sums[2],
        small_sums[3],
        small_sums[4],
    )


def contract(left, right, left_axis, right_axis):
    return lax.dot_general(
        left, right, (((left_axis,), (right_axis,)), ((), ())), preferred_element_type=jnp.float32
    )


def head_parts(project_ref, head):
    span = project_ref.shape[1] // 3
    at = head * HD
    return (project_ref[:, base + at : base + at + HD] for base in (0, span, 2 * span))


def head_weights(queries, key_rows, allowed):
    scores = contract(queries, key_rows, 1, 1) * (1.0 / math.sqrt(HD))
    scores = jnp.where(allowed, scores, -1e30)
    exponent = jnp.exp(scores - jnp.max(scores, axis=-1, keepdims=True))
    return exponent / jnp.sum(exponent, axis=-1, keepdims=True)


def allowed_pairs(starts_ref):
    length = starts_ref.shape[0]
    row = lax.broadcasted_iota(jnp.int32, (length, length), 0)
    col = lax.broadcasted_iota(jnp.int32, (length, length), 1)
    return (col >= starts_ref[...]) & (col <= row)


def attention_forward(scale_ref, project_ref, starts_ref, scaled_ref):
    allowed = allowed_pairs(starts_ref)
    for pair in range(scaled_ref.shape[1] // (2 * HD)):
        parts = []
        for head in (2 * pair, 2 * pair + 1):
            queries, key_rows, value_rows = head_parts(project_ref, head)
            weights = head_weights(queries, key_rows, allowed).astype(jnp.bfloat16)
            attended = contract(weights, value_rows, 1, 0)
            parts.append((attended * scale_ref[head]).astype(jnp.bfloat16))
        at = 2 * HD * pair
        scaled_ref[:, at : at + 2 * HD] = jnp.concatenate(parts, axis=1)


def attention_backward(scale_ref, project_ref, starts_ref, grad_ref, out_ref, scale_grad_ref):
    allowed = allowed_pairs(starts_ref)
    span = grad_ref.shape[1]
    score_scale = 1.0 / math.sqrt(HD)
    for pair in range(span // (2 * HD)):
        parts = ([], [], [])
        sums = []
        for head in (2 * pair, 2 * pair + 1):
            queries, key_rows, value_rows = head_parts(project_ref, head)
            upstream = grad_ref[:, head * HD : head * HD + HD]
            weights = head_weights(queries, key_rows, allowed)
            weights_low = weights.astype(jnp.bfloat16)
            attended = contract(weights_low, value_rows, 1, 0)
            wide = upstream.astype(jnp.float32)
            sums.append(jnp.sum(wide * attended, axis=0, keepdims=True))
            grad_attended = (wide * scale_ref[head]).astype(jnp.bfloat16)
            grad_weights = contract(grad_attended, value_rows, 1, 1)
            inner = jnp.sum(weights * grad_weights, axis=-1, keepdims=True)
            grad_scores = (weights * (grad_weights - inner)).astype(jnp.bfloat16)
            parts[0].append(contract(grad_scores, key_rows, 1, 0) * score_scale)
            parts[1].append(contract(grad_scores, queries, 0, 0) * score_scale)
            parts[2].append(contract(weights_low, grad_attended, 0, 0))
        at = 2 * HD * pair
        for which in range(3):
            both = jnp.concatenate(parts[which], axis=1).astype(jnp.bfloat16)
            out_ref[:, which * span + at : which * span + at + 2 * HD] = both
        scale_grad_ref[pair : pair + 1, :] = jnp.concatenate(sums, axis=1)


def pack_columns(place_ref, qkv_ref, up_ref, own_ref, there_ref):
    core, near = place_ref[0], place_ref[1]
    layers, shard, width = qkv_ref.shape
    span = width // 2
    blocks = up_ref.shape[2] // 512
    for layer in range(layers):
        for at in range(0, width, 256):
            parts = [qkv_ref[layer, :, at + HD * i : at + HD * (i + 1)] for i in range(4)]
            even = jnp.concatenate([parts[0], parts[2]], axis=1)
            odd = jnp.concatenate([parts[1], parts[3]], axis=1)

            @pl.when(core == 0)
            def _():
                own_ref[layer, :, at // 2 : at // 2 + 128] = even
                there_ref[layer, :, at // 2 : at // 2 + 128] = odd

            @pl.when(core == 1)
            def _():
                own_ref[layer, :, at // 2 : at // 2 + 128] = odd
                there_ref[layer, :, at // 2 : at // 2 + 128] = even

        for out_ref, which in ((own_ref, core), (there_ref, 1 - core)):
            for part, side in enumerate((near, 1 - near)):
                for block in range(blocks):
                    at = span + (part * blocks + block) * 128
                    source = pl.multiple_of(block * 512 + which * 256 + side * 128, 128)
                    out_ref[layer, :, at : at + 128] = up_ref[layer, :, pl.ds(source, 128)]


def pack_rows(place_ref, own_ref, there_ref, out_ref, down_ref, *units):
    core, near = place_ref[0], place_ref[1]
    layers, shard, width = out_ref.shape
    half = width // 2
    span = own_ref.shape[2] - 2 * width
    first, second, up, *downs = units
    attention, ups = (first, second.at[:, : 2 * width]), (up, second.at[:, 2 * width :])
    for layer in range(layers):
        for source_ref, which in ((own_ref, core), (there_ref, 1 - core)):
            rows = pl.ds(pl.multiple_of(which * shard, shard), shard)
            attention[layer][rows, :span] = source_ref[layer, :, :span]
            ups[layer][rows, :] = source_ref[layer, :, span : span + width]
        attention[layer][:shard, span:] = out_ref[layer, :, :half]
        attention[layer][shard:, span:] = out_ref[layer, :, half:]
        for part in range(downs[layer].shape[1] // width):
            side = near if part == 0 else 1 - near
            rows = pl.ds(pl.multiple_of(side * 2 * shard, 2 * shard), 2 * shard)
            downs[layer][:, part * width : part * width + width] = down_ref[layer, rows, :]


def term_product(arrays, parts, shape):
    def body(left_ref, left_there_ref, right_ref, right_there_ref, out_ref):
        for left_at, right_at, columns, out_at in parts:
            right = right_ref[:, right_at : right_at + columns]
            right_there = right_there_ref[:, right_at : right_at + columns]
            for row in range(0, shape[0], 256):
                left = left_ref[:, left_at + row : left_at + row + 256]
                left_there = left_there_ref[:, left_at + row : left_at + row + 256]
                total = contract(left, right, 0, 0) + contract(left_there, right_there, 0, 0)
                out_ref[row : row + 256, out_at : out_at + columns] = total.astype(jnp.bfloat16)

    vmem = pl.BlockSpec(memory_space=pltpu.VMEM)
    return pl.pallas_call(
        body,
        out_shape=jax.ShapeDtypeStruct(shape, jnp.bfloat16),
        in_specs=[vmem] * 4,
        out_specs=vmem,
    )(*arrays)


def run_small(body, scale, arrays, outs):
    vmem = pl.BlockSpec(memory_space=pltpu.VMEM)
    return pl.pallas_call(
        body,
        out_shape=[jax.ShapeDtypeStruct(*out) for out in outs],
        in_specs=[pl.BlockSpec(memory_space=pltpu.SMEM)] + [vmem] * len(arrays),
        out_specs=[vmem] * len(outs),
    )(scale, *arrays)


SWAP = ((0, 1), (1, 0))


def swap(array, axis):
    return lax.ppermute(array, axis, SWAP)


def turn(array):
    return lax.ppermute(array, ("c", "y"), ((0, 0), (1, 2), (2, 1), (3, 3)))


def norm_parts(values):
    center = values - jnp.mean(values, axis=-1, keepdims=True)
    inverse = lax.rsqrt(jnp.mean(center * center, axis=-1, keepdims=True) + norm_eps)
    return center * inverse, inverse


def local_chip(
    tokens,
    seq_start,
    qkv_weight,
    out_weight,
    fc1_weight,
    fc2_weight,
    norm_gain,
    norm_bias,
    mid_gain,
    mid_bias,
    head_scale,
    cotangent,
):
    nz, nx = lax.axis_size("z"), lax.axis_size("x")
    iz, ix, ic, iy = (lax.axis_index(name) for name in ("z", "x", "c", "y"))
    chips = nz * nx
    rows, width = tokens.shape
    group_rows = seq_start.shape[0]
    hidden_width = fc1_weight.shape[2]
    shard = qkv_weight.shape[1]
    block = hidden_width // (4 * chips)
    heads_here = H // 2
    head_width = width // 2
    units = hidden_width // 2
    half_units = units // 2
    half = width // 2
    wide = 3 * head_width // 2
    f32, bf16 = jnp.float32, jnp.bfloat16

    def pick(array, which, axis):
        return lax.dynamic_index_in_dim(array, which, axis, keepdims=False)

    def cores(own, other, axis=0):
        first = jnp.where(ic == 0, own, other)
        second = jnp.where(ic == 0, other, own)
        return jnp.concatenate([first, second], axis=axis)

    def both_cores(partial_sum):
        low = lax.optimization_barrier(partial_sum.astype(bf16))
        return low.astype(f32) + swap(low, "c").astype(f32)

    def ordered(first, second, axis):
        near = jnp.where(iy == 0, first, second)
        far = jnp.where(iy == 0, second, first)
        return jnp.concatenate([near, far], axis=axis)

    def gather(array):
        return lax.all_gather(array, ("z", "x"), axis=0, tiled=True)

    def scatter(array):
        return lax.psum_scatter(
            array.astype(bf16), ("z", "x"), scatter_dimension=0, tiled=True
        ).astype(f32)

    def step_x(array):
        split = array.reshape(nz, nx, -1, array.shape[1])
        there = swap(pick(split, 1 - ix, 1).astype(bf16), "x")
        return pick(split, ix, 1).astype(f32) + there.astype(f32)

    def step_z(array):
        total = pick(array, iz, 0)
        for step in range(1, nz):
            there = pick(array, (iz + step) % nz, 0).astype(bf16)
            ring = [(i, (i + step) % nz) for i in range(nz)]
            total = total + lax.ppermute(there, "z", ring).astype(f32)
        return total

    def steps(array):
        return step_z(step_x(array))

    def tie(value, *others):
        return lax.optimization_barrier((value,) + others)

    def z_pieces(array):
        return [array] + [
            lax.ppermute(array, "z", [(i, (i + step) % nz) for i in range(nz)])
            for step in range(1, nz)
        ]

    def join(pieces):
        held = jnp.zeros((nz, nx) + pieces[0].shape, pieces[0].dtype)
        for step, piece in enumerate(pieces):
            for at_x, part in ((ix, piece), (1 - ix, swap(piece, "x"))):
                at = ((iz - step) % nz, at_x, 0, 0)
                held = lax.dynamic_update_slice(held, part[None, None], at)
        return held.reshape(-1, pieces[0].shape[1])

    place = jnp.stack([ic, iy]).astype(jnp.int32)
    narrow = (LAYERS, shard, 3 * head_width + units)
    own, there = run_small(
        pack_columns, place, (qkv_weight, fc1_weight), [(narrow, bf16), (narrow, bf16)]
    )
    wides = (4 * head_width, 4 * head_width + width, width, width, 2 * width)
    packed = run_small(
        pack_rows,
        place,
        (own, swap(there, "c"), out_weight, fc2_weight),
        [((2 * shard, columns), bf16) for columns in wides],
    )
    got = []
    for unit in (packed[0], packed[2], packed[3]):
        if got:
            unit, got[-1][1] = tie(unit, got[-1][1])
        got.append(z_pieces(unit))
    late = packed[1]
    late, *got[0] = tie(late, *got[0])
    late = gather(late)
    got = [join(pieces) for pieces in got]
    last_down = gather(packed[4])
    last_up = late[:, 4 * head_width :]
    ups = [(got[1], swap(got[1], "y")), (last_up, swap(last_up, "y"))]
    downs = [(got[2], swap(got[2], "y")), (last_down[:, :width], last_down[:, width:])]
    attention_mats = [got[0], late]

    def matrices(which):
        packed = attention_mats[which]
        qkv = packed[:, : 3 * head_width]
        out = packed[:, 3 * head_width : 4 * head_width].reshape(chips, 2, shard, half)
        out = jnp.concatenate(
            [out[:, 0].reshape(head_width, half), out[:, 1].reshape(head_width, half)], axis=1
        )
        return qkv, out, ups[which], downs[which]

    def mine_of(vector):
        mine = pick(vector.reshape(chips, 2, 2, block), ic, 1)
        return ordered(mine[:, 0].reshape(-1), mine[:, 1].reshape(-1), 0)

    def slice_of(values, first, size):
        return lax.dynamic_slice_in_dim(values, first, size, 1)

    turned = turn(tokens)
    hidden = cores(turned, swap(turned, "c")).astype(f32)
    starts = jnp.where(ic == iy, seq_start, swap(seq_start, "c"))
    starts = starts[:, None]

    cotangent_late, attention_mats[0] = tie(cotangent, attention_mats[0])
    mats = [matrices(which) for which in range(LAYERS)]
    kept = []
    for which in range(LAYERS):
        qkv_mat, out_mat, up_mat, down_mat = mats[which]
        scale_here = pick(head_scale[which].reshape(heads_here, 2), ic, 1)
        if which == 1:
            hidden, far_up = tie(hidden, up_mat[1])
            up_mat = (up_mat[0], far_up)
            mats[1] = (qkv_mat, out_mat, up_mat, down_mat)
        norm_a, inv_a = norm_parts(hidden)
        a_low = (norm_a * norm_gain[which, 0] + norm_bias[which, 0]).astype(bf16)
        project = product(a_low, qkv_mat).astype(bf16)
        (scaled,) = run_small(
            attention_forward, scale_here, (project, starts), [((group_rows, head_width), bf16)]
        )
        branch = both_cores(product(scaled, out_mat))
        if which == 0:
            branch, far_up, far_down = tie(branch, up_mat[1], down_mat[1])
            up_mat, down_mat = (up_mat[0], far_up), (down_mat[0], far_down)
            mats[0] = (qkv_mat, out_mat, up_mat, down_mat)
        norm_z, inv_z = norm_parts(branch)
        middle = hidden + norm_z * norm_gain[which, 1] + norm_bias[which, 1]
        norm_b, inv_b = norm_parts(middle)
        b_low = (norm_b * norm_gain[which, 2] + norm_bias[which, 2]).astype(bf16)
        pre_act = jnp.concatenate([product(b_low, part) for part in up_mat], axis=1)
        below = 0.5 * (1.0 + lax.erf(pre_act * (1.0 / math.sqrt(2.0))))
        activated = pre_act * below
        mean_here = jnp.mean(activated, axis=-1)
        center = activated - mean_here[:, None]
        stats = jnp.stack([mean_here, jnp.mean(center * center, axis=-1)])
        stats_there = swap(stats, "c")
        mean_all = 0.5 * (stats[0] + stats_there[0])
        apart = 0.5 * (stats[0] - stats_there[0])
        spread = 0.5 * (stats[1] + stats_there[1]) + apart * apart
        inv_m = lax.rsqrt(spread + norm_eps)[:, None]
        norm_m = (activated - mean_all[:, None]) * inv_m
        gain_m, bias_m = mine_of(mid_gain[which]), mine_of(mid_bias[which])
        mixed_low = (norm_m * gain_m + bias_m).astype(bf16)
        if which == 1:
            last = kept[0]
            mixed_low, there_a, there_h = tie(mixed_low, last[-3], last[-1])
            kept[0] = last[:-3] + (there_a, last[-2], there_h)
        near, far = mixed_low[:, :half_units], mixed_low[:, half_units:]
        hidden = middle + both_cores(product(near, down_mat[0]) + product(far, down_mat[1]))
        attention_in = jnp.concatenate([a_low, scaled], axis=1)
        hidden_in = jnp.concatenate([b_low, mixed_low], axis=1)
        hidden_there = swap(jnp.concatenate([b_low, far, near], axis=1), "y")
        attention_there = swap(attention_in, "y")
        kept.append(
            (
                norm_a, inv_a, project, scale_here, norm_z, inv_z, norm_b, inv_b, pre_act, below, norm_m, inv_m, gain_m,
                attention_in, attention_there, hidden_in, hidden_there,
            )
        )
    output = lax.dynamic_slice_in_dim(hidden.astype(bf16), ic * rows, rows, 0)
    turned = turn(cotangent_late)
    grad_hidden = cores(turned, swap(turned, "c")).astype(f32)

    def natural(values):
        return ordered(values[:half_units], values[half_units:], 0)

    vectors, pending = [None] * LAYERS, [None] * LAYERS
    for which in reversed(range(LAYERS)):
        qkv_mat, out_mat, up_mat, down_mat = mats[which]
        (
            norm_a, inv_a, project, scale_here, norm_z, inv_z, norm_b, inv_b, pre_act, below, norm_m, inv_m, gain_m,
            attention_in, attention_there, hidden_in, hidden_there,
        ) = kept[which]
        final_low = grad_hidden.astype(bf16)
        grad_mixed = jnp.concatenate([product(final_low, part.T) for part in down_mat], axis=1)
        mid_gain_grad = jnp.sum(grad_mixed * norm_m, axis=0)
        mid_bias_grad = jnp.sum(grad_mixed, axis=0)
        scaled_grad = grad_mixed * gain_m
        sums = jnp.stack([jnp.sum(scaled_grad, axis=-1), jnp.sum(scaled_grad * norm_m, axis=-1)])
        sums = (sums + swap(sums, "c")) / hidden_width
        grad_act = inv_m * (scaled_grad - sums[0][:, None] - norm_m * sums[1][:, None])
        slope = below + pre_act * jnp.exp(-0.5 * pre_act * pre_act) * (1.0 / math.sqrt(2 * math.pi))
        grad_pre = (grad_act * slope).astype(bf16)
        if which == 0:
            grad_pre, at_there = tie(grad_pre, at_there)
            later = finish_attention(at_there)
        near, far = grad_pre[:, :half_units], grad_pre[:, half_units:]

        def unit_columns(side):
            first = side * (half_units // 2)
            return (
                slice_of(near, first, half_units // 2),
                slice_of(far, first, half_units // 2),
                slice_of(final_low, side * half, half),
            )

        keep_n, keep_f, keep_c = unit_columns(iy)
        send_n, send_f, send_c = unit_columns(1 - iy)
        ff_there = swap(jnp.concatenate([send_f, send_n, send_c], axis=1), "y")
        ff_out = jnp.concatenate([keep_n, keep_f, keep_c], axis=1)
        grad_ff_in = both_cores(product(near, up_mat[0].T) + product(far, up_mat[1].T))
        grad_mid_in, gain_two, bias_two = norm_backward(
            grad_ff_in, norm_b, inv_b, norm_gain[which, 2]
        )
        grad_middle = grad_hidden + grad_mid_in
        grad_branch, gain_one, bias_one = norm_backward(
            grad_middle, norm_z, inv_z, norm_gain[which, 1]
        )
        branch_low = grad_branch.astype(bf16)
        if which == 0:
            branch_low, later = tie(branch_low, later)
            later = step_x(later)
        grad_heads = product(branch_low, out_mat.T).astype(bf16)
        grad_project, scale_grad = run_small(
            attention_backward,
            scale_here,
            (project, starts, grad_heads),
            [((group_rows, 3 * head_width), bf16), ((heads_here // 2, 2 * HD), f32)],
        )
        scale_grad = jnp.sum(scale_grad.reshape(heads_here, HD), axis=1)
        grad_normed = both_cores(product(grad_project, qkv_mat.T))
        grad_input, gain_zero, bias_zero = norm_backward(
            grad_normed, norm_a, inv_a, norm_gain[which, 0]
        )

        at_out = jnp.concatenate(
            [slice_of(grad_project, iy * wide, wide), slice_of(branch_low, iy * half, half)], axis=1
        )
        at_there = jnp.concatenate(
            [
                slice_of(grad_project, (1 - iy) * wide, wide),
                slice_of(branch_low, (1 - iy) * half, half),
            ],
            axis=1,
        )
        at_there = swap(at_there, "y")
        if which == 1:
            grad_input, ff_there, hidden_there, attention_there = tie(
                grad_input, ff_there, hidden_there, attention_there
            )
        ff_term = term_product(
            (hidden_in, hidden_there, ff_out, ff_there),
            ((0, 0, width, 0), (width, width, half, width), (2 * width, width, half, width + half)),
            (width, 2 * width),
        )
        grad_hidden = grad_middle + grad_input
        if which == 1:
            grad_hidden, ff_term = tie(grad_hidden, ff_term)
            ff_rows = scatter(ff_term)
        else:
            ff_rows = jnp.concatenate(
                [steps(ff_term[:, :width]), steps(ff_term[:, width:])], axis=1
            )

        def attention_term(there, here=at_out, ins=attention_in, ins_there=attention_there):
            split = half // 2
            out_term = term_product(
                (ins[:, width:], ins_there[:, width:], here[:, wide:], there[:, wide:]),
                ((0, 0, half, 0),),
                (head_width, half),
            ).reshape(chips, shard, half)
            out_term = jnp.concatenate([out_term[..., :split], out_term[..., split:]], axis=1)
            qkv_term = term_product((ins, ins_there, here, there), ((0, 0, wide, 0),), (width, wide))
            return jnp.concatenate([qkv_term, out_term.reshape(-1, split)], axis=1)

        if which == 1:
            finish_attention = attention_term
        else:
            grad_hidden, later = tie(grad_hidden, later)
            at_rows_last = step_z(later)
            at_rows = step_x(attention_term(at_there))
        pending[which] = ff_rows
        shared = jnp.concatenate([gain_zero, gain_one, gain_two, bias_zero, bias_one, bias_two])
        vectors[which] = jnp.concatenate(
            [0.5 * shared, natural(mid_gain_grad), natural(mid_bias_grad), jnp.pad(scale_grad, (0, 128 - heads_here))]
        )

    vector = jnp.stack(vectors)
    vector = vector + swap(vector, "y")
    vector, at_rows, output = tie(vector, at_rows, output)
    at_rows = step_z(at_rows)
    vector = vector + swap(vector, "x")
    matrix_grads = []
    for at_rows, ff_rows in ((at_rows, pending[0]), (at_rows_last, pending[1])):
        grad_out = at_rows[:, wide:].reshape(2, shard, half // 2)
        grad_out = jnp.concatenate([grad_out[0], grad_out[1]], axis=1)
        down_near, down_far = ff_rows[:, width : width + half], ff_rows[:, width + half :]
        grad_down = jnp.concatenate(
            [jnp.where(iy == 0, down_near, down_far), jnp.where(iy == 0, down_far, down_near)], axis=0
        )
        mixed_rows = jnp.concatenate([at_rows[:, :wide], ff_rows[:, :width]], axis=1)
        mixed_rows = mixed_rows.reshape(2, shard, -1)
        own = pick(mixed_rows, ic, 0)
        other = swap(pick(mixed_rows, 1 - ic, 0).astype(bf16), "c").astype(f32)
        columns = cores(own[None], other[None])
        grad_qkv = columns[:, :, :wide].reshape(2, shard, wide // HD, HD)
        grad_qkv = grad_qkv.transpose(1, 2, 0, 3).reshape(shard, 2 * wide)
        near, far = columns[:, :, wide : wide + half], columns[:, :, wide + half :]
        grad_up = jnp.stack(
            [jnp.where(iy == 0, near, far), jnp.where(iy == 0, far, near)], axis=2
        ).reshape(2, shard, 2, chips // 2, block)
        grad_up = grad_up.transpose(1, 3, 0, 2, 4).reshape(shard, 2 * width)
        matrix_grads.append((grad_qkv, grad_out, grad_up, grad_down))

    grad_tokens = turn(lax.dynamic_slice_in_dim(grad_hidden, ic * rows, rows, 0))
    output = turn(output)
    for bit in (1, 2):
        vector = vector + lax.ppermute(vector, "z", [(i, i ^ bit) for i in range(nz)])
    there = swap(vector, "c")
    shared = vector[:, : 6 * width] + there[:, : 6 * width]

    def spread_units(first):
        view = (LAYERS, 2, chips, 1, block)
        own, other = (part[:, first : first + units] for part in (vector, there))
        own, other = own.reshape(view), other.reshape(view)
        return cores(own, other, 3).transpose(0, 2, 3, 1, 4).reshape(LAYERS, hidden_width)

    scale_at = 6 * width + 2 * units
    own, other = (
        part[:, scale_at : scale_at + heads_here].reshape(LAYERS, heads_here, 1)
        for part in (vector, there)
    )
    summed = [jnp.stack([grads[which] for grads in matrix_grads]) for which in range(4)]
    return (
        output,
        grad_tokens,
        summed[0],
        summed[1],
        summed[2],
        summed[3],
        shared[:, : 3 * width].reshape(LAYERS, 3, width),
        shared[:, 3 * width :].reshape(LAYERS, 3, width),
        spread_units(6 * width),
        spread_units(6 * width + units),
        cores(own, other, 2).reshape(LAYERS, H),
    )


def solution(mesh):
    dp, sp = mesh.shape["dp"], mesh.shape["sp"]
    if sp == 2 and dp == 16:
        mesh = Mesh(mesh.devices.reshape(4, dp // 8, 2, 2), ("z", "x", "c", "y"))
        rows, every, cols, body = ("z", "x", "c"), ("z", "x", "c", "y"), "y", local_chip
    else:
        rows, every, cols, body = "dp", ("dp", "sp"), "sp", local_any
    weight = P(None, rows, None)
    in_specs = (P(every, None), P(rows), weight, weight, weight, weight)
    in_specs = in_specs + (P(),) * 5 + (P(every, None),)
    grad = P(None, rows, cols)
    out_specs = (P(every, None), P(every, None), grad, grad, grad, grad) + (P(),) * 5
    return jax.shard_map(body, mesh=mesh, in_specs=in_specs, out_specs=out_specs, check_vma=False)
```

```python
from functools import partial
import math

import jax
import jax.numpy as jnp
from jax import lax
from jax.experimental import pallas as pl
from jax.experimental.pallas import tpu as pltpu
from jax.sharding import Mesh, PartitionSpec as P

H = 16
HD = 64
LAYERS = 2


norm_eps = 1e-05


def for_sending(array):

    def short(part):
        return part.astype(jnp.bfloat16) if part.dtype == jnp.float32 else part

    return jax.tree.map(short, array)


def norm_forward(values, gain, bias):
    center = values - jnp.mean(values, axis=-1, keepdims=True)
    inverse = lax.rsqrt(jnp.mean(center * center, axis=-1, keepdims=True) + norm_eps)
    normal = center * inverse
    return (normal * gain + bias, normal, inverse)


def norm_backward(upstream, normal, inverse, gain):
    scaled = upstream * gain
    grad_values = inverse * (
        scaled
        - jnp.mean(scaled, axis=-1, keepdims=True)
        - normal * jnp.mean(scaled * normal, axis=-1, keepdims=True)
    )
    return (grad_values, jnp.sum(upstream * normal, axis=0), jnp.sum(upstream, axis=0))


def product(left, right):
    return jnp.dot(left, right, preferred_element_type=jnp.float32)


def block_layout(length):
    block_count = min(4, max(1, length // 512))
    return (block_count, length // block_count)


def score_block(query_block, query_pos, query_start, key_rows, score_scale):
    key_pos = jnp.arange(key_rows.shape[0], dtype=jnp.int32)
    scores = (
        jnp.einsum("qhd,khd->hqk", query_block, key_rows, preferred_element_type=jnp.float32)
        * score_scale
    )
    allowed = (key_pos[None, :] >= query_start[:, None]) & (key_pos[None, :] <= query_pos[:, None])
    return jnp.where(allowed[None], scores, -1e30)


def attend_forward(queries, key_rows, value_rows, starts, score_scale):
    length = queries.shape[0]
    block_count, block_rows = block_layout(length)
    positions = jnp.arange(length, dtype=jnp.int32)
    results, maxima, totals = ([], [], [])
    for block_index in range(block_count):
        row_first = block_index * block_rows
        row_end = row_first + block_rows
        scores = score_block(
            queries[row_first:row_end],
            positions[row_first:row_end],
            starts[row_first:row_end],
            key_rows[:row_end],
            score_scale,
        )
        row_max = jnp.max(scores, axis=-1, keepdims=True)
        exponent = jnp.exp(scores - row_max)
        row_total = jnp.sum(exponent, axis=-1, keepdims=True)
        weights_low = (exponent / row_total).astype(jnp.bfloat16)
        results.append(
            jnp.einsum(
                "hqk,khd->qhd",
                weights_low,
                value_rows[:row_end],
                preferred_element_type=jnp.float32,
            )
        )
        maxima.append(row_max)
        totals.append(row_total)
    return (jnp.concatenate(results, axis=0), maxima, totals)


def attend_backward(queries, key_rows, value_rows, starts, score_scale, grad_out, maxima, totals):
    length, heads_here, head_dim = queries.shape
    block_count, block_rows = block_layout(length)
    positions = jnp.arange(length, dtype=jnp.int32)
    grad_keys = jnp.zeros((length, heads_here, head_dim), jnp.float32)
    grad_values = jnp.zeros((length, heads_here, head_dim), jnp.float32)
    query_grads = []
    for block_index in range(block_count):
        row_first = block_index * block_rows
        row_end = row_first + block_rows
        query_block = queries[row_first:row_end]
        grad_block = grad_out[row_first:row_end]
        scores = score_block(
            query_block,
            positions[row_first:row_end],
            starts[row_first:row_end],
            key_rows[:row_end],
            score_scale,
        )
        weights_full = jnp.exp(scores - maxima[block_index]) / totals[block_index]
        weights_low = weights_full.astype(jnp.bfloat16)
        grad_weights = jnp.einsum(
            "qhd,khd->hqk", grad_block, value_rows[:row_end], preferred_element_type=jnp.float32
        )
        inner = jnp.sum(weights_full * grad_weights, axis=-1, keepdims=True)
        grad_scores = (weights_full * (grad_weights - inner)).astype(jnp.bfloat16)
        query_grads.append(
            jnp.einsum(
                "hqk,khd->qhd", grad_scores, key_rows[:row_end], preferred_element_type=jnp.float32
            )
            * score_scale
        )
        grad_keys = grad_keys.at[:row_end].add(
            jnp.einsum("hqk,qhd->khd", grad_scores, query_block, preferred_element_type=jnp.float32)
            * score_scale
        )
        grad_values = grad_values.at[:row_end].add(
            jnp.einsum("hqk,qhd->khd", weights_low, grad_block, preferred_element_type=jnp.float32)
        )
    return (jnp.concatenate(query_grads, axis=0), grad_keys, grad_values)


def local_any(
    tokens,
    seq_start,
    qkv_weight,
    out_weight,
    fc1_weight,
    fc2_weight,
    norm_gain,
    norm_bias,
    mid_gain,
    mid_bias,
    head_scale,
    cotangent,
):
    split_count = lax.axis_size("sp")
    split_rank = lax.axis_index("sp")
    local_rows, width_model = tokens.shape
    group_rows = seq_start.shape[0]
    heads_here = H // split_count
    head_width = heads_here * HD
    score_scale = 1.0 / math.sqrt(HD)
    scale_here = lax.dynamic_slice_in_dim(head_scale, split_rank * heads_here, heads_here, axis=1)
    hidden = tokens.astype(jnp.float32)
    kept_layers = []
    kept_matrices = []
    for which_layer in range(LAYERS):
        matrices = (
            lax.all_gather(qkv_weight[which_layer], "dp", axis=0, tiled=True),
            lax.all_gather(out_weight[which_layer], "dp", axis=0, tiled=True),
            lax.all_gather(fc1_weight[which_layer], "dp", axis=0, tiled=True),
            lax.all_gather(fc2_weight[which_layer], "dp", axis=0, tiled=True),
        )
        qkv_full, out_full, up_full, down_full = matrices
        normed, norm_a, inv_a = norm_forward(
            hidden, norm_gain[which_layer, 0], norm_bias[which_layer, 0]
        )
        normed_low = normed.astype(jnp.bfloat16)
        project = (
            product(normed_low, qkv_full)
            .astype(jnp.bfloat16)
            .reshape(local_rows, 3, split_count, head_width)
        )
        by_heads = lax.all_to_all(project, "sp", split_axis=2, concat_axis=0, tiled=True)
        queries = by_heads[:, 0, 0].reshape(group_rows, heads_here, HD)
        key_rows = by_heads[:, 1, 0].reshape(group_rows, heads_here, HD)
        value_rows = by_heads[:, 2, 0].reshape(group_rows, heads_here, HD)
        attended, maxima, totals = attend_forward(
            queries, key_rows, value_rows, seq_start, score_scale
        )
        scaled = (
            (attended * scale_here[which_layer][None, :, None])
            .astype(jnp.bfloat16)
            .reshape(group_rows, 1, head_width)
        )
        gathered = lax.all_to_all(scaled, "sp", split_axis=0, concat_axis=1, tiled=True).reshape(
            local_rows, width_model
        )
        branch = product(gathered, out_full)
        branch_norm, norm_z, inv_z = norm_forward(
            branch, norm_gain[which_layer, 1], norm_bias[which_layer, 1]
        )
        middle = hidden + branch_norm
        normed_ff, norm_b, inv_b = norm_forward(
            middle, norm_gain[which_layer, 2], norm_bias[which_layer, 2]
        )
        ff_low = normed_ff.astype(jnp.bfloat16)
        pre_act = product(ff_low, up_full)
        activated = jax.nn.gelu(pre_act, approximate=False)
        mixed, norm_m, inv_m = norm_forward(activated, mid_gain[which_layer], mid_bias[which_layer])
        mixed_low = mixed.astype(jnp.bfloat16)
        hidden = middle + product(mixed_low, down_full)
        kept_layers.append(
            (
                norm_a,
                inv_a,
                normed_low,
                queries,
                key_rows,
                value_rows,
                attended,
                maxima,
                totals,
                gathered,
                norm_z,
                inv_z,
                norm_b,
                inv_b,
                ff_low,
                pre_act,
                norm_m,
                inv_m,
                mixed_low,
            )
        )
        kept_matrices.append(matrices)
    output = hidden.astype(jnp.bfloat16)
    grad_hidden = cotangent.astype(jnp.float32)
    matrix_grads = [None] * LAYERS
    gain_grads = [None] * LAYERS
    bias_grads = [None] * LAYERS
    mid_gain_grads = [None] * LAYERS
    mid_bias_grads = [None] * LAYERS
    scale_grads = [None] * LAYERS
    for which_layer in reversed(range(LAYERS)):
        (
            norm_a,
            inv_a,
            normed_low,
            queries,
            key_rows,
            value_rows,
            attended,
            maxima,
            totals,
            gathered,
            norm_z,
            inv_z,
            norm_b,
            inv_b,
            ff_low,
            pre_act,
            norm_m,
            inv_m,
            mixed_low,
        ) = kept_layers[which_layer]
        qkv_full, out_full, up_full, down_full = (
            lax.all_gather(qkv_weight[which_layer], "dp", axis=0, tiled=True),
            lax.all_gather(out_weight[which_layer], "dp", axis=0, tiled=True),
            lax.all_gather(fc1_weight[which_layer], "dp", axis=0, tiled=True),
            lax.all_gather(fc2_weight[which_layer], "dp", axis=0, tiled=True),
        )
        grad_final = grad_hidden.astype(jnp.bfloat16)
        grad_mixed = product(grad_final, down_full.T)
        grad_act, mid_gain_grad, mid_bias_grad = norm_backward(
            grad_mixed, norm_m, inv_m, mid_gain[which_layer]
        )
        gelu_value, gelu_pull = jax.vjp(partial(jax.nn.gelu, approximate=False), pre_act)
        grad_pre = gelu_pull(grad_act)[0].astype(jnp.bfloat16)
        grad_ff_in = product(grad_pre, up_full.T)
        grad_mid_in, gain_two, bias_two = norm_backward(
            grad_ff_in, norm_b, inv_b, norm_gain[which_layer, 2]
        )
        grad_middle = grad_hidden + grad_mid_in
        grad_branch_full, gain_one, bias_one = norm_backward(
            grad_middle, norm_z, inv_z, norm_gain[which_layer, 1]
        )
        grad_branch = grad_branch_full.astype(jnp.bfloat16)
        grad_gathered = (
            product(grad_branch, out_full.T)
            .astype(jnp.bfloat16)
            .reshape(local_rows, split_count, head_width)
        )
        grad_heads = lax.all_to_all(
            grad_gathered, "sp", split_axis=1, concat_axis=0, tiled=True
        ).reshape(group_rows, heads_here, HD)
        scale_grad_here = jnp.sum(grad_heads.astype(jnp.float32) * attended, axis=(0, 2))
        grad_attended = (grad_heads * scale_here[which_layer][None, :, None]).astype(jnp.bfloat16)
        grad_queries, grad_keys, grad_values = attend_backward(
            queries, key_rows, value_rows, seq_start, score_scale, grad_attended, maxima, totals
        )
        stacked = jnp.stack(
            [
                grad_queries.reshape(group_rows, head_width),
                grad_keys.reshape(group_rows, head_width),
                grad_values.reshape(group_rows, head_width),
            ],
            axis=1,
        )
        stacked = stacked.astype(jnp.bfloat16).reshape(group_rows, 3, 1, head_width)
        back_rows = lax.all_to_all(stacked, "sp", split_axis=0, concat_axis=2, tiled=True).reshape(
            local_rows, 3 * width_model
        )
        grad_normed = product(back_rows, qkv_full.T)
        grad_input, gain_zero, bias_zero = norm_backward(
            grad_normed, norm_a, inv_a, norm_gain[which_layer, 0]
        )
        grad_hidden = grad_middle + grad_input
        group_inputs = (
            lax.all_gather(normed_low, "sp", axis=0, tiled=True),
            lax.all_gather(gathered, "sp", axis=0, tiled=True),
            lax.all_gather(ff_low, "sp", axis=0, tiled=True),
            lax.all_gather(mixed_low, "sp", axis=0, tiled=True),
        )
        group_columns = (
            lax.all_to_all(
                back_rows.reshape(local_rows, split_count, -1),
                "sp",
                split_axis=1,
                concat_axis=0,
                tiled=True,
            ),
            lax.all_to_all(
                grad_branch.reshape(local_rows, split_count, -1),
                "sp",
                split_axis=1,
                concat_axis=0,
                tiled=True,
            ),
            lax.all_to_all(
                grad_pre.reshape(local_rows, split_count, -1),
                "sp",
                split_axis=1,
                concat_axis=0,
                tiled=True,
            ),
            lax.all_to_all(
                grad_final.reshape(local_rows, split_count, -1),
                "sp",
                split_axis=1,
                concat_axis=0,
                tiled=True,
            ),
        )
        terms = tuple(
            (
                product(group_inputs[which].T, group_columns[which].reshape(group_rows, -1))
                for which in range(4)
            )
        )
        matrix_grads[which_layer] = jax.tree.map(
            lambda part: part.astype(jnp.float32),
            lax.psum_scatter(for_sending(terms), "dp", scatter_dimension=0, tiled=True),
        )
        gain_grads[which_layer] = jnp.stack([gain_zero, gain_one, gain_two])
        bias_grads[which_layer] = jnp.stack([bias_zero, bias_one, bias_two])
        mid_gain_grads[which_layer] = mid_gain_grad
        mid_bias_grads[which_layer] = mid_bias_grad
        scale_grads[which_layer] = lax.dynamic_update_slice(
            jnp.zeros((H,), jnp.float32), scale_grad_here, (split_rank * heads_here,)
        )
    summed = tuple((jnp.stack([pieces[which] for pieces in matrix_grads]) for which in range(4)))
    small_sums = lax.psum(
        (
            jnp.stack(gain_grads),
            jnp.stack(bias_grads),
            jnp.stack(mid_gain_grads),
            jnp.stack(mid_bias_grads),
            jnp.stack(scale_grads),
        ),
        ("dp", "sp"),
    )
    return (
        output,
        grad_hidden,
        summed[0],
        summed[1],
        summed[2],
        summed[3],
        small_sums[0],
        small_sums[1],
        small_sums[2],
        small_sums[3],
        small_sums[4],
    )


def contract(left, right, left_axis, right_axis):
    return lax.dot_general(
        left, right, (((left_axis,), (right_axis,)), ((), ())), preferred_element_type=jnp.float32
    )


def head_parts(project_ref, head):
    span = project_ref.shape[1] // 3
    at = head * HD
    return (project_ref[:, base + at : base + at + HD] for base in (0, span, 2 * span))


def head_weights(queries, key_rows, allowed):
    scores = contract(queries, key_rows, 1, 1) * (1.0 / math.sqrt(HD))
    scores = jnp.where(allowed, scores, -1e30)
    exponent = jnp.exp(scores - jnp.max(scores, axis=-1, keepdims=True))
    return exponent / jnp.sum(exponent, axis=-1, keepdims=True)


def allowed_pairs(starts_ref):
    length = starts_ref.shape[0]
    row = lax.broadcasted_iota(jnp.int32, (length, length), 0)
    col = lax.broadcasted_iota(jnp.int32, (length, length), 1)
    return (col >= starts_ref[...]) & (col <= row)


def attention_forward(scale_ref, project_ref, starts_ref, scaled_ref):
    allowed = allowed_pairs(starts_ref)
    for pair in range(scaled_ref.shape[1] // (2 * HD)):
        parts = []
        for head in (2 * pair, 2 * pair + 1):
            queries, key_rows, value_rows = head_parts(project_ref, head)
            weights = head_weights(queries, key_rows, allowed).astype(jnp.bfloat16)
            attended = contract(weights, value_rows, 1, 0)
            parts.append((attended * scale_ref[head]).astype(jnp.bfloat16))
        at = 2 * HD * pair
        scaled_ref[:, at : at + 2 * HD] = jnp.concatenate(parts, axis=1)


def attention_backward(scale_ref, project_ref, starts_ref, grad_ref, out_ref, scale_grad_ref):
    allowed = allowed_pairs(starts_ref)
    span = grad_ref.shape[1]
    score_scale = 1.0 / math.sqrt(HD)
    for pair in range(span // (2 * HD)):
        parts = ([], [], [])
        sums = []
        for head in (2 * pair, 2 * pair + 1):
            queries, key_rows, value_rows = head_parts(project_ref, head)
            upstream = grad_ref[:, head * HD : head * HD + HD]
            weights = head_weights(queries, key_rows, allowed)
            weights_low = weights.astype(jnp.bfloat16)
            attended = contract(weights_low, value_rows, 1, 0)
            wide = upstream.astype(jnp.float32)
            sums.append(jnp.sum(wide * attended, axis=0, keepdims=True))
            grad_attended = (wide * scale_ref[head]).astype(jnp.bfloat16)
            grad_weights = contract(grad_attended, value_rows, 1, 1)
            inner = jnp.sum(weights * grad_weights, axis=-1, keepdims=True)
            grad_scores = (weights * (grad_weights - inner)).astype(jnp.bfloat16)
            parts[0].append(contract(grad_scores, key_rows, 1, 0) * score_scale)
            parts[1].append(contract(grad_scores, queries, 0, 0) * score_scale)
            parts[2].append(contract(weights_low, grad_attended, 0, 0))
        at = 2 * HD * pair
        for which in range(3):
            both = jnp.concatenate(parts[which], axis=1).astype(jnp.bfloat16)
            out_ref[:, which * span + at : which * span + at + 2 * HD] = both
        scale_grad_ref[pair : pair + 1, :] = jnp.concatenate(sums, axis=1)


def pack_columns(place_ref, qkv_ref, up_ref, own_ref, there_ref):
    core, near = place_ref[0], place_ref[1]
    layers, shard, width = qkv_ref.shape
    span = width // 2
    blocks = up_ref.shape[2] // 512
    for layer in range(layers):
        for at in range(0, width, 256):
            parts = [qkv_ref[layer, :, at + HD * i : at + HD * (i + 1)] for i in range(4)]
            even = jnp.concatenate([parts[0], parts[2]], axis=1)
            odd = jnp.concatenate([parts[1], parts[3]], axis=1)

            @pl.when(core == 0)
            def _():
                own_ref[layer, :, at // 2 : at // 2 + 128] = even
                there_ref[layer, :, at // 2 : at // 2 + 128] = odd

            @pl.when(core == 1)
            def _():
                own_ref[layer, :, at // 2 : at // 2 + 128] = odd
                there_ref[layer, :, at // 2 : at // 2 + 128] = even

        for out_ref, which in ((own_ref, core), (there_ref, 1 - core)):
            for part, side in enumerate((near, 1 - near)):
                for block in range(blocks):
                    at = span + (part * blocks + block) * 128
                    source = pl.multiple_of(block * 512 + which * 256 + side * 128, 128)
                    out_ref[layer, :, at : at + 128] = up_ref[layer, :, pl.ds(source, 128)]


def pack_rows(place_ref, own_ref, there_ref, out_ref, down_ref, *units):
    core, near = place_ref[0], place_ref[1]
    layers, shard, width = out_ref.shape
    half = width // 2
    span = own_ref.shape[2] - 2 * width
    first, up, down, second = units
    attention, ups = (first, second.at[:, : 2 * width]), (up, second.at[:, 2 * width : 4 * width])
    downs = (down, second.at[:, 4 * width :])
    for layer in range(layers):
        for source_ref, which in ((own_ref, core), (there_ref, 1 - core)):
            rows = pl.ds(pl.multiple_of(which * shard, shard), shard)
            attention[layer][rows, :span] = source_ref[layer, :, :span]
            columns = ups[layer].shape[1]
            ups[layer][rows, :] = source_ref[layer, :, span : span + columns]
        attention[layer][:shard, span:] = out_ref[layer, :, :half]
        attention[layer][shard:, span:] = out_ref[layer, :, half:]
        for part in range(downs[layer].shape[1] // width):
            side = near if part == 0 else 1 - near
            rows = pl.ds(pl.multiple_of(side * 2 * shard, 2 * shard), 2 * shard)
            downs[layer][:, part * width : part * width + width] = down_ref[layer, rows, :]


def term_product(lefts, lefts_there, rights, parts, shape):
    count = len(lefts)

    def body(*refs):
        right_ref, right_there_ref, out_ref = refs[2 * count :]
        for which, left_at, right_at, columns, out_at in parts:
            right = right_ref[:, right_at : right_at + columns]
            right_there = right_there_ref[:, right_at : right_at + columns]
            for row in range(0, shape[0], 256):
                left = refs[which][:, left_at + row : left_at + row + 256]
                left_there = refs[count + which][:, left_at + row : left_at + row + 256]
                total = contract(left, right, 0, 0) + contract(left_there, right_there, 0, 0)
                out_ref[row : row + 256, out_at : out_at + columns] = total.astype(jnp.bfloat16)

    vmem = pl.BlockSpec(memory_space=pltpu.VMEM)
    return pl.pallas_call(
        body,
        out_shape=jax.ShapeDtypeStruct(shape, jnp.bfloat16),
        in_specs=[vmem] * (2 * count + 2),
        out_specs=vmem,
    )(*lefts, *lefts_there, *rights)


def run_small(body, scale, arrays, outs):
    vmem = pl.BlockSpec(memory_space=pltpu.VMEM)
    return pl.pallas_call(
        body,
        out_shape=[jax.ShapeDtypeStruct(*out) for out in outs],
        in_specs=[pl.BlockSpec(memory_space=pltpu.SMEM)] + [vmem] * len(arrays),
        out_specs=[vmem] * len(outs),
    )(scale, *arrays)


SWAP = ((0, 1), (1, 0))


def swap(array, axis):
    return lax.ppermute(array, axis, SWAP)


def turn(array):
    return lax.ppermute(array, ("c", "y"), ((0, 0), (1, 2), (2, 1), (3, 3)))


def norm_parts(values):
    center = values - jnp.mean(values, axis=-1, keepdims=True)
    inverse = lax.rsqrt(jnp.mean(center * center, axis=-1, keepdims=True) + norm_eps)
    return center * inverse, inverse


def local_chip(
    tokens,
    seq_start,
    qkv_weight,
    out_weight,
    fc1_weight,
    fc2_weight,
    norm_gain,
    norm_bias,
    mid_gain,
    mid_bias,
    head_scale,
    cotangent,
):
    nz, nx = lax.axis_size("z"), lax.axis_size("x")
    iz, ix, ic, iy = (lax.axis_index(name) for name in ("z", "x", "c", "y"))
    chips = nz * nx
    rows, width = tokens.shape
    group_rows = seq_start.shape[0]
    hidden_width = fc1_weight.shape[2]
    shard = qkv_weight.shape[1]
    block = hidden_width // (4 * chips)
    heads_here = H // 2
    head_width = width // 2
    units = hidden_width // 2
    half_units = units // 2
    half = width // 2
    wide = 3 * head_width // 2
    f32, bf16 = jnp.float32, jnp.bfloat16

    def pick(array, which, axis):
        return lax.dynamic_index_in_dim(array, which, axis, keepdims=False)

    def cores(own, other, axis=0):
        first = jnp.where(ic == 0, own, other)
        second = jnp.where(ic == 0, other, own)
        return jnp.concatenate([first, second], axis=axis)

    def both_cores(partial_sum):
        low = lax.optimization_barrier(partial_sum.astype(bf16))
        return low.astype(f32) + swap(low, "c").astype(f32)

    def ordered(first, second, axis):
        near = jnp.where(iy == 0, first, second)
        far = jnp.where(iy == 0, second, first)
        return jnp.concatenate([near, far], axis=axis)

    def gather(array):
        return lax.all_gather(array, ("z", "x"), axis=0, tiled=True)

    def scatter(array):
        return lax.psum_scatter(
            array.astype(bf16), ("z", "x"), scatter_dimension=0, tiled=True
        ).astype(f32)

    def step_x(array):
        split = array.reshape(nz, nx, -1, array.shape[1])
        there = swap(pick(split, 1 - ix, 1).astype(bf16), "x")
        return pick(split, ix, 1).astype(f32) + there.astype(f32)

    def step_z(array):
        total = pick(array, iz, 0)
        for step in range(1, nz):
            there = pick(array, (iz + step) % nz, 0).astype(bf16)
            ring = [(i, (i + step) % nz) for i in range(nz)]
            total = total + lax.ppermute(there, "z", ring).astype(f32)
        return total

    def steps(array):
        return step_z(step_x(array))

    def tie(value, *others):
        return lax.optimization_barrier((value,) + others)

    def z_pieces(array):
        return [array] + [
            lax.ppermute(array, "z", [(i, (i + step) % nz) for i in range(nz)])
            for step in range(1, nz)
        ]

    def join(pieces):
        held = jnp.zeros((nz, nx) + pieces[0].shape, pieces[0].dtype)
        for step, piece in enumerate(pieces):
            for at_x, part in ((ix, piece), (1 - ix, swap(piece, "x"))):
                at = ((iz - step) % nz, at_x, 0, 0)
                held = lax.dynamic_update_slice(held, part[None, None], at)
        return held.reshape(-1, pieces[0].shape[1])

    place = jnp.stack([ic, iy]).astype(jnp.int32)
    narrow = (LAYERS, shard, 3 * head_width + units)
    own, there = run_small(
        pack_columns, place, (qkv_weight, fc1_weight), [(narrow, bf16), (narrow, bf16)]
    )
    packed = run_small(
        pack_rows,
        place,
        (own, swap(there, "c"), out_weight, fc2_weight),
        [((2 * shard, columns), bf16) for columns in (2 * width, width, width, 6 * width)],
    )
    got = []
    for unit in (packed[1], packed[2], packed[0]):
        if got:
            unit, got[-1][1] = tie(unit, got[-1][1])
        got.append(z_pieces(unit))
    got = [join(pieces) for pieces in got]
    late, got[0] = tie(packed[3], got[0])
    late = gather(late)
    up_there, down_there = swap(got[0], "y"), swap(got[1], "y")
    late_parts = [late[:, width * part : width * (part + 1)] for part in range(2, 6)]
    ups = [(got[0], up_there), late_parts[:2]]
    downs = [(got[1], down_there), late_parts[2:]]
    attention_mats = [got[2], late]

    def matrices(which):
        packed = attention_mats[which]
        qkv = packed[:, : 3 * head_width]
        out = packed[:, 3 * head_width : 4 * head_width].reshape(chips, 2, shard, half)
        out = jnp.concatenate(
            [out[:, 0].reshape(head_width, half), out[:, 1].reshape(head_width, half)], axis=1
        )
        return qkv, out, ups[which], downs[which]

    def mine_of(vector):
        mine = pick(vector.reshape(chips, 2, 2, block), ic, 1)
        return ordered(mine[:, 0].reshape(-1), mine[:, 1].reshape(-1), 0)

    def slice_of(values, first, size):
        return lax.dynamic_slice_in_dim(values, first, size, 1)

    turned = turn(tokens)
    hidden = cores(turned, swap(turned, "c")).astype(f32)
    starts = jnp.where(ic == iy, seq_start, swap(seq_start, "c"))
    starts = starts[:, None]

    mats = [matrices(which) for which in range(LAYERS)]
    kept = []
    for which in range(LAYERS):
        qkv_mat, out_mat, up_mat, down_mat = mats[which]
        scale_here = pick(head_scale[which].reshape(heads_here, 2), ic, 1)
        norm_a, inv_a = norm_parts(hidden)
        a_low = (norm_a * norm_gain[which, 0] + norm_bias[which, 0]).astype(bf16)
        project = product(a_low, qkv_mat).astype(bf16)
        (scaled,) = run_small(
            attention_forward, scale_here, (project, starts), [((group_rows, head_width), bf16)]
        )
        branch = both_cores(product(scaled, out_mat))
        if which == 1:
            branch, *there = tie(branch, *kept[0][-1][:2])
            kept[0] = kept[0][:-1] + ((*there, kept[0][-1][2]),)
        else:
            branch, far_up, far_down = tie(branch, up_mat[1], down_mat[1])
            up_mat, down_mat = (up_mat[0], far_up), (down_mat[0], far_down)
            mats[0] = (qkv_mat, out_mat, up_mat, down_mat)
        norm_z, inv_z = norm_parts(branch)
        middle = hidden + norm_z * norm_gain[which, 1] + norm_bias[which, 1]
        norm_b, inv_b = norm_parts(middle)
        b_low = (norm_b * norm_gain[which, 2] + norm_bias[which, 2]).astype(bf16)
        pre_act = jnp.concatenate([product(b_low, part) for part in up_mat], axis=1)
        below = 0.5 * (1.0 + lax.erf(pre_act * (1.0 / math.sqrt(2.0))))
        activated = pre_act * below
        mean_here = jnp.mean(activated, axis=-1)
        center = activated - mean_here[:, None]
        stats = jnp.stack([mean_here, jnp.mean(center * center, axis=-1)])
        stats_there = swap(stats, "c")
        mean_all = 0.5 * (stats[0] + stats_there[0])
        apart = 0.5 * (stats[0] - stats_there[0])
        spread = 0.5 * (stats[1] + stats_there[1]) + apart * apart
        inv_m = lax.rsqrt(spread + norm_eps)[:, None]
        norm_m = (activated - mean_all[:, None]) * inv_m
        gain_m, bias_m = mine_of(mid_gain[which]), mine_of(mid_bias[which])
        mixed_low = (norm_m * gain_m + bias_m).astype(bf16)
        near, far = mixed_low[:, :half_units], mixed_low[:, half_units:]
        hidden = middle + both_cores(product(near, down_mat[0]) + product(far, down_mat[1]))
        attention_in = jnp.concatenate([a_low, scaled], axis=1)
        mixed_there = swap(jnp.concatenate([far, near], axis=1), "y")
        ins_there = (swap(attention_in, "y"), swap(b_low, "y"), mixed_there)
        kept.append(
            (
                norm_a, inv_a, project, scale_here, norm_z, inv_z, norm_b, inv_b, pre_act, below, norm_m, inv_m, gain_m,
                attention_in, b_low, mixed_low, ins_there,
            )
        )
    output = lax.dynamic_slice_in_dim(hidden.astype(bf16), ic * rows, rows, 0)
    turned = turn(cotangent)
    grad_hidden = cores(turned, swap(turned, "c")).astype(f32)

    def natural(values):
        return ordered(values[:half_units], values[half_units:], 0)

    vectors, pending = [None] * LAYERS, [None] * LAYERS
    for which in reversed(range(LAYERS)):
        qkv_mat, out_mat, up_mat, down_mat = mats[which]
        (
            norm_a, inv_a, project, scale_here, norm_z, inv_z, norm_b, inv_b, pre_act, below, norm_m, inv_m, gain_m,
            attention_in, b_low, mixed_low, ins_there,
        ) = kept[which]
        final_low = grad_hidden.astype(bf16)
        grad_mixed = jnp.concatenate([product(final_low, part.T) for part in down_mat], axis=1)
        mid_gain_grad = jnp.sum(grad_mixed * norm_m, axis=0)
        mid_bias_grad = jnp.sum(grad_mixed, axis=0)
        scaled_grad = grad_mixed * gain_m
        sums = jnp.stack([jnp.sum(scaled_grad, axis=-1), jnp.sum(scaled_grad * norm_m, axis=-1)])
        sums = (sums + swap(sums, "c")) / hidden_width
        grad_act = inv_m * (scaled_grad - sums[0][:, None] - norm_m * sums[1][:, None])
        slope = below + pre_act * jnp.exp(-0.5 * pre_act * pre_act) * (1.0 / math.sqrt(2 * math.pi))
        grad_pre = (grad_act * slope).astype(bf16)
        attention_there, b_there, mixed_there = ins_there
        if which == 1:
            grad_pre, attention_there, b_there = tie(grad_pre, attention_there, b_there)
        else:
            grad_pre, at_there = tie(grad_pre, at_there)
            later = finish_attention(at_there)
        near, far = grad_pre[:, :half_units], grad_pre[:, half_units:]

        def unit_columns(side):
            first = side * (half_units // 2)
            return (
                slice_of(near, first, half_units // 2),
                slice_of(far, first, half_units // 2),
                slice_of(final_low, side * half, half),
            )

        keep_n, keep_f, keep_c = unit_columns(iy)
        send_n, send_f, send_c = unit_columns(1 - iy)
        ff_there = swap(jnp.concatenate([send_f, send_n, send_c], axis=1), "y")
        ff_out = jnp.concatenate([keep_n, keep_f, keep_c], axis=1)
        grad_ff_in = both_cores(product(near, up_mat[0].T) + product(far, up_mat[1].T))
        grad_mid_in, gain_two, bias_two = norm_backward(
            grad_ff_in, norm_b, inv_b, norm_gain[which, 2]
        )
        grad_middle = grad_hidden + grad_mid_in
        grad_branch, gain_one, bias_one = norm_backward(
            grad_middle, norm_z, inv_z, norm_gain[which, 1]
        )
        branch_low = grad_branch.astype(bf16)
        if which == 0:
            branch_low, later = tie(branch_low, later)
            later = step_x(later)
        grad_heads = product(branch_low, out_mat.T).astype(bf16)
        grad_project, scale_grad = run_small(
            attention_backward,
            scale_here,
            (project, starts, grad_heads),
            [((group_rows, 3 * head_width), bf16), ((heads_here // 2, 2 * HD), f32)],
        )
        scale_grad = jnp.sum(scale_grad.reshape(heads_here, HD), axis=1)
        grad_project, ff_there, mixed_there = tie(grad_project, ff_there, mixed_there)
        ff_term = term_product(
            (b_low, mixed_low),
            (b_there, mixed_there),
            (ff_out, ff_there),
            ((0, 0, 0, width, 0), (1, 0, width, half, width), (1, width, width, half, width + half)),
            (width, 2 * width),
        )
        if which == 1:
            grad_project, ff_term = tie(grad_project, ff_term)
            ff_rows = scatter(ff_term)
        grad_normed = both_cores(product(grad_project, qkv_mat.T))
        grad_input, gain_zero, bias_zero = norm_backward(
            grad_normed, norm_a, inv_a, norm_gain[which, 0]
        )

        at_out = jnp.concatenate(
            [slice_of(grad_project, iy * wide, wide), slice_of(branch_low, iy * half, half)], axis=1
        )
        at_there = jnp.concatenate(
            [
                slice_of(grad_project, (1 - iy) * wide, wide),
                slice_of(branch_low, (1 - iy) * half, half),
            ],
            axis=1,
        )
        at_there = swap(at_there, "y")
        grad_hidden = grad_middle + grad_input

        def attention_term(there, here=at_out, ins=attention_in, ins_there=attention_there):
            split = half // 2
            rights = (here, there)
            out_term = term_product(
                (ins,), (ins_there,), rights, ((0, width, wide, half, 0),), (head_width, half)
            ).reshape(chips, shard, half)
            out_term = jnp.concatenate([out_term[..., :split], out_term[..., split:]], axis=1)
            qkv_term = term_product(
                (ins,), (ins_there,), rights, ((0, 0, 0, wide, 0),), (width, wide)
            )
            return jnp.concatenate([qkv_term, out_term.reshape(-1, split)], axis=1)

        if which == 1:
            finish_attention = attention_term
        else:
            grad_hidden, later = tie(grad_hidden, later)
            at_rows_last = step_z(later)
        if which == 1:
            pending[1] = ff_rows
        shared = jnp.concatenate([gain_zero, gain_one, gain_two, bias_zero, bias_one, bias_two])
        vectors[which] = jnp.concatenate(
            [0.5 * shared, natural(mid_gain_grad), natural(mid_bias_grad), jnp.pad(scale_grad, (0, 128 - heads_here))]
        )

    vector = jnp.stack(vectors)
    vector = vector + swap(vector, "y")
    vector = vector + swap(vector, "x")
    vector, ff_term = tie(vector, ff_term)
    up_held, down_held = step_x(ff_term[:, :width]), step_x(ff_term[:, width:])
    for bit in (1, 2):
        vector = vector + lax.ppermute(vector, "z", [(i, i ^ bit) for i in range(nz)])
    at_held = step_x(attention_term(at_there))
    at_held, output, grad_hidden = tie(at_held, output, grad_hidden)
    pending[0] = jnp.concatenate([step_z(up_held), step_z(down_held)], axis=1)
    at_rows = step_z(at_held)
    matrix_grads = []
    for at_rows, ff_rows in ((at_rows, pending[0]), (at_rows_last, pending[1])):
        grad_out = at_rows[:, wide:].reshape(2, shard, half // 2)
        grad_out = jnp.concatenate([grad_out[0], grad_out[1]], axis=1)
        down_near, down_far = ff_rows[:, width : width + half], ff_rows[:, width + half :]
        grad_down = jnp.concatenate(
            [jnp.where(iy == 0, down_near, down_far), jnp.where(iy == 0, down_far, down_near)], axis=0
        )
        mixed_rows = jnp.concatenate([at_rows[:, :wide], ff_rows[:, :width]], axis=1)
        mixed_rows = mixed_rows.reshape(2, shard, -1)
        own = pick(mixed_rows, ic, 0)
        other = swap(pick(mixed_rows, 1 - ic, 0).astype(bf16), "c").astype(f32)
        columns = cores(own[None], other[None])
        grad_qkv = columns[:, :, :wide].reshape(2, shard, wide // HD, HD)
        grad_qkv = grad_qkv.transpose(1, 2, 0, 3).reshape(shard, 2 * wide)
        near, far = columns[:, :, wide : wide + half], columns[:, :, wide + half :]
        grad_up = jnp.stack(
            [jnp.where(iy == 0, near, far), jnp.where(iy == 0, far, near)], axis=2
        ).reshape(2, shard, 2, chips // 2, block)
        grad_up = grad_up.transpose(1, 3, 0, 2, 4).reshape(shard, 2 * width)
        matrix_grads.append((grad_qkv, grad_out, grad_up, grad_down))

    grad_tokens = turn(lax.dynamic_slice_in_dim(grad_hidden, ic * rows, rows, 0))
    output = turn(output)
    there = swap(vector, "c")
    shared = vector[:, : 6 * width] + there[:, : 6 * width]

    def spread_units(first):
        view = (LAYERS, 2, chips, 1, block)
        own, other = (part[:, first : first + units] for part in (vector, there))
        own, other = own.reshape(view), other.reshape(view)
        return cores(own, other, 3).transpose(0, 2, 3, 1, 4).reshape(LAYERS, hidden_width)

    scale_at = 6 * width + 2 * units
    own, other = (
        part[:, scale_at : scale_at + heads_here].reshape(LAYERS, heads_here, 1)
        for part in (vector, there)
    )
    summed = [jnp.stack([grads[which] for grads in matrix_grads]) for which in range(4)]
    return (
        output,
        grad_tokens,
        summed[0],
        summed[1],
        summed[2],
        summed[3],
        shared[:, : 3 * width].reshape(LAYERS, 3, width),
        shared[:, 3 * width :].reshape(LAYERS, 3, width),
        spread_units(6 * width),
        spread_units(6 * width + units),
        cores(own, other, 2).reshape(LAYERS, H),
    )


def solution(mesh):
    dp, sp = mesh.shape["dp"], mesh.shape["sp"]
    if sp == 2 and dp == 16:
        mesh = Mesh(mesh.devices.reshape(4, dp // 8, 2, 2), ("z", "x", "c", "y"))
        rows, every, cols, body = ("z", "x", "c"), ("z", "x", "c", "y"), "y", local_chip
    else:
        rows, every, cols, body = "dp", ("dp", "sp"), "sp", local_any
    weight = P(None, rows, None)
    in_specs = (P(every, None), P(rows), weight, weight, weight, weight)
    in_specs = in_specs + (P(),) * 5 + (P(every, None),)
    grad = P(None, rows, cols)
    out_specs = (P(every, None), P(every, None), grad, grad, grad, grad) + (P(),) * 5
    return jax.shard_map(body, mesh=mesh, in_specs=in_specs, out_specs=out_specs, check_vma=False)
```

```python
from functools import partial
import math

import jax
import jax.numpy as jnp
from jax import lax
from jax.experimental import pallas as pl
from jax.experimental.pallas import tpu as pltpu
from jax.sharding import Mesh, PartitionSpec as P

H = 16
HD = 64
LAYERS = 2


norm_eps = 1e-05


def for_sending(array):

    def short(part):
        return part.astype(jnp.bfloat16) if part.dtype == jnp.float32 else part

    return jax.tree.map(short, array)


def norm_forward(values, gain, bias):
    center = values - jnp.mean(values, axis=-1, keepdims=True)
    inverse = lax.rsqrt(jnp.mean(center * center, axis=-1, keepdims=True) + norm_eps)
    normal = center * inverse
    return (normal * gain + bias, normal, inverse)


def norm_backward(upstream, normal, inverse, gain):
    scaled = upstream * gain
    grad_values = inverse * (
        scaled
        - jnp.mean(scaled, axis=-1, keepdims=True)
        - normal * jnp.mean(scaled * normal, axis=-1, keepdims=True)
    )
    return (grad_values, jnp.sum(upstream * normal, axis=0), jnp.sum(upstream, axis=0))


def product(left, right):
    return jnp.dot(left, right, preferred_element_type=jnp.float32)


def block_layout(length):
    block_count = min(4, max(1, length // 512))
    return (block_count, length // block_count)


def score_block(query_block, query_pos, query_start, key_rows, score_scale):
    key_pos = jnp.arange(key_rows.shape[0], dtype=jnp.int32)
    scores = (
        jnp.einsum("qhd,khd->hqk", query_block, key_rows, preferred_element_type=jnp.float32)
        * score_scale
    )
    allowed = (key_pos[None, :] >= query_start[:, None]) & (key_pos[None, :] <= query_pos[:, None])
    return jnp.where(allowed[None], scores, -1e30)


def attend_forward(queries, key_rows, value_rows, starts, score_scale):
    length = queries.shape[0]
    block_count, block_rows = block_layout(length)
    positions = jnp.arange(length, dtype=jnp.int32)
    results, maxima, totals = ([], [], [])
    for block_index in range(block_count):
        row_first = block_index * block_rows
        row_end = row_first + block_rows
        scores = score_block(
            queries[row_first:row_end],
            positions[row_first:row_end],
            starts[row_first:row_end],
            key_rows[:row_end],
            score_scale,
        )
        row_max = jnp.max(scores, axis=-1, keepdims=True)
        exponent = jnp.exp(scores - row_max)
        row_total = jnp.sum(exponent, axis=-1, keepdims=True)
        weights_low = (exponent / row_total).astype(jnp.bfloat16)
        results.append(
            jnp.einsum(
                "hqk,khd->qhd",
                weights_low,
                value_rows[:row_end],
                preferred_element_type=jnp.float32,
            )
        )
        maxima.append(row_max)
        totals.append(row_total)
    return (jnp.concatenate(results, axis=0), maxima, totals)


def attend_backward(queries, key_rows, value_rows, starts, score_scale, grad_out, maxima, totals):
    length, heads_here, head_dim = queries.shape
    block_count, block_rows = block_layout(length)
    positions = jnp.arange(length, dtype=jnp.int32)
    grad_keys = jnp.zeros((length, heads_here, head_dim), jnp.float32)
    grad_values = jnp.zeros((length, heads_here, head_dim), jnp.float32)
    query_grads = []
    for block_index in range(block_count):
        row_first = block_index * block_rows
        row_end = row_first + block_rows
        query_block = queries[row_first:row_end]
        grad_block = grad_out[row_first:row_end]
        scores = score_block(
            query_block,
            positions[row_first:row_end],
            starts[row_first:row_end],
            key_rows[:row_end],
            score_scale,
        )
        weights_full = jnp.exp(scores - maxima[block_index]) / totals[block_index]
        weights_low = weights_full.astype(jnp.bfloat16)
        grad_weights = jnp.einsum(
            "qhd,khd->hqk", grad_block, value_rows[:row_end], preferred_element_type=jnp.float32
        )
        inner = jnp.sum(weights_full * grad_weights, axis=-1, keepdims=True)
        grad_scores = (weights_full * (grad_weights - inner)).astype(jnp.bfloat16)
        query_grads.append(
            jnp.einsum(
                "hqk,khd->qhd", grad_scores, key_rows[:row_end], preferred_element_type=jnp.float32
            )
            * score_scale
        )
        grad_keys = grad_keys.at[:row_end].add(
            jnp.einsum("hqk,qhd->khd", grad_scores, query_block, preferred_element_type=jnp.float32)
            * score_scale
        )
        grad_values = grad_values.at[:row_end].add(
            jnp.einsum("hqk,qhd->khd", weights_low, grad_block, preferred_element_type=jnp.float32)
        )
    return (jnp.concatenate(query_grads, axis=0), grad_keys, grad_values)


def local_any(
    tokens,
    seq_start,
    qkv_weight,
    out_weight,
    fc1_weight,
    fc2_weight,
    norm_gain,
    norm_bias,
    mid_gain,
    mid_bias,
    head_scale,
    cotangent,
):
    split_count = lax.axis_size("sp")
    split_rank = lax.axis_index("sp")
    local_rows, width_model = tokens.shape
    group_rows = seq_start.shape[0]
    heads_here = H // split_count
    head_width = heads_here * HD
    score_scale = 1.0 / math.sqrt(HD)
    scale_here = lax.dynamic_slice_in_dim(head_scale, split_rank * heads_here, heads_here, axis=1)
    hidden = tokens.astype(jnp.float32)
    kept_layers = []
    kept_matrices = []
    for which_layer in range(LAYERS):
        matrices = (
            lax.all_gather(qkv_weight[which_layer], "dp", axis=0, tiled=True),
            lax.all_gather(out_weight[which_layer], "dp", axis=0, tiled=True),
            lax.all_gather(fc1_weight[which_layer], "dp", axis=0, tiled=True),
            lax.all_gather(fc2_weight[which_layer], "dp", axis=0, tiled=True),
        )
        qkv_full, out_full, up_full, down_full = matrices
        normed, norm_a, inv_a = norm_forward(
            hidden, norm_gain[which_layer, 0], norm_bias[which_layer, 0]
        )
        normed_low = normed.astype(jnp.bfloat16)
        project = (
            product(normed_low, qkv_full)
            .astype(jnp.bfloat16)
            .reshape(local_rows, 3, split_count, head_width)
        )
        by_heads = lax.all_to_all(project, "sp", split_axis=2, concat_axis=0, tiled=True)
        queries = by_heads[:, 0, 0].reshape(group_rows, heads_here, HD)
        key_rows = by_heads[:, 1, 0].reshape(group_rows, heads_here, HD)
        value_rows = by_heads[:, 2, 0].reshape(group_rows, heads_here, HD)
        attended, maxima, totals = attend_forward(
            queries, key_rows, value_rows, seq_start, score_scale
        )
        scaled = (
            (attended * scale_here[which_layer][None, :, None])
            .astype(jnp.bfloat16)
            .reshape(group_rows, 1, head_width)
        )
        gathered = lax.all_to_all(scaled, "sp", split_axis=0, concat_axis=1, tiled=True).reshape(
            local_rows, width_model
        )
        branch = product(gathered, out_full)
        branch_norm, norm_z, inv_z = norm_forward(
            branch, norm_gain[which_layer, 1], norm_bias[which_layer, 1]
        )
        middle = hidden + branch_norm
        normed_ff, norm_b, inv_b = norm_forward(
            middle, norm_gain[which_layer, 2], norm_bias[which_layer, 2]
        )
        ff_low = normed_ff.astype(jnp.bfloat16)
        pre_act = product(ff_low, up_full)
        activated = jax.nn.gelu(pre_act, approximate=False)
        mixed, norm_m, inv_m = norm_forward(activated, mid_gain[which_layer], mid_bias[which_layer])
        mixed_low = mixed.astype(jnp.bfloat16)
        hidden = middle + product(mixed_low, down_full)
        kept_layers.append(
            (
                norm_a,
                inv_a,
                normed_low,
                queries,
                key_rows,
                value_rows,
                attended,
                maxima,
                totals,
                gathered,
                norm_z,
                inv_z,
                norm_b,
                inv_b,
                ff_low,
                pre_act,
                norm_m,
                inv_m,
                mixed_low,
            )
        )
        kept_matrices.append(matrices)
    output = hidden.astype(jnp.bfloat16)
    grad_hidden = cotangent.astype(jnp.float32)
    matrix_grads = [None] * LAYERS
    gain_grads = [None] * LAYERS
    bias_grads = [None] * LAYERS
    mid_gain_grads = [None] * LAYERS
    mid_bias_grads = [None] * LAYERS
    scale_grads = [None] * LAYERS
    for which_layer in reversed(range(LAYERS)):
        (
            norm_a,
            inv_a,
            normed_low,
            queries,
            key_rows,
            value_rows,
            attended,
            maxima,
            totals,
            gathered,
            norm_z,
            inv_z,
            norm_b,
            inv_b,
            ff_low,
            pre_act,
            norm_m,
            inv_m,
            mixed_low,
        ) = kept_layers[which_layer]
        qkv_full, out_full, up_full, down_full = (
            lax.all_gather(qkv_weight[which_layer], "dp", axis=0, tiled=True),
            lax.all_gather(out_weight[which_layer], "dp", axis=0, tiled=True),
            lax.all_gather(fc1_weight[which_layer], "dp", axis=0, tiled=True),
            lax.all_gather(fc2_weight[which_layer], "dp", axis=0, tiled=True),
        )
        grad_final = grad_hidden.astype(jnp.bfloat16)
        grad_mixed = product(grad_final, down_full.T)
        grad_act, mid_gain_grad, mid_bias_grad = norm_backward(
            grad_mixed, norm_m, inv_m, mid_gain[which_layer]
        )
        gelu_value, gelu_pull = jax.vjp(partial(jax.nn.gelu, approximate=False), pre_act)
        grad_pre = gelu_pull(grad_act)[0].astype(jnp.bfloat16)
        grad_ff_in = product(grad_pre, up_full.T)
        grad_mid_in, gain_two, bias_two = norm_backward(
            grad_ff_in, norm_b, inv_b, norm_gain[which_layer, 2]
        )
        grad_middle = grad_hidden + grad_mid_in
        grad_branch_full, gain_one, bias_one = norm_backward(
            grad_middle, norm_z, inv_z, norm_gain[which_layer, 1]
        )
        grad_branch = grad_branch_full.astype(jnp.bfloat16)
        grad_gathered = (
            product(grad_branch, out_full.T)
            .astype(jnp.bfloat16)
            .reshape(local_rows, split_count, head_width)
        )
        grad_heads = lax.all_to_all(
            grad_gathered, "sp", split_axis=1, concat_axis=0, tiled=True
        ).reshape(group_rows, heads_here, HD)
        scale_grad_here = jnp.sum(grad_heads.astype(jnp.float32) * attended, axis=(0, 2))
        grad_attended = (grad_heads * scale_here[which_layer][None, :, None]).astype(jnp.bfloat16)
        grad_queries, grad_keys, grad_values = attend_backward(
            queries, key_rows, value_rows, seq_start, score_scale, grad_attended, maxima, totals
        )
        stacked = jnp.stack(
            [
                grad_queries.reshape(group_rows, head_width),
                grad_keys.reshape(group_rows, head_width),
                grad_values.reshape(group_rows, head_width),
            ],
            axis=1,
        )
        stacked = stacked.astype(jnp.bfloat16).reshape(group_rows, 3, 1, head_width)
        back_rows = lax.all_to_all(stacked, "sp", split_axis=0, concat_axis=2, tiled=True).reshape(
            local_rows, 3 * width_model
        )
        grad_normed = product(back_rows, qkv_full.T)
        grad_input, gain_zero, bias_zero = norm_backward(
            grad_normed, norm_a, inv_a, norm_gain[which_layer, 0]
        )
        grad_hidden = grad_middle + grad_input
        group_inputs = (
            lax.all_gather(normed_low, "sp", axis=0, tiled=True),
            lax.all_gather(gathered, "sp", axis=0, tiled=True),
            lax.all_gather(ff_low, "sp", axis=0, tiled=True),
            lax.all_gather(mixed_low, "sp", axis=0, tiled=True),
        )
        group_columns = (
            lax.all_to_all(
                back_rows.reshape(local_rows, split_count, -1),
                "sp",
                split_axis=1,
                concat_axis=0,
                tiled=True,
            ),
            lax.all_to_all(
                grad_branch.reshape(local_rows, split_count, -1),
                "sp",
                split_axis=1,
                concat_axis=0,
                tiled=True,
            ),
            lax.all_to_all(
                grad_pre.reshape(local_rows, split_count, -1),
                "sp",
                split_axis=1,
                concat_axis=0,
                tiled=True,
            ),
            lax.all_to_all(
                grad_final.reshape(local_rows, split_count, -1),
                "sp",
                split_axis=1,
                concat_axis=0,
                tiled=True,
            ),
        )
        terms = tuple(
            (
                product(group_inputs[which].T, group_columns[which].reshape(group_rows, -1))
                for which in range(4)
            )
        )
        matrix_grads[which_layer] = jax.tree.map(
            lambda part: part.astype(jnp.float32),
            lax.psum_scatter(for_sending(terms), "dp", scatter_dimension=0, tiled=True),
        )
        gain_grads[which_layer] = jnp.stack([gain_zero, gain_one, gain_two])
        bias_grads[which_layer] = jnp.stack([bias_zero, bias_one, bias_two])
        mid_gain_grads[which_layer] = mid_gain_grad
        mid_bias_grads[which_layer] = mid_bias_grad
        scale_grads[which_layer] = lax.dynamic_update_slice(
            jnp.zeros((H,), jnp.float32), scale_grad_here, (split_rank * heads_here,)
        )
    summed = tuple((jnp.stack([pieces[which] for pieces in matrix_grads]) for which in range(4)))
    small_sums = lax.psum(
        (
            jnp.stack(gain_grads),
            jnp.stack(bias_grads),
            jnp.stack(mid_gain_grads),
            jnp.stack(mid_bias_grads),
            jnp.stack(scale_grads),
        ),
        ("dp", "sp"),
    )
    return (
        output,
        grad_hidden,
        summed[0],
        summed[1],
        summed[2],
        summed[3],
        small_sums[0],
        small_sums[1],
        small_sums[2],
        small_sums[3],
        small_sums[4],
    )


def contract(left, right, left_axis, right_axis):
    return lax.dot_general(
        left, right, (((left_axis,), (right_axis,)), ((), ())), preferred_element_type=jnp.float32
    )


def head_parts(project_ref, head):
    span = project_ref.shape[1] // 3
    at = head * HD
    return (project_ref[:, base + at : base + at + HD] for base in (0, span, 2 * span))


def head_weights(queries, key_rows, allowed):
    scores = contract(queries, key_rows, 1, 1) * (1.0 / math.sqrt(HD))
    scores = jnp.where(allowed, scores, -1e30)
    exponent = jnp.exp(scores - jnp.max(scores, axis=-1, keepdims=True))
    return exponent / jnp.sum(exponent, axis=-1, keepdims=True)


def allowed_pairs(starts_ref):
    length = starts_ref.shape[0]
    row = lax.broadcasted_iota(jnp.int32, (length, length), 0)
    col = lax.broadcasted_iota(jnp.int32, (length, length), 1)
    return (col >= starts_ref[...]) & (col <= row)


def attention_forward(scale_ref, project_ref, starts_ref, scaled_ref):
    allowed = allowed_pairs(starts_ref)
    for pair in range(scaled_ref.shape[1] // (2 * HD)):
        parts = []
        for head in (2 * pair, 2 * pair + 1):
            queries, key_rows, value_rows = head_parts(project_ref, head)
            weights = head_weights(queries, key_rows, allowed).astype(jnp.bfloat16)
            attended = contract(weights, value_rows, 1, 0)
            parts.append((attended * scale_ref[head]).astype(jnp.bfloat16))
        at = 2 * HD * pair
        scaled_ref[:, at : at + 2 * HD] = jnp.concatenate(parts, axis=1)


def attention_backward(scale_ref, project_ref, starts_ref, grad_ref, out_ref, scale_grad_ref):
    allowed = allowed_pairs(starts_ref)
    span = grad_ref.shape[1]
    score_scale = 1.0 / math.sqrt(HD)
    for pair in range(span // (2 * HD)):
        parts = ([], [], [])
        sums = []
        for head in (2 * pair, 2 * pair + 1):
            queries, key_rows, value_rows = head_parts(project_ref, head)
            upstream = grad_ref[:, head * HD : head * HD + HD]
            weights = head_weights(queries, key_rows, allowed)
            weights_low = weights.astype(jnp.bfloat16)
            attended = contract(weights_low, value_rows, 1, 0)
            wide = upstream.astype(jnp.float32)
            sums.append(jnp.sum(wide * attended, axis=0, keepdims=True))
            grad_attended = (wide * scale_ref[head]).astype(jnp.bfloat16)
            grad_weights = contract(grad_attended, value_rows, 1, 1)
            inner = jnp.sum(weights * grad_weights, axis=-1, keepdims=True)
            grad_scores = (weights * (grad_weights - inner)).astype(jnp.bfloat16)
            parts[0].append(contract(grad_scores, key_rows, 1, 0) * score_scale)
            parts[1].append(contract(grad_scores, queries, 0, 0) * score_scale)
            parts[2].append(contract(weights_low, grad_attended, 0, 0))
        at = 2 * HD * pair
        for which in range(3):
            both = jnp.concatenate(parts[which], axis=1).astype(jnp.bfloat16)
            out_ref[:, which * span + at : which * span + at + 2 * HD] = both
        scale_grad_ref[pair : pair + 1, :] = jnp.concatenate(sums, axis=1)


def pack_columns(place_ref, qkv_ref, up_ref, own_ref, there_ref):
    core, near = place_ref[0], place_ref[1]
    layers, shard, width = qkv_ref.shape
    span = width // 2
    blocks = up_ref.shape[2] // 512
    for layer in range(layers):
        for at in range(0, width, 256):
            parts = [qkv_ref[layer, :, at + HD * i : at + HD * (i + 1)] for i in range(4)]
            even = jnp.concatenate([parts[0], parts[2]], axis=1)
            odd = jnp.concatenate([parts[1], parts[3]], axis=1)

            @pl.when(core == 0)
            def _():
                own_ref[layer, :, at // 2 : at // 2 + 128] = even
                there_ref[layer, :, at // 2 : at // 2 + 128] = odd

            @pl.when(core == 1)
            def _():
                own_ref[layer, :, at // 2 : at // 2 + 128] = odd
                there_ref[layer, :, at // 2 : at // 2 + 128] = even

        for out_ref, which in ((own_ref, core), (there_ref, 1 - core)):
            for part, side in enumerate((near, 1 - near)):
                for block in range(blocks):
                    at = span + (part * blocks + block) * 128
                    source = pl.multiple_of(block * 512 + which * 256 + side * 128, 128)
                    out_ref[layer, :, at : at + 128] = up_ref[layer, :, pl.ds(source, 128)]


def pack_rows(place_ref, own_ref, there_ref, out_ref, down_ref, *units):
    core, near = place_ref[0], place_ref[1]
    layers, shard, width = out_ref.shape
    half = width // 2
    span = own_ref.shape[2] - 2 * width
    first, up, down, second = units
    attention, ups = (first, second.at[:, : 2 * width]), (up, second.at[:, 2 * width : 4 * width])
    downs = (down, second.at[:, 4 * width :])
    for layer in range(layers):
        for source_ref, which in ((own_ref, core), (there_ref, 1 - core)):
            rows = pl.ds(pl.multiple_of(which * shard, shard), shard)
            attention[layer][rows, :span] = source_ref[layer, :, :span]
            columns = ups[layer].shape[1]
            ups[layer][rows, :] = source_ref[layer, :, span : span + columns]
        attention[layer][:shard, span:] = out_ref[layer, :, :half]
        attention[layer][shard:, span:] = out_ref[layer, :, half:]
        for part in range(downs[layer].shape[1] // width):
            side = near if part == 0 else 1 - near
            rows = pl.ds(pl.multiple_of(side * 2 * shard, 2 * shard), 2 * shard)
            downs[layer][:, part * width : part * width + width] = down_ref[layer, rows, :]


def finish_rows(place_ref, *refs):
    core, near = place_ref[0], place_ref[1]
    outs = refs[-4:]
    for layer in range(len(refs[:-4]) // 3):
        at_ref, ff_ref, there_ref = refs[3 * layer : 3 * layer + 3]
        qkv_ref, out_ref, up_ref, down_ref = (out.at[layer] for out in outs)
        shard, half = out_ref.shape
        span = qkv_ref.shape[1] // 2
        rows = pl.ds(pl.multiple_of(core * shard, shard), shard)
        out_ref[:, : half // 2] = at_ref[:shard, span:]
        out_ref[:, half // 2 :] = at_ref[shard:, span:]
        for side in range(2):
            part = near if side == 0 else 1 - near
            first = pl.multiple_of(2 * half + half * part, half)
            down_ref[2 * shard * side : 2 * shard * (side + 1), :] = ff_ref[:, pl.ds(first, half)]
        own = at_ref[rows, :span]
        other = there_ref[:, :span].astype(jnp.float32)
        even = jnp.where(core == 0, own, other)
        odd = jnp.where(core == 0, other, own)
        for at in range(0, span, HD):
            both = jnp.concatenate([even[:, at : at + HD], odd[:, at : at + HD]], axis=1)
            qkv_ref[:, 2 * at : 2 * at + 2 * HD] = both
        blocks = half // 128
        for part in range(2):
            side = near if part == 0 else 1 - near
            for block in range(blocks):
                at = half * part + 128 * block
                to = block * 512 + side * 128
                mine = pl.ds(pl.multiple_of(to + core * 256, 128), 128)
                up_ref[:, mine] = ff_ref[rows, at : at + 128]
                theirs = pl.ds(pl.multiple_of(to + (1 - core) * 256, 128), 128)
                up_ref[:, theirs] = there_ref[:, span + at : span + at + 128].astype(jnp.float32)


def term_product(lefts, lefts_there, rights, parts, shape):
    count = len(lefts)

    def body(*refs):
        right_ref, right_there_ref, out_ref = refs[2 * count :]
        for which, left_at, right_at, columns, out_at in parts:
            right = right_ref[:, right_at : right_at + columns]
            right_there = right_there_ref[:, right_at : right_at + columns]
            for row in range(0, shape[0], 256):
                left = refs[which][:, left_at + row : left_at + row + 256]
                left_there = refs[count + which][:, left_at + row : left_at + row + 256]
                total = contract(left, right, 0, 0) + contract(left_there, right_there, 0, 0)
                out_ref[row : row + 256, out_at : out_at + columns] = total.astype(jnp.bfloat16)

    vmem = pl.BlockSpec(memory_space=pltpu.VMEM)
    return pl.pallas_call(
        body,
        out_shape=jax.ShapeDtypeStruct(shape, jnp.bfloat16),
        in_specs=[vmem] * (2 * count + 2),
        out_specs=vmem,
    )(*lefts, *lefts_there, *rights)


def run_small(body, scale, arrays, outs):
    vmem = pl.BlockSpec(memory_space=pltpu.VMEM)
    return pl.pallas_call(
        body,
        out_shape=[jax.ShapeDtypeStruct(*out) for out in outs],
        in_specs=[pl.BlockSpec(memory_space=pltpu.SMEM)] + [vmem] * len(arrays),
        out_specs=[vmem] * len(outs),
    )(scale, *arrays)


SWAP = ((0, 1), (1, 0))


def swap(array, axis):
    return lax.ppermute(array, axis, SWAP)


def turn(array):
    return lax.ppermute(array, ("c", "y"), ((0, 0), (1, 2), (2, 1), (3, 3)))


def norm_parts(values):
    center = values - jnp.mean(values, axis=-1, keepdims=True)
    inverse = lax.rsqrt(jnp.mean(center * center, axis=-1, keepdims=True) + norm_eps)
    return center * inverse, inverse


def local_chip(
    tokens,
    seq_start,
    qkv_weight,
    out_weight,
    fc1_weight,
    fc2_weight,
    norm_gain,
    norm_bias,
    mid_gain,
    mid_bias,
    head_scale,
    cotangent,
):
    nz, nx = lax.axis_size("z"), lax.axis_size("x")
    iz, ix, ic, iy = (lax.axis_index(name) for name in ("z", "x", "c", "y"))
    chips = nz * nx
    rows, width = tokens.shape
    group_rows = seq_start.shape[0]
    hidden_width = fc1_weight.shape[2]
    shard = qkv_weight.shape[1]
    block = hidden_width // (4 * chips)
    heads_here = H // 2
    head_width = width // 2
    units = hidden_width // 2
    half_units = units // 2
    half = width // 2
    wide = 3 * head_width // 2
    f32, bf16 = jnp.float32, jnp.bfloat16

    def pick(array, which, axis):
        return lax.dynamic_index_in_dim(array, which, axis, keepdims=False)

    def cores(own, other, axis=0):
        first = jnp.where(ic == 0, own, other)
        second = jnp.where(ic == 0, other, own)
        return jnp.concatenate([first, second], axis=axis)

    def both_cores(partial_sum):
        low = lax.optimization_barrier(partial_sum.astype(bf16))
        return low.astype(f32) + swap(low, "c").astype(f32)

    def ordered(first, second, axis):
        near = jnp.where(iy == 0, first, second)
        far = jnp.where(iy == 0, second, first)
        return jnp.concatenate([near, far], axis=axis)

    def gather(array):
        return lax.all_gather(array, ("z", "x"), axis=0, tiled=True)

    def scatter(array):
        return lax.psum_scatter(
            array.astype(bf16), ("z", "x"), scatter_dimension=0, tiled=True
        ).astype(f32)

    def step_x(array):
        split = array.reshape(nz, nx, -1, array.shape[1])
        there = swap(pick(split, 1 - ix, 1).astype(bf16), "x")
        return pick(split, ix, 1).astype(f32) + there.astype(f32)

    def step_z(array):
        total = pick(array, iz, 0)
        for step in range(1, nz):
            there = pick(array, (iz + step) % nz, 0).astype(bf16)
            ring = [(i, (i + step) % nz) for i in range(nz)]
            total = total + lax.ppermute(there, "z", ring).astype(f32)
        return total

    def steps(array):
        return step_z(step_x(array))

    def tie(value, *others):
        return lax.optimization_barrier((value,) + others)

    def z_pieces(array):
        return [array] + [
            lax.ppermute(array, "z", [(i, (i + step) % nz) for i in range(nz)])
            for step in range(1, nz)
        ]

    def join(pieces):
        held = jnp.zeros((nz, nx) + pieces[0].shape, pieces[0].dtype)
        for step, piece in enumerate(pieces):
            for at_x, part in ((ix, piece), (1 - ix, swap(piece, "x"))):
                at = ((iz - step) % nz, at_x, 0, 0)
                held = lax.dynamic_update_slice(held, part[None, None], at)
        return held.reshape(-1, pieces[0].shape[1])

    place = jnp.stack([ic, iy]).astype(jnp.int32)
    narrow = (LAYERS, shard, 3 * head_width + units)
    own, there = run_small(
        pack_columns, place, (qkv_weight, fc1_weight), [(narrow, bf16), (narrow, bf16)]
    )
    packed = run_small(
        pack_rows,
        place,
        (own, swap(there, "c"), out_weight, fc2_weight),
        [((2 * shard, columns), bf16) for columns in (2 * width, width, width, 6 * width)],
    )
    late = gather(packed[3])
    got = []
    for unit in (packed[1], packed[2], packed[0]):
        if got:
            unit, got[-1][1] = tie(unit, got[-1][1])
        got.append(z_pieces(unit))
    got = [join(pieces) for pieces in got]
    up_there, down_there = swap(got[0], "y"), swap(got[1], "y")
    late_parts = [late[:, width * part : width * (part + 1)] for part in range(2, 6)]
    ups = [(got[0], up_there), late_parts[:2]]
    downs = [(got[1], down_there), late_parts[2:]]
    attention_mats = [got[2], late]

    def matrices(which):
        packed = attention_mats[which]
        qkv = packed[:, : 3 * head_width]
        out = packed[:, 3 * head_width : 4 * head_width].reshape(chips, 2, shard, half)
        out = jnp.concatenate(
            [out[:, 0].reshape(head_width, half), out[:, 1].reshape(head_width, half)], axis=1
        )
        return qkv, out, ups[which], downs[which]

    def mine_of(vector):
        mine = pick(vector.reshape(chips, 2, 2, block), ic, 1)
        return ordered(mine[:, 0].reshape(-1), mine[:, 1].reshape(-1), 0)

    def slice_of(values, first, size):
        return lax.dynamic_slice_in_dim(values, first, size, 1)

    turned = turn(tokens)
    hidden = cores(turned, swap(turned, "c")).astype(f32)
    starts = jnp.where(ic == iy, seq_start, swap(seq_start, "c"))
    starts = starts[:, None]

    mats = [matrices(which) for which in range(LAYERS)]
    kept = []
    for which in range(LAYERS):
        qkv_mat, out_mat, up_mat, down_mat = mats[which]
        scale_here = pick(head_scale[which].reshape(heads_here, 2), ic, 1)
        norm_a, inv_a = norm_parts(hidden)
        a_low = (norm_a * norm_gain[which, 0] + norm_bias[which, 0]).astype(bf16)
        project = product(a_low, qkv_mat).astype(bf16)
        (scaled,) = run_small(
            attention_forward, scale_here, (project, starts), [((group_rows, head_width), bf16)]
        )
        branch = both_cores(product(scaled, out_mat))
        if which == 1:
            branch, *there = tie(branch, *kept[0][-1][:2])
            kept[0] = kept[0][:-1] + ((*there, kept[0][-1][2]),)
        else:
            branch, far_up, far_down = tie(branch, up_mat[1], down_mat[1])
            up_mat, down_mat = (up_mat[0], far_up), (down_mat[0], far_down)
            mats[0] = (qkv_mat, out_mat, up_mat, down_mat)
        norm_z, inv_z = norm_parts(branch)
        middle = hidden + norm_z * norm_gain[which, 1] + norm_bias[which, 1]
        norm_b, inv_b = norm_parts(middle)
        b_low = (norm_b * norm_gain[which, 2] + norm_bias[which, 2]).astype(bf16)
        pre_act = jnp.concatenate([product(b_low, part) for part in up_mat], axis=1)
        below = 0.5 * (1.0 + lax.erf(pre_act * (1.0 / math.sqrt(2.0))))
        activated = pre_act * below
        mean_here = jnp.mean(activated, axis=-1)
        center = activated - mean_here[:, None]
        stats = jnp.stack([mean_here, jnp.mean(center * center, axis=-1)])
        stats_there = swap(stats, "c")
        mean_all = 0.5 * (stats[0] + stats_there[0])
        apart = 0.5 * (stats[0] - stats_there[0])
        spread = 0.5 * (stats[1] + stats_there[1]) + apart * apart
        inv_m = lax.rsqrt(spread + norm_eps)[:, None]
        norm_m = (activated - mean_all[:, None]) * inv_m
        gain_m, bias_m = mine_of(mid_gain[which]), mine_of(mid_bias[which])
        mixed_low = (norm_m * gain_m + bias_m).astype(bf16)
        near, far = mixed_low[:, :half_units], mixed_low[:, half_units:]
        hidden = middle + both_cores(product(near, down_mat[0]) + product(far, down_mat[1]))
        attention_in = jnp.concatenate([a_low, scaled], axis=1)
        mixed_there = jnp.concatenate([far, near], axis=1)
        if which == 1:
            mixed_there = swap(mixed_there, "y")
        ins_there = (swap(attention_in, "y"), swap(b_low, "y"), mixed_there)
        kept.append(
            (
                norm_a, inv_a, project, scale_here, norm_z, inv_z, norm_b, inv_b, pre_act, below, norm_m, inv_m, gain_m,
                attention_in, b_low, mixed_low, ins_there,
            )
        )
    output = lax.dynamic_slice_in_dim(hidden.astype(bf16), ic * rows, rows, 0)
    turned = turn(cotangent)
    grad_hidden = cores(turned, swap(turned, "c")).astype(f32)

    def natural(values):
        return ordered(values[:half_units], values[half_units:], 0)

    vectors, pending = [None] * LAYERS, [None] * LAYERS
    for which in reversed(range(LAYERS)):
        qkv_mat, out_mat, up_mat, down_mat = mats[which]
        (
            norm_a, inv_a, project, scale_here, norm_z, inv_z, norm_b, inv_b, pre_act, below, norm_m, inv_m, gain_m,
            attention_in, b_low, mixed_low, ins_there,
        ) = kept[which]
        attention_there, b_there, mixed_there = ins_there
        if which == 0:
            grad_hidden, mixed_there = tie(grad_hidden, mixed_there)
            mixed_there = swap(mixed_there, "y")
        final_low = grad_hidden.astype(bf16)
        grad_mixed = jnp.concatenate([product(final_low, part.T) for part in down_mat], axis=1)
        mid_gain_grad = jnp.sum(grad_mixed * norm_m, axis=0)
        mid_bias_grad = jnp.sum(grad_mixed, axis=0)
        scaled_grad = grad_mixed * gain_m
        sums = jnp.stack([jnp.sum(scaled_grad, axis=-1), jnp.sum(scaled_grad * norm_m, axis=-1)])
        sums = (sums + swap(sums, "c")) / hidden_width
        grad_act = inv_m * (scaled_grad - sums[0][:, None] - norm_m * sums[1][:, None])
        slope = below + pre_act * jnp.exp(-0.5 * pre_act * pre_act) * (1.0 / math.sqrt(2 * math.pi))
        grad_pre = (grad_act * slope).astype(bf16)
        if which == 1:
            grad_pre, attention_there, b_there = tie(grad_pre, attention_there, b_there)
        else:
            grad_pre, at_there = tie(grad_pre, at_there)
            later = finish_attention(at_there)
        near, far = grad_pre[:, :half_units], grad_pre[:, half_units:]

        def unit_columns(side):
            first = side * (half_units // 2)
            return (
                slice_of(near, first, half_units // 2),
                slice_of(far, first, half_units // 2),
                slice_of(final_low, side * half, half),
            )

        keep_n, keep_f, keep_c = unit_columns(iy)
        send_n, send_f, send_c = unit_columns(1 - iy)
        ff_there = swap(jnp.concatenate([send_f, send_n, send_c], axis=1), "y")
        ff_out = jnp.concatenate([keep_n, keep_f, keep_c], axis=1)
        grad_ff_in = both_cores(product(near, up_mat[0].T) + product(far, up_mat[1].T))
        grad_mid_in, gain_two, bias_two = norm_backward(
            grad_ff_in, norm_b, inv_b, norm_gain[which, 2]
        )
        grad_middle = grad_hidden + grad_mid_in
        grad_branch, gain_one, bias_one = norm_backward(
            grad_middle, norm_z, inv_z, norm_gain[which, 1]
        )
        branch_low = grad_branch.astype(bf16)
        if which == 0:
            branch_low, later = tie(branch_low, later)
            later = step_x(later)
        grad_heads = product(branch_low, out_mat.T).astype(bf16)
        grad_project, scale_grad = run_small(
            attention_backward,
            scale_here,
            (project, starts, grad_heads),
            [((group_rows, 3 * head_width), bf16), ((heads_here // 2, 2 * HD), f32)],
        )
        scale_grad = jnp.sum(scale_grad.reshape(heads_here, HD), axis=1)
        grad_project, ff_there, mixed_there = tie(grad_project, ff_there, mixed_there)
        ff_term = term_product(
            (b_low, mixed_low),
            (b_there, mixed_there),
            (ff_out, ff_there),
            ((0, 0, 0, width, 0), (1, 0, width, half, width), (1, width, width, half, width + half)),
            (width, 2 * width),
        )
        if which == 1:
            grad_project, ff_term = tie(grad_project, ff_term)
            ff_rows = scatter(ff_term)
        grad_normed = both_cores(product(grad_project, qkv_mat.T))
        grad_input, gain_zero, bias_zero = norm_backward(
            grad_normed, norm_a, inv_a, norm_gain[which, 0]
        )

        at_out = jnp.concatenate(
            [slice_of(grad_project, iy * wide, wide), slice_of(branch_low, iy * half, half)], axis=1
        )
        at_there = jnp.concatenate(
            [
                slice_of(grad_project, (1 - iy) * wide, wide),
                slice_of(branch_low, (1 - iy) * half, half),
            ],
            axis=1,
        )
        at_there = swap(at_there, "y")
        grad_hidden = grad_middle + grad_input

        def attention_term(there, here=at_out, ins=attention_in, ins_there=attention_there):
            split = half // 2
            rights = (here, there)
            out_term = term_product(
                (ins,), (ins_there,), rights, ((0, width, wide, half, 0),), (head_width, half)
            ).reshape(chips, shard, half)
            out_term = jnp.concatenate([out_term[..., :split], out_term[..., split:]], axis=1)
            qkv_term = term_product(
                (ins,), (ins_there,), rights, ((0, 0, 0, wide, 0),), (width, wide)
            )
            return jnp.concatenate([qkv_term, out_term.reshape(-1, split)], axis=1)

        if which == 1:
            finish_attention = attention_term
        else:
            grad_hidden, later = tie(grad_hidden, later)
            at_rows_last = step_z(later)
        if which == 1:
            pending[1] = ff_rows
        shared = jnp.concatenate([gain_zero, gain_one, gain_two, bias_zero, bias_one, bias_two])
        vectors[which] = jnp.concatenate(
            [0.5 * shared, natural(mid_gain_grad), natural(mid_bias_grad), jnp.pad(scale_grad, (0, 128 - heads_here))]
        )

    vector = jnp.stack(vectors)
    vector = vector + swap(vector, "y")
    vector = vector + swap(vector, "x")
    vector, ff_term = tie(vector, ff_term)
    up_held, down_held = step_x(ff_term[:, :width]), step_x(ff_term[:, width:])
    vector = sum(z_pieces(vector))
    at_held = step_x(attention_term(at_there))
    at_held, output, grad_hidden = tie(at_held, output, grad_hidden)
    pending[0] = jnp.concatenate([step_z(up_held), step_z(down_held)], axis=1)
    at_rows = step_z(at_held)
    finals = []
    for at_rows, ff_rows in ((at_rows, pending[0]), (at_rows_last, pending[1])):
        send = jnp.concatenate([at_rows[:, :wide], ff_rows[:, :width]], axis=1)
        send = lax.dynamic_slice_in_dim(send, (1 - ic) * shard, shard, 0).astype(bf16)
        finals.extend([at_rows, ff_rows, swap(send, "c")])
    shapes = ((shard, 2 * wide), (shard, half), (shard, 2 * width), (4 * shard, half))
    summed = run_small(
        finish_rows, place, finals, [((LAYERS,) + shape, f32) for shape in shapes]
    )
    grad_tokens = turn(lax.dynamic_slice_in_dim(grad_hidden, ic * rows, rows, 0))
    output = turn(output)
    there = swap(vector, "c")
    shared = vector[:, : 6 * width] + there[:, : 6 * width]

    def spread_units(first):
        view = (LAYERS, 2, chips, 1, block)
        own, other = (part[:, first : first + units] for part in (vector, there))
        own, other = own.reshape(view), other.reshape(view)
        return cores(own, other, 3).transpose(0, 2, 3, 1, 4).reshape(LAYERS, hidden_width)

    scale_at = 6 * width + 2 * units
    own, other = (
        part[:, scale_at : scale_at + heads_here].reshape(LAYERS, heads_here, 1)
        for part in (vector, there)
    )
    return (
        output,
        grad_tokens,
        summed[0],
        summed[1],
        summed[2],
        summed[3],
        shared[:, : 3 * width].reshape(LAYERS, 3, width),
        shared[:, 3 * width :].reshape(LAYERS, 3, width),
        spread_units(6 * width),
        spread_units(6 * width + units),
        cores(own, other, 2).reshape(LAYERS, H),
    )


def solution(mesh):
    dp, sp = mesh.shape["dp"], mesh.shape["sp"]
    if sp == 2 and dp == 16:
        mesh = Mesh(mesh.devices.reshape(4, dp // 8, 2, 2), ("z", "x", "c", "y"))
        rows, every, cols, body = ("z", "x", "c"), ("z", "x", "c", "y"), "y", local_chip
    else:
        rows, every, cols, body = "dp", ("dp", "sp"), "sp", local_any
    weight = P(None, rows, None)
    in_specs = (P(every, None), P(rows), weight, weight, weight, weight)
    in_specs = in_specs + (P(),) * 5 + (P(every, None),)
    grad = P(None, rows, cols)
    out_specs = (P(every, None), P(every, None), grad, grad, grad, grad) + (P(),) * 5
    return jax.shard_map(body, mesh=mesh, in_specs=in_specs, out_specs=out_specs, check_vma=False)
```

```python
from functools import partial
import math

import jax
import jax.numpy as jnp
from jax import lax
from jax.experimental import pallas as pl
from jax.experimental.pallas import tpu as pltpu
from jax.sharding import Mesh, PartitionSpec as P

H = 16
HD = 64
LAYERS = 2


norm_eps = 1e-05


def for_sending(array):

    def short(part):
        return part.astype(jnp.bfloat16) if part.dtype == jnp.float32 else part

    return jax.tree.map(short, array)


def norm_forward(values, gain, bias):
    center = values - jnp.mean(values, axis=-1, keepdims=True)
    inverse = lax.rsqrt(jnp.mean(center * center, axis=-1, keepdims=True) + norm_eps)
    normal = center * inverse
    return (normal * gain + bias, normal, inverse)


def norm_backward(upstream, normal, inverse, gain):
    scaled = upstream * gain
    grad_values = inverse * (
        scaled
        - jnp.mean(scaled, axis=-1, keepdims=True)
        - normal * jnp.mean(scaled * normal, axis=-1, keepdims=True)
    )
    return (grad_values, jnp.sum(upstream * normal, axis=0), jnp.sum(upstream, axis=0))


def product(left, right):
    return jnp.dot(left, right, preferred_element_type=jnp.float32)


def block_layout(length):
    block_count = min(4, max(1, length // 512))
    return (block_count, length // block_count)


def score_block(query_block, query_pos, query_start, key_rows, score_scale):
    key_pos = jnp.arange(key_rows.shape[0], dtype=jnp.int32)
    scores = (
        jnp.einsum("qhd,khd->hqk", query_block, key_rows, preferred_element_type=jnp.float32)
        * score_scale
    )
    allowed = (key_pos[None, :] >= query_start[:, None]) & (key_pos[None, :] <= query_pos[:, None])
    return jnp.where(allowed[None], scores, -1e30)


def attend_forward(queries, key_rows, value_rows, starts, score_scale):
    length = queries.shape[0]
    block_count, block_rows = block_layout(length)
    positions = jnp.arange(length, dtype=jnp.int32)
    results, maxima, totals = ([], [], [])
    for block_index in range(block_count):
        row_first = block_index * block_rows
        row_end = row_first + block_rows
        scores = score_block(
            queries[row_first:row_end],
            positions[row_first:row_end],
            starts[row_first:row_end],
            key_rows[:row_end],
            score_scale,
        )
        row_max = jnp.max(scores, axis=-1, keepdims=True)
        exponent = jnp.exp(scores - row_max)
        row_total = jnp.sum(exponent, axis=-1, keepdims=True)
        weights_low = (exponent / row_total).astype(jnp.bfloat16)
        results.append(
            jnp.einsum(
                "hqk,khd->qhd",
                weights_low,
                value_rows[:row_end],
                preferred_element_type=jnp.float32,
            )
        )
        maxima.append(row_max)
        totals.append(row_total)
    return (jnp.concatenate(results, axis=0), maxima, totals)


def attend_backward(queries, key_rows, value_rows, starts, score_scale, grad_out, maxima, totals):
    length, heads_here, head_dim = queries.shape
    block_count, block_rows = block_layout(length)
    positions = jnp.arange(length, dtype=jnp.int32)
    grad_keys = jnp.zeros((length, heads_here, head_dim), jnp.float32)
    grad_values = jnp.zeros((length, heads_here, head_dim), jnp.float32)
    query_grads = []
    for block_index in range(block_count):
        row_first = block_index * block_rows
        row_end = row_first + block_rows
        query_block = queries[row_first:row_end]
        grad_block = grad_out[row_first:row_end]
        scores = score_block(
            query_block,
            positions[row_first:row_end],
            starts[row_first:row_end],
            key_rows[:row_end],
            score_scale,
        )
        weights_full = jnp.exp(scores - maxima[block_index]) / totals[block_index]
        weights_low = weights_full.astype(jnp.bfloat16)
        grad_weights = jnp.einsum(
            "qhd,khd->hqk", grad_block, value_rows[:row_end], preferred_element_type=jnp.float32
        )
        inner = jnp.sum(weights_full * grad_weights, axis=-1, keepdims=True)
        grad_scores = (weights_full * (grad_weights - inner)).astype(jnp.bfloat16)
        query_grads.append(
            jnp.einsum(
                "hqk,khd->qhd", grad_scores, key_rows[:row_end], preferred_element_type=jnp.float32
            )
            * score_scale
        )
        grad_keys = grad_keys.at[:row_end].add(
            jnp.einsum("hqk,qhd->khd", grad_scores, query_block, preferred_element_type=jnp.float32)
            * score_scale
        )
        grad_values = grad_values.at[:row_end].add(
            jnp.einsum("hqk,qhd->khd", weights_low, grad_block, preferred_element_type=jnp.float32)
        )
    return (jnp.concatenate(query_grads, axis=0), grad_keys, grad_values)


def local_any(
    tokens,
    seq_start,
    qkv_weight,
    out_weight,
    fc1_weight,
    fc2_weight,
    norm_gain,
    norm_bias,
    mid_gain,
    mid_bias,
    head_scale,
    cotangent,
):
    split_count = lax.axis_size("sp")
    split_rank = lax.axis_index("sp")
    local_rows, width_model = tokens.shape
    group_rows = seq_start.shape[0]
    heads_here = H // split_count
    head_width = heads_here * HD
    score_scale = 1.0 / math.sqrt(HD)
    scale_here = lax.dynamic_slice_in_dim(head_scale, split_rank * heads_here, heads_here, axis=1)
    hidden = tokens.astype(jnp.float32)
    kept_layers = []
    kept_matrices = []
    for which_layer in range(LAYERS):
        matrices = (
            lax.all_gather(qkv_weight[which_layer], "dp", axis=0, tiled=True),
            lax.all_gather(out_weight[which_layer], "dp", axis=0, tiled=True),
            lax.all_gather(fc1_weight[which_layer], "dp", axis=0, tiled=True),
            lax.all_gather(fc2_weight[which_layer], "dp", axis=0, tiled=True),
        )
        qkv_full, out_full, up_full, down_full = matrices
        normed, norm_a, inv_a = norm_forward(
            hidden, norm_gain[which_layer, 0], norm_bias[which_layer, 0]
        )
        normed_low = normed.astype(jnp.bfloat16)
        project = (
            product(normed_low, qkv_full)
            .astype(jnp.bfloat16)
            .reshape(local_rows, 3, split_count, head_width)
        )
        by_heads = lax.all_to_all(project, "sp", split_axis=2, concat_axis=0, tiled=True)
        queries = by_heads[:, 0, 0].reshape(group_rows, heads_here, HD)
        key_rows = by_heads[:, 1, 0].reshape(group_rows, heads_here, HD)
        value_rows = by_heads[:, 2, 0].reshape(group_rows, heads_here, HD)
        attended, maxima, totals = attend_forward(
            queries, key_rows, value_rows, seq_start, score_scale
        )
        scaled = (
            (attended * scale_here[which_layer][None, :, None])
            .astype(jnp.bfloat16)
            .reshape(group_rows, 1, head_width)
        )
        gathered = lax.all_to_all(scaled, "sp", split_axis=0, concat_axis=1, tiled=True).reshape(
            local_rows, width_model
        )
        branch = product(gathered, out_full)
        branch_norm, norm_z, inv_z = norm_forward(
            branch, norm_gain[which_layer, 1], norm_bias[which_layer, 1]
        )
        middle = hidden + branch_norm
        normed_ff, norm_b, inv_b = norm_forward(
            middle, norm_gain[which_layer, 2], norm_bias[which_layer, 2]
        )
        ff_low = normed_ff.astype(jnp.bfloat16)
        pre_act = product(ff_low, up_full)
        activated = jax.nn.gelu(pre_act, approximate=False)
        mixed, norm_m, inv_m = norm_forward(activated, mid_gain[which_layer], mid_bias[which_layer])
        mixed_low = mixed.astype(jnp.bfloat16)
        hidden = middle + product(mixed_low, down_full)
        kept_layers.append(
            (
                norm_a,
                inv_a,
                normed_low,
                queries,
                key_rows,
                value_rows,
                attended,
                maxima,
                totals,
                gathered,
                norm_z,
                inv_z,
                norm_b,
                inv_b,
                ff_low,
                pre_act,
                norm_m,
                inv_m,
                mixed_low,
            )
        )
        kept_matrices.append(matrices)
    output = hidden.astype(jnp.bfloat16)
    grad_hidden = cotangent.astype(jnp.float32)
    matrix_grads = [None] * LAYERS
    gain_grads = [None] * LAYERS
    bias_grads = [None] * LAYERS
    mid_gain_grads = [None] * LAYERS
    mid_bias_grads = [None] * LAYERS
    scale_grads = [None] * LAYERS
    for which_layer in reversed(range(LAYERS)):
        (
            norm_a,
            inv_a,
            normed_low,
            queries,
            key_rows,
            value_rows,
            attended,
            maxima,
            totals,
            gathered,
            norm_z,
            inv_z,
            norm_b,
            inv_b,
            ff_low,
            pre_act,
            norm_m,
            inv_m,
            mixed_low,
        ) = kept_layers[which_layer]
        qkv_full, out_full, up_full, down_full = (
            lax.all_gather(qkv_weight[which_layer], "dp", axis=0, tiled=True),
            lax.all_gather(out_weight[which_layer], "dp", axis=0, tiled=True),
            lax.all_gather(fc1_weight[which_layer], "dp", axis=0, tiled=True),
            lax.all_gather(fc2_weight[which_layer], "dp", axis=0, tiled=True),
        )
        grad_final = grad_hidden.astype(jnp.bfloat16)
        grad_mixed = product(grad_final, down_full.T)
        grad_act, mid_gain_grad, mid_bias_grad = norm_backward(
            grad_mixed, norm_m, inv_m, mid_gain[which_layer]
        )
        gelu_value, gelu_pull = jax.vjp(partial(jax.nn.gelu, approximate=False), pre_act)
        grad_pre = gelu_pull(grad_act)[0].astype(jnp.bfloat16)
        grad_ff_in = product(grad_pre, up_full.T)
        grad_mid_in, gain_two, bias_two = norm_backward(
            grad_ff_in, norm_b, inv_b, norm_gain[which_layer, 2]
        )
        grad_middle = grad_hidden + grad_mid_in
        grad_branch_full, gain_one, bias_one = norm_backward(
            grad_middle, norm_z, inv_z, norm_gain[which_layer, 1]
        )
        grad_branch = grad_branch_full.astype(jnp.bfloat16)
        grad_gathered = (
            product(grad_branch, out_full.T)
            .astype(jnp.bfloat16)
            .reshape(local_rows, split_count, head_width)
        )
        grad_heads = lax.all_to_all(
            grad_gathered, "sp", split_axis=1, concat_axis=0, tiled=True
        ).reshape(group_rows, heads_here, HD)
        scale_grad_here = jnp.sum(grad_heads.astype(jnp.float32) * attended, axis=(0, 2))
        grad_attended = (grad_heads * scale_here[which_layer][None, :, None]).astype(jnp.bfloat16)
        grad_queries, grad_keys, grad_values = attend_backward(
            queries, key_rows, value_rows, seq_start, score_scale, grad_attended, maxima, totals
        )
        stacked = jnp.stack(
            [
                grad_queries.reshape(group_rows, head_width),
                grad_keys.reshape(group_rows, head_width),
                grad_values.reshape(group_rows, head_width),
            ],
            axis=1,
        )
        stacked = stacked.astype(jnp.bfloat16).reshape(group_rows, 3, 1, head_width)
        back_rows = lax.all_to_all(stacked, "sp", split_axis=0, concat_axis=2, tiled=True).reshape(
            local_rows, 3 * width_model
        )
        grad_normed = product(back_rows, qkv_full.T)
        grad_input, gain_zero, bias_zero = norm_backward(
            grad_normed, norm_a, inv_a, norm_gain[which_layer, 0]
        )
        grad_hidden = grad_middle + grad_input
        group_inputs = (
            lax.all_gather(normed_low, "sp", axis=0, tiled=True),
            lax.all_gather(gathered, "sp", axis=0, tiled=True),
            lax.all_gather(ff_low, "sp", axis=0, tiled=True),
            lax.all_gather(mixed_low, "sp", axis=0, tiled=True),
        )
        group_columns = (
            lax.all_to_all(
                back_rows.reshape(local_rows, split_count, -1),
                "sp",
                split_axis=1,
                concat_axis=0,
                tiled=True,
            ),
            lax.all_to_all(
                grad_branch.reshape(local_rows, split_count, -1),
                "sp",
                split_axis=1,
                concat_axis=0,
                tiled=True,
            ),
            lax.all_to_all(
                grad_pre.reshape(local_rows, split_count, -1),
                "sp",
                split_axis=1,
                concat_axis=0,
                tiled=True,
            ),
            lax.all_to_all(
                grad_final.reshape(local_rows, split_count, -1),
                "sp",
                split_axis=1,
                concat_axis=0,
                tiled=True,
            ),
        )
        terms = tuple(
            (
                product(group_inputs[which].T, group_columns[which].reshape(group_rows, -1))
                for which in range(4)
            )
        )
        matrix_grads[which_layer] = jax.tree.map(
            lambda part: part.astype(jnp.float32),
            lax.psum_scatter(for_sending(terms), "dp", scatter_dimension=0, tiled=True),
        )
        gain_grads[which_layer] = jnp.stack([gain_zero, gain_one, gain_two])
        bias_grads[which_layer] = jnp.stack([bias_zero, bias_one, bias_two])
        mid_gain_grads[which_layer] = mid_gain_grad
        mid_bias_grads[which_layer] = mid_bias_grad
        scale_grads[which_layer] = lax.dynamic_update_slice(
            jnp.zeros((H,), jnp.float32), scale_grad_here, (split_rank * heads_here,)
        )
    summed = tuple((jnp.stack([pieces[which] for pieces in matrix_grads]) for which in range(4)))
    small_sums = lax.psum(
        (
            jnp.stack(gain_grads),
            jnp.stack(bias_grads),
            jnp.stack(mid_gain_grads),
            jnp.stack(mid_bias_grads),
            jnp.stack(scale_grads),
        ),
        ("dp", "sp"),
    )
    return (
        output,
        grad_hidden,
        summed[0],
        summed[1],
        summed[2],
        summed[3],
        small_sums[0],
        small_sums[1],
        small_sums[2],
        small_sums[3],
        small_sums[4],
    )


def contract(left, right, left_axis, right_axis):
    return lax.dot_general(
        left, right, (((left_axis,), (right_axis,)), ((), ())), preferred_element_type=jnp.float32
    )


def head_parts(project_ref, head):
    span = project_ref.shape[1] // 3
    at = head * HD
    return (project_ref[:, base + at : base + at + HD] for base in (0, span, 2 * span))


def head_weights(queries, key_rows, allowed):
    scores = contract(queries, key_rows, 1, 1) * (1.0 / math.sqrt(HD))
    scores = jnp.where(allowed, scores, -1e30)
    exponent = jnp.exp(scores - jnp.max(scores, axis=-1, keepdims=True))
    return exponent / jnp.sum(exponent, axis=-1, keepdims=True)


def allowed_pairs(starts_ref):
    length = starts_ref.shape[0]
    row = lax.broadcasted_iota(jnp.int32, (length, length), 0)
    col = lax.broadcasted_iota(jnp.int32, (length, length), 1)
    return (col >= starts_ref[...]) & (col <= row)


def attention_forward(scale_ref, project_ref, starts_ref, scaled_ref):
    allowed = allowed_pairs(starts_ref)
    for pair in range(scaled_ref.shape[1] // (2 * HD)):
        parts = []
        for head in (2 * pair, 2 * pair + 1):
            queries, key_rows, value_rows = head_parts(project_ref, head)
            weights = head_weights(queries, key_rows, allowed).astype(jnp.bfloat16)
            attended = contract(weights, value_rows, 1, 0)
            parts.append((attended * scale_ref[head]).astype(jnp.bfloat16))
        at = 2 * HD * pair
        scaled_ref[:, at : at + 2 * HD] = jnp.concatenate(parts, axis=1)


def attention_backward(scale_ref, project_ref, starts_ref, grad_ref, out_ref, scale_grad_ref):
    allowed = allowed_pairs(starts_ref)
    span = grad_ref.shape[1]
    score_scale = 1.0 / math.sqrt(HD)
    for pair in range(span // (2 * HD)):
        parts = ([], [], [])
        sums = []
        for head in (2 * pair, 2 * pair + 1):
            queries, key_rows, value_rows = head_parts(project_ref, head)
            upstream = grad_ref[:, head * HD : head * HD + HD]
            weights = head_weights(queries, key_rows, allowed)
            weights_low = weights.astype(jnp.bfloat16)
            attended = contract(weights_low, value_rows, 1, 0)
            wide = upstream.astype(jnp.float32)
            sums.append(jnp.sum(wide * attended, axis=0, keepdims=True))
            grad_attended = (wide * scale_ref[head]).astype(jnp.bfloat16)
            grad_weights = contract(grad_attended, value_rows, 1, 1)
            inner = jnp.sum(weights * grad_weights, axis=-1, keepdims=True)
            grad_scores = (weights * (grad_weights - inner)).astype(jnp.bfloat16)
            parts[0].append(contract(grad_scores, key_rows, 1, 0) * score_scale)
            parts[1].append(contract(grad_scores, queries, 0, 0) * score_scale)
            parts[2].append(contract(weights_low, grad_attended, 0, 0))
        at = 2 * HD * pair
        for which in range(3):
            both = jnp.concatenate(parts[which], axis=1).astype(jnp.bfloat16)
            out_ref[:, which * span + at : which * span + at + 2 * HD] = both
        scale_grad_ref[pair : pair + 1, :] = jnp.concatenate(sums, axis=1)


def pack_columns(place_ref, qkv_ref, up_ref, own_ref, there_ref):
    core, near = place_ref[0], place_ref[1]
    layers, shard, width = qkv_ref.shape
    span = width // 2
    blocks = up_ref.shape[2] // 512
    for layer in range(layers):
        for at in range(0, width, 256):
            parts = [qkv_ref[layer, :, at + HD * i : at + HD * (i + 1)] for i in range(4)]
            even = jnp.concatenate([parts[0], parts[2]], axis=1)
            odd = jnp.concatenate([parts[1], parts[3]], axis=1)

            @pl.when(core == 0)
            def _():
                own_ref[layer, :, at // 2 : at // 2 + 128] = even
                there_ref[layer, :, at // 2 : at // 2 + 128] = odd

            @pl.when(core == 1)
            def _():
                own_ref[layer, :, at // 2 : at // 2 + 128] = odd
                there_ref[layer, :, at // 2 : at // 2 + 128] = even

        for out_ref, which in ((own_ref, core), (there_ref, 1 - core)):
            for part, side in enumerate((near, 1 - near)):
                for block in range(blocks):
                    at = span + (part * blocks + block) * 128
                    source = pl.multiple_of(block * 512 + which * 256 + side * 128, 128)
                    out_ref[layer, :, at : at + 128] = up_ref[layer, :, pl.ds(source, 128)]


def pack_rows(place_ref, own_ref, there_ref, out_ref, down_ref, *units):
    core, near = place_ref[0], place_ref[1]
    layers, shard, width = out_ref.shape
    half = width // 2
    span = own_ref.shape[2] - 2 * width
    first, up, down, second = units
    attention, ups = (first, second.at[:, : 2 * width]), (up, second.at[:, 2 * width : 4 * width])
    downs = (down, second.at[:, 4 * width :])
    for layer in range(layers):
        for source_ref, which in ((own_ref, core), (there_ref, 1 - core)):
            rows = pl.ds(pl.multiple_of(which * shard, shard), shard)
            attention[layer][rows, :span] = source_ref[layer, :, :span]
            columns = ups[layer].shape[1]
            ups[layer][rows, :] = source_ref[layer, :, span : span + columns]
        attention[layer][:shard, span:] = out_ref[layer, :, :half]
        attention[layer][shard:, span:] = out_ref[layer, :, half:]
        for part in range(downs[layer].shape[1] // width):
            side = near if part == 0 else 1 - near
            rows = pl.ds(pl.multiple_of(side * 2 * shard, 2 * shard), 2 * shard)
            downs[layer][:, part * width : part * width + width] = down_ref[layer, rows, :]


def finish_rows(place_ref, *refs):
    core, near = place_ref[0], place_ref[1]
    outs = refs[-4:]
    for layer in range(len(refs[:-4]) // 3):
        at_ref, ff_ref, there_ref = refs[3 * layer : 3 * layer + 3]
        qkv_ref, out_ref, up_ref, down_ref = (out.at[layer] for out in outs)
        shard, half = out_ref.shape
        span = qkv_ref.shape[1] // 2
        rows = pl.ds(pl.multiple_of(core * shard, shard), shard)
        out_ref[:, : half // 2] = at_ref[:shard, span:]
        out_ref[:, half // 2 :] = at_ref[shard:, span:]
        for side in range(2):
            part = near if side == 0 else 1 - near
            first = pl.multiple_of(2 * half + half * part, half)
            down_ref[2 * shard * side : 2 * shard * (side + 1), :] = ff_ref[:, pl.ds(first, half)]
        own = at_ref[rows, :span]
        other = there_ref[:, :span].astype(jnp.float32)
        even = jnp.where(core == 0, own, other)
        odd = jnp.where(core == 0, other, own)
        for at in range(0, span, HD):
            both = jnp.concatenate([even[:, at : at + HD], odd[:, at : at + HD]], axis=1)
            qkv_ref[:, 2 * at : 2 * at + 2 * HD] = both
        blocks = half // 128
        for part in range(2):
            side = near if part == 0 else 1 - near
            for block in range(blocks):
                at = half * part + 128 * block
                to = block * 512 + side * 128
                mine = pl.ds(pl.multiple_of(to + core * 256, 128), 128)
                up_ref[:, mine] = ff_ref[rows, at : at + 128]
                theirs = pl.ds(pl.multiple_of(to + (1 - core) * 256, 128), 128)
                up_ref[:, theirs] = there_ref[:, span + at : span + at + 128].astype(jnp.float32)


def term_product(lefts, lefts_there, rights, parts, shape):
    count = len(lefts)

    def body(*refs):
        right_ref, right_there_ref, out_ref = refs[2 * count :]
        for which, left_at, right_at, columns, out_at in parts:
            right = right_ref[:, right_at : right_at + columns]
            right_there = right_there_ref[:, right_at : right_at + columns]
            for row in range(0, shape[0], 256):
                left = refs[which][:, left_at + row : left_at + row + 256]
                left_there = refs[count + which][:, left_at + row : left_at + row + 256]
                total = contract(left, right, 0, 0) + contract(left_there, right_there, 0, 0)
                out_ref[row : row + 256, out_at : out_at + columns] = total.astype(jnp.bfloat16)

    vmem = pl.BlockSpec(memory_space=pltpu.VMEM)
    return pl.pallas_call(
        body,
        out_shape=jax.ShapeDtypeStruct(shape, jnp.bfloat16),
        in_specs=[vmem] * (2 * count + 2),
        out_specs=vmem,
    )(*lefts, *lefts_there, *rights)


def run_small(body, scale, arrays, outs):
    vmem = pl.BlockSpec(memory_space=pltpu.VMEM)
    return pl.pallas_call(
        body,
        out_shape=[jax.ShapeDtypeStruct(*out) for out in outs],
        in_specs=[pl.BlockSpec(memory_space=pltpu.SMEM)] + [vmem] * len(arrays),
        out_specs=[vmem] * len(outs),
    )(scale, *arrays)


SWAP = ((0, 1), (1, 0))


def swap(array, axis):
    return lax.ppermute(array, axis, SWAP)


def turn(array):
    return lax.ppermute(array, ("c", "y"), ((0, 0), (1, 2), (2, 1), (3, 3)))


def norm_parts(values):
    center = values - jnp.mean(values, axis=-1, keepdims=True)
    inverse = lax.rsqrt(jnp.mean(center * center, axis=-1, keepdims=True) + norm_eps)
    return center * inverse, inverse


def local_chip(
    tokens,
    seq_start,
    qkv_weight,
    out_weight,
    fc1_weight,
    fc2_weight,
    norm_gain,
    norm_bias,
    mid_gain,
    mid_bias,
    head_scale,
    cotangent,
):
    nz, nx = lax.axis_size("z"), lax.axis_size("x")
    iz, ix, ic, iy = (lax.axis_index(name) for name in ("z", "x", "c", "y"))
    chips = nz * nx
    rows, width = tokens.shape
    group_rows = seq_start.shape[0]
    hidden_width = fc1_weight.shape[2]
    shard = qkv_weight.shape[1]
    block = hidden_width // (4 * chips)
    heads_here = H // 2
    head_width = width // 2
    units = hidden_width // 2
    half_units = units // 2
    half = width // 2
    wide = 3 * head_width // 2
    f32, bf16 = jnp.float32, jnp.bfloat16

    def pick(array, which, axis):
        return lax.dynamic_index_in_dim(array, which, axis, keepdims=False)

    def cores(own, other, axis=0):
        first = jnp.where(ic == 0, own, other)
        second = jnp.where(ic == 0, other, own)
        return jnp.concatenate([first, second], axis=axis)

    def across(values):
        there = swap(lax.dynamic_slice_in_dim(values, ic * rows, rows, 0), "y")
        return cores(there, swap(there, "c"))

    def both_cores(partial_sum):
        low = lax.optimization_barrier(partial_sum.astype(bf16))
        return low.astype(f32) + swap(low, "c").astype(f32)

    def ordered(first, second, axis):
        near = jnp.where(iy == 0, first, second)
        far = jnp.where(iy == 0, second, first)
        return jnp.concatenate([near, far], axis=axis)

    def gather(array):
        return lax.all_gather(array, ("z", "x"), axis=0, tiled=True)

    def scatter(array):
        return lax.psum_scatter(
            array.astype(bf16), ("z", "x"), scatter_dimension=0, tiled=True
        ).astype(f32)

    def step_x(array):
        split = array.reshape(nz, nx, -1, array.shape[1])
        there = swap(pick(split, 1 - ix, 1).astype(bf16), "x")
        return pick(split, ix, 1).astype(f32) + there.astype(f32)

    def step_z(array):
        total = pick(array, iz, 0)
        for step in range(1, nz):
            there = pick(array, (iz + step) % nz, 0).astype(bf16)
            ring = [(i, (i + step) % nz) for i in range(nz)]
            total = total + lax.ppermute(there, "z", ring).astype(f32)
        return total

    def steps(array):
        return step_z(step_x(array))

    def tie(value, *others):
        return lax.optimization_barrier((value,) + others)

    def z_pieces(array):
        return [array] + [
            lax.ppermute(array, "z", [(i, (i + step) % nz) for i in range(nz)])
            for step in range(1, nz)
        ]

    def join(pieces):
        held = jnp.zeros((nz, nx) + pieces[0].shape, pieces[0].dtype)
        for step, piece in enumerate(pieces):
            for at_x, part in ((ix, piece), (1 - ix, swap(piece, "x"))):
                at = ((iz - step) % nz, at_x, 0, 0)
                held = lax.dynamic_update_slice(held, part[None, None], at)
        return held.reshape(-1, pieces[0].shape[1])

    place = jnp.stack([ic, iy]).astype(jnp.int32)
    narrow = (LAYERS, shard, 3 * head_width + units)
    own, there = run_small(
        pack_columns, place, (qkv_weight, fc1_weight), [(narrow, bf16), (narrow, bf16)]
    )
    packed = run_small(
        pack_rows,
        place,
        (own, swap(there, "c"), out_weight, fc2_weight),
        [((2 * shard, columns), bf16) for columns in (2 * width, width, width, 6 * width)],
    )
    late = gather(packed[3])
    got = []
    for unit in (packed[1], packed[2], packed[0]):
        if got:
            unit, got[-1][1] = tie(unit, got[-1][1])
        got.append(z_pieces(unit))
    got = [join(pieces) for pieces in got]
    up_there, down_there = swap(got[0], "y"), swap(got[1], "y")
    late_parts = [late[:, width * part : width * (part + 1)] for part in range(2, 6)]
    ups = [(got[0], up_there), late_parts[:2]]
    downs = [(got[1], down_there), late_parts[2:]]
    attention_mats = [got[2], late]

    def matrices(which):
        packed = attention_mats[which]
        qkv = packed[:, : 3 * head_width]
        out = packed[:, 3 * head_width : 4 * head_width].reshape(chips, 2, shard, half)
        out = jnp.concatenate(
            [out[:, 0].reshape(head_width, half), out[:, 1].reshape(head_width, half)], axis=1
        )
        return qkv, out, ups[which], downs[which]

    def mine_of(vector):
        mine = pick(vector.reshape(chips, 2, 2, block), ic, 1)
        return ordered(mine[:, 0].reshape(-1), mine[:, 1].reshape(-1), 0)

    def slice_of(values, first, size):
        return lax.dynamic_slice_in_dim(values, first, size, 1)

    turned = turn(tokens)
    hidden = cores(turned, swap(turned, "c")).astype(f32)
    starts = jnp.where(ic == iy, seq_start, swap(seq_start, "c"))
    starts = starts[:, None]

    mats = [matrices(which) for which in range(LAYERS)]
    kept = []
    for which in range(LAYERS):
        qkv_mat, out_mat, up_mat, down_mat = mats[which]
        scale_here = pick(head_scale[which].reshape(heads_here, 2), ic, 1)
        norm_a, inv_a = norm_parts(hidden)
        a_low = (norm_a * norm_gain[which, 0] + norm_bias[which, 0]).astype(bf16)
        project = product(a_low, qkv_mat).astype(bf16)
        (scaled,) = run_small(
            attention_forward, scale_here, (project, starts), [((group_rows, head_width), bf16)]
        )
        branch = both_cores(product(scaled, out_mat))
        if which == 1:
            branch, *there = tie(branch, *kept[0][-1][:3])
            kept[0] = kept[0][:-1] + ((*there, kept[0][-1][3]),)
        else:
            branch, far_up, far_down = tie(branch, up_mat[1], down_mat[1])
            up_mat, down_mat = (up_mat[0], far_up), (down_mat[0], far_down)
            mats[0] = (qkv_mat, out_mat, up_mat, down_mat)
        norm_z, inv_z = norm_parts(branch)
        middle = hidden + norm_z * norm_gain[which, 1] + norm_bias[which, 1]
        norm_b, inv_b = norm_parts(middle)
        b_low = (norm_b * norm_gain[which, 2] + norm_bias[which, 2]).astype(bf16)
        pre_act = jnp.concatenate([product(b_low, part) for part in up_mat], axis=1)
        below = 0.5 * (1.0 + lax.erf(pre_act * (1.0 / math.sqrt(2.0))))
        activated = pre_act * below
        mean_here = jnp.mean(activated, axis=-1)
        center = activated - mean_here[:, None]
        stats = jnp.stack([mean_here, jnp.mean(center * center, axis=-1)])
        stats_there = swap(stats, "c")
        mean_all = 0.5 * (stats[0] + stats_there[0])
        apart = 0.5 * (stats[0] - stats_there[0])
        spread = 0.5 * (stats[1] + stats_there[1]) + apart * apart
        inv_m = lax.rsqrt(spread + norm_eps)[:, None]
        norm_m = (activated - mean_all[:, None]) * inv_m
        gain_m, bias_m = mine_of(mid_gain[which]), mine_of(mid_bias[which])
        mixed_low = (norm_m * gain_m + bias_m).astype(bf16)
        near, far = mixed_low[:, :half_units], mixed_low[:, half_units:]
        hidden = middle + both_cores(product(near, down_mat[0]) + product(far, down_mat[1]))
        mixed_there = jnp.concatenate([far, near], axis=1)
        if which == 1:
            mixed_there = swap(mixed_there, "y")
        ins_there = (across(a_low), swap(scaled, "y"), across(b_low), mixed_there)
        kept.append(
            (
                norm_a, inv_a, project, scale_here, norm_z, inv_z, norm_b, inv_b, pre_act, below, norm_m, inv_m, gain_m,
                a_low, scaled, b_low, mixed_low, ins_there,
            )
        )
    output = lax.dynamic_slice_in_dim(hidden.astype(bf16), ic * rows, rows, 0)
    turned = turn(cotangent)
    grad_hidden = cores(turned, swap(turned, "c")).astype(f32)

    def natural(values):
        return ordered(values[:half_units], values[half_units:], 0)

    vectors, pending = [None] * LAYERS, [None] * LAYERS
    for which in reversed(range(LAYERS)):
        qkv_mat, out_mat, up_mat, down_mat = mats[which]
        (
            norm_a, inv_a, project, scale_here, norm_z, inv_z, norm_b, inv_b, pre_act, below, norm_m, inv_m, gain_m,
            a_low, scaled, b_low, mixed_low, ins_there,
        ) = kept[which]
        a_there, scaled_there, b_there, mixed_there = ins_there
        if which == 0:
            grad_hidden, mixed_there = tie(grad_hidden, mixed_there)
            mixed_there = swap(mixed_there, "y")
        final_low = grad_hidden.astype(bf16)
        grad_mixed = jnp.concatenate([product(final_low, part.T) for part in down_mat], axis=1)
        mid_gain_grad = jnp.sum(grad_mixed * norm_m, axis=0)
        mid_bias_grad = jnp.sum(grad_mixed, axis=0)
        scaled_grad = grad_mixed * gain_m
        sums = jnp.stack([jnp.sum(scaled_grad, axis=-1), jnp.sum(scaled_grad * norm_m, axis=-1)])
        sums = (sums + swap(sums, "c")) / hidden_width
        grad_act = inv_m * (scaled_grad - sums[0][:, None] - norm_m * sums[1][:, None])
        slope = below + pre_act * jnp.exp(-0.5 * pre_act * pre_act) * (1.0 / math.sqrt(2 * math.pi))
        grad_pre = (grad_act * slope).astype(bf16)
        if which == 1:
            grad_pre, a_there, scaled_there, b_there = tie(
                grad_pre, a_there, scaled_there, b_there
            )
        else:
            grad_pre, at_there = tie(grad_pre, at_there)
            later = finish_attention(at_there)
        near, far = grad_pre[:, :half_units], grad_pre[:, half_units:]

        def unit_columns(side):
            first = side * (half_units // 2)
            return (
                slice_of(near, first, half_units // 2),
                slice_of(far, first, half_units // 2),
                slice_of(final_low, side * half, half),
            )

        keep_n, keep_f, keep_c = unit_columns(iy)
        send_n, send_f, send_c = unit_columns(1 - iy)
        ff_there = swap(jnp.concatenate([send_f, send_n, send_c], axis=1), "y")
        ff_out = jnp.concatenate([keep_n, keep_f, keep_c], axis=1)
        grad_ff_in = both_cores(product(near, up_mat[0].T) + product(far, up_mat[1].T))
        grad_mid_in, gain_two, bias_two = norm_backward(
            grad_ff_in, norm_b, inv_b, norm_gain[which, 2]
        )
        grad_middle = grad_hidden + grad_mid_in
        grad_branch, gain_one, bias_one = norm_backward(
            grad_middle, norm_z, inv_z, norm_gain[which, 1]
        )
        branch_low = grad_branch.astype(bf16)
        if which == 0:
            branch_low, later = tie(branch_low, later)
            later = step_x(later)
        grad_heads = product(branch_low, out_mat.T).astype(bf16)
        grad_project, scale_grad = run_small(
            attention_backward,
            scale_here,
            (project, starts, grad_heads),
            [((group_rows, 3 * head_width), bf16), ((heads_here // 2, 2 * HD), f32)],
        )
        scale_grad = jnp.sum(scale_grad.reshape(heads_here, HD), axis=1)
        grad_project, ff_there, mixed_there = tie(grad_project, ff_there, mixed_there)
        ff_term = term_product(
            (b_low, mixed_low),
            (b_there, mixed_there),
            (ff_out, ff_there),
            ((0, 0, 0, width, 0), (1, 0, width, half, width), (1, width, width, half, width + half)),
            (width, 2 * width),
        )
        if which == 1:
            grad_project, ff_term = tie(grad_project, ff_term)
            ff_rows = scatter(ff_term)
        grad_normed = both_cores(product(grad_project, qkv_mat.T))
        grad_input, gain_zero, bias_zero = norm_backward(
            grad_normed, norm_a, inv_a, norm_gain[which, 0]
        )

        at_out = jnp.concatenate(
            [slice_of(grad_project, iy * wide, wide), slice_of(branch_low, iy * half, half)], axis=1
        )
        at_there = jnp.concatenate(
            [
                slice_of(grad_project, (1 - iy) * wide, wide),
                slice_of(branch_low, (1 - iy) * half, half),
            ],
            axis=1,
        )
        at_there = swap(at_there, "y")
        grad_hidden = grad_middle + grad_input

        def attention_term(
            there, here=at_out, ins=(a_low, scaled), ins_there=(a_there, scaled_there)
        ):
            split = half // 2
            rights = (here, there)
            out_term = term_product(
                ins[1:], ins_there[1:], rights, ((0, 0, wide, half, 0),), (head_width, half)
            ).reshape(chips, shard, half)
            out_term = jnp.concatenate([out_term[..., :split], out_term[..., split:]], axis=1)
            qkv_term = term_product(
                ins[:1], ins_there[:1], rights, ((0, 0, 0, wide, 0),), (width, wide)
            )
            return jnp.concatenate([qkv_term, out_term.reshape(-1, split)], axis=1)

        if which == 1:
            finish_attention = attention_term
        else:
            grad_hidden, later = tie(grad_hidden, later)
            at_rows_last = step_z(later)
        if which == 1:
            pending[1] = ff_rows
        shared = jnp.concatenate([gain_zero, gain_one, gain_two, bias_zero, bias_one, bias_two])
        vectors[which] = jnp.concatenate(
            [0.5 * shared, natural(mid_gain_grad), natural(mid_bias_grad), jnp.pad(scale_grad, (0, 128 - heads_here))]
        )

    vector = jnp.stack(vectors)
    vector = vector + swap(vector, "y")
    vector = vector + swap(vector, "x")
    vector, ff_term = tie(vector, ff_term)
    up_held, down_held = step_x(ff_term[:, :width]), step_x(ff_term[:, width:])
    vector = sum(z_pieces(vector))
    at_held = step_x(attention_term(at_there))
    at_held, output, grad_hidden = tie(at_held, output, grad_hidden)
    pending[0] = jnp.concatenate([step_z(up_held), step_z(down_held)], axis=1)
    at_rows = step_z(at_held)
    finals = []
    for at_rows, ff_rows in ((at_rows, pending[0]), (at_rows_last, pending[1])):
        send = jnp.concatenate([at_rows[:, :wide], ff_rows[:, :width]], axis=1)
        send = lax.dynamic_slice_in_dim(send, (1 - ic) * shard, shard, 0).astype(bf16)
        finals.extend([at_rows, ff_rows, swap(send, "c")])
    shapes = ((shard, 2 * wide), (shard, half), (shard, 2 * width), (4 * shard, half))
    summed = run_small(
        finish_rows, place, finals, [((LAYERS,) + shape, f32) for shape in shapes]
    )
    grad_tokens = turn(lax.dynamic_slice_in_dim(grad_hidden, ic * rows, rows, 0))
    output = turn(output)
    there = swap(vector, "c")
    shared = vector[:, : 6 * width] + there[:, : 6 * width]

    def spread_units(first):
        view = (LAYERS, 2, chips, 1, block)
        own, other = (part[:, first : first + units] for part in (vector, there))
        own, other = own.reshape(view), other.reshape(view)
        return cores(own, other, 3).transpose(0, 2, 3, 1, 4).reshape(LAYERS, hidden_width)

    scale_at = 6 * width + 2 * units
    own, other = (
        part[:, scale_at : scale_at + heads_here].reshape(LAYERS, heads_here, 1)
        for part in (vector, there)
    )
    return (
        output,
        grad_tokens,
        summed[0],
        summed[1],
        summed[2],
        summed[3],
        shared[:, : 3 * width].reshape(LAYERS, 3, width),
        shared[:, 3 * width :].reshape(LAYERS, 3, width),
        spread_units(6 * width),
        spread_units(6 * width + units),
        cores(own, other, 2).reshape(LAYERS, H),
    )


def solution(mesh):
    dp, sp = mesh.shape["dp"], mesh.shape["sp"]
    if sp == 2 and dp == 16:
        mesh = Mesh(mesh.devices.reshape(4, dp // 8, 2, 2), ("z", "x", "c", "y"))
        rows, every, cols, body = ("z", "x", "c"), ("z", "x", "c", "y"), "y", local_chip
    else:
        rows, every, cols, body = "dp", ("dp", "sp"), "sp", local_any
    weight = P(None, rows, None)
    in_specs = (P(every, None), P(rows), weight, weight, weight, weight)
    in_specs = in_specs + (P(),) * 5 + (P(every, None),)
    grad = P(None, rows, cols)
    out_specs = (P(every, None), P(every, None), grad, grad, grad, grad) + (P(),) * 5
    return jax.shard_map(body, mesh=mesh, in_specs=in_specs, out_specs=out_specs, check_vma=False)
```
